32 devices in a mesh: ctx: 8 (over y, x, core), mp: 4 (over z).
Axes of the slice: x: 2, y: 2, z: 4, core: 2. Of those that a mesh axis runs over, the one named last changes fastest.
Arguments:
- tile_embeds: bfloat16 [4, 2048, 768], P('mp', 'ctx'), may hold values from -10 to 10
- norm_gain: float32 [768], replicated, may hold values from 0.1 to 1.9
- norm_bias: float32 [768], replicated, may hold values from -3 to 3
- w_qkv: bfloat16 [768, 2304], P('mp'), may hold values from -1.5 to 1.5
- w_out: bfloat16 [768, 768], P('mp'), may hold values from -0.21875 to 0.21875
- valid_count: int32 [4], P('mp'), may hold values from 256 to 2048
Outputs:
- encoded: bfloat16 [4, 2048, 768], P('mp', 'ctx')
The draws below stay inside these ranges and needn't reach their ends.
All inputs are finite; a program needn't handle non-finite values.
Results may differ from the reference program's by a relative error of at most 0.008.
The reference program's roundings to bfloat16 on the way count: a program that leaves them out, or rounds other values in their place, can miss the bound.
Values may be sent and summed in bfloat16 or wider, within the bound.
No kernel may reach another device: no remote copies, remote signals or barrier semaphores. Data moves between devices by JAX's collectives and lax.ppermute only.
A program may use at most 64 MiB of HBM per device.

```python
import math
from functools import reduce
import jax
import jax.numpy as jnp
from jax import lax

D = 768
HEADS = 12
HEAD_DIM = 64
TILES_PER_SHARD = 256
MIDDLE_DILATION = 4
SLIDE_DILATION = 16
SHARDS_PER_SEG = 4
LENGTH = 2048
SLIDES = 4


def common_direction(key):
    return jax.random.normal(jax.random.fold_in(key, 4242), (D,), jnp.float32)


def draw_tile_embeds(key, part):
    noise_key, shard_key = jax.random.split(jax.random.fold_in(key, 23))
    sign_key = jax.random.fold_in(key, 31)
    amplitude_key = jax.random.fold_in(key, 37)
    noise = jax.random.normal(noise_key, (SLIDES, LENGTH, D), jnp.float32)
    shard_count = LENGTH // TILES_PER_SHARD
    shard_vectors = jax.random.normal(shard_key, (SLIDES, shard_count, 1, D), jnp.float32)
    shard_part = jnp.broadcast_to(shard_vectors, (SLIDES, shard_count, TILES_PER_SHARD, D)).reshape(SLIDES, LENGTH, D)
    tile_sign = (2 * jax.random.randint(sign_key, (SLIDES, LENGTH), 0, 2) - 1).astype(jnp.float32)
    amplitude = jax.random.uniform(amplitude_key, (SLIDES, LENGTH), jnp.float32, 1.0, 2.0)
    direction = common_direction(key)
    matrix = noise + shard_part + (amplitude * tile_sign)[:, :, None] * direction[None, None, :]
    return jnp.clip(matrix, -10.0, 10.0).astype(jnp.bfloat16)


def draw_w_qkv(key, part):
    first_key = jax.random.fold_in(jax.random.fold_in(key, 11), 0)
    third_key = jax.random.fold_in(key, 97)
    matrix = jax.random.normal(first_key, (D, 3 * D), jnp.float32) / math.sqrt(D)
    direction = common_direction(key) / math.sqrt(D)
    row_factor = jax.random.normal(third_key, (HEAD_DIM,), jnp.float32)
    outer = 0.43 * direction[:, None] * jnp.tile(row_factor, (HEADS,))[None, :]
    matrix = matrix.at[:, :D].add(outer)
    matrix = matrix.at[:, D:2 * D].add(-outer)
    return jnp.clip(matrix, -1.5, 1.5).astype(jnp.bfloat16)


def with_ends(entries, stream_key, low, top_value):
    longest = entries.shape.index(max(entries.shape))
    spots = []
    for shift in (0, 1):
        where = [jax.random.randint(jax.random.fold_in(stream_key, axis), (), 0, length) for axis, length in enumerate(entries.shape)]
        where[longest] = (where[longest] + shift) % entries.shape[longest]
        spots.append(tuple(where))
    return entries.at[spots[0]].set(low).at[spots[1]].set(top_value)


def block_scale(rng, dims, cuts, least, top_value):
    def one(axis_at, shards_of):
        steps = jax.random.uniform(jax.random.fold_in(jax.random.fold_in(rng, 6), axis_at), (shards_of,), jnp.float32, least / len(cuts), top_value / len(cuts))
        return jnp.repeat(jnp.exp(steps), dims[axis_at] // shards_of).reshape((-1,) + (1,) * (len(dims) - axis_at - 1))

    gain = one(*cuts[0])
    for cut in cuts[1:]:
        gain = gain * one(*cut)
    return gain


def gaussian(rng, dims, scale, limit, cuts=(), kind=jnp.bfloat16):
    entries = scale * jax.random.normal(rng, dims, jnp.float32)
    if cuts:
        entries = entries * block_scale(rng, dims, cuts, -0.22, 0.18)
    return jnp.clip(entries, -limit, limit).astype(kind)


def setup_inputs(seed: int = 0) -> dict:
    keys = jax.random.split(jax.random.key(seed), 7)
    tile_embeds = draw_tile_embeds(jax.random.fold_in(keys[6], 71), 0)
    norm_gain = jnp.clip(1.0 + 0.18 * jax.random.normal(keys[1], (D,), jnp.float32), 0.1, 1.9)
    norm_bias = gaussian(keys[2], (D,), 0.5, 3.0, (), jnp.float32)
    w_qkv = draw_w_qkv(jax.random.fold_in(keys[6], 71), 0)
    w_out = gaussian(keys[4], (D, D), D ** -0.5, 0.21875, ((0, 4),))
    valid_count = with_ends(jax.random.randint(keys[5], (SLIDES,), TILES_PER_SHARD, LENGTH + 1), jax.random.fold_in(keys[5], 1), TILES_PER_SHARD, LENGTH).astype(jnp.int32)
    return {"tile_embeds": tile_embeds, "norm_gain": norm_gain, "norm_bias": norm_bias, "w_qkv": w_qkv, "w_out": w_out, "valid_count": valid_count}


NEG_FILL = -1e+30

def layer_norm(row_data, norm_gain, norm_bias):
    floats = row_data.astype(jnp.float32)
    centre = lax.optimization_barrier(jnp.mean(floats, axis=-1, keepdims=True))
    spread = lax.optimization_barrier(jnp.mean((floats - centre) ** 2, axis=-1, keepdims=True))
    return ((floats - centre) * lax.rsqrt(spread + 1e-05) * norm_gain + norm_bias).astype(jnp.bfloat16)

def attend_block(query_block, key_matrix, value_matrix, allowed):
    rescale_factor = 1.0 / math.sqrt(query_block.shape[-1])
    logit_matrix = jnp.einsum('pty,pcy->ptc', query_block.astype(jnp.float32), key_matrix.astype(jnp.float32)) * rescale_factor
    logit_matrix = jnp.where(allowed, logit_matrix, NEG_FILL)
    largest = lax.optimization_barrier(jnp.max(logit_matrix, axis=-1))
    weights = jnp.where(allowed, jnp.exp(logit_matrix - largest[..., None]), 0.0)
    denominator = lax.optimization_barrier(jnp.sum(weights, axis=-1))
    rounded_length = lax.optimization_barrier(weights.astype(jnp.bfloat16)).astype(jnp.float32)
    weighted_sum = jnp.einsum('drj,djz->drz', rounded_length, value_matrix.astype(jnp.float32))
    return (largest, denominator, weighted_sum)

def dilated(head_rows, offset, dilation_rate):
    return head_rows.reshape(head_rows.shape[0] // dilation_rate, dilation_rate, head_rows.shape[-1])[:, offset]

def widen_rows(values, offset, dilation_rate, fill_value):
    picked = jnp.arange(dilation_rate) == offset
    if values.ndim == 1:
        return jnp.where(picked[None, :], values[:, None], fill_value).reshape(-1)
    return jnp.where(picked[None, :, None], values[:, None, :], fill_value).reshape(-1, values.shape[-1])

def one_slide(tile_rows, total_valid, norm_gain, norm_bias, w_qkv, w_out):
    valid_length = tile_rows.shape[0]
    model_width = tile_rows.shape[1]
    normed = layer_norm(tile_rows, norm_gain, norm_bias)
    projected = jnp.dot(normed, w_qkv, preferred_element_type=jnp.float32).astype(jnp.bfloat16)
    position = jnp.arange(valid_length, dtype=jnp.int32)
    key_valid = position < total_valid
    outputs = []
    for head_number in range(HEADS):
        low = head_number * HEAD_DIM
        query_rows = projected[:, low:low + HEAD_DIM]
        key_matrix = projected[:, model_width + low:model_width + low + HEAD_DIM]
        value_matrix = projected[:, 2 * model_width + low:2 * model_width + low + HEAD_DIM]
        seg_count = valid_length // TILES_PER_SHARD
        first_stats = attend_block(query_rows.reshape(seg_count, TILES_PER_SHARD, HEAD_DIM), key_matrix.reshape(seg_count, TILES_PER_SHARD, HEAD_DIM), value_matrix.reshape(seg_count, TILES_PER_SHARD, HEAD_DIM), key_valid.reshape(seg_count, 1, TILES_PER_SHARD))
        branches = [(first_stats[0].reshape(valid_length), first_stats[1].reshape(valid_length), first_stats[2].reshape(valid_length, HEAD_DIM))]
        for dilation_rate, segment_length in ((MIDDLE_DILATION, SHARDS_PER_SEG * TILES_PER_SHARD), (SLIDE_DILATION, valid_length)):
            offset = head_number % dilation_rate
            seg_rows = segment_length // dilation_rate
            segments = valid_length // segment_length
            sub_query = dilated(query_rows, offset, dilation_rate).reshape(segments, seg_rows, HEAD_DIM)
            sub_key = dilated(key_matrix, offset, dilation_rate).reshape(segments, seg_rows, HEAD_DIM)
            sub_value = dilated(value_matrix, offset, dilation_rate).reshape(segments, seg_rows, HEAD_DIM)
            sub_valid = key_valid.reshape(-1, dilation_rate)[:, offset].reshape(segments, 1, seg_rows)
            largest, denominator, weighted_sum = attend_block(sub_query, sub_key, sub_value, sub_valid)
            branches.append((widen_rows(largest.reshape(-1), offset, dilation_rate, NEG_FILL), widen_rows(denominator.reshape(-1), offset, dilation_rate, 0.0), widen_rows(weighted_sum.reshape(-1, HEAD_DIM), offset, dilation_rate, 0.0)))
        top_score = reduce(jnp.maximum, [entry[0] for entry in branches])
        denominator = sum((jnp.exp(entry[0] - top_score) * entry[1] for entry in branches))
        weighted_sum = sum((jnp.exp(entry[0] - top_score)[:, None] * entry[2] for entry in branches))
        head_result = jnp.where(key_valid[:, None], weighted_sum / denominator[:, None], 0.0)
        outputs.append(head_result)
    attention = jnp.stack(outputs, axis=1).reshape(valid_length, model_width).astype(jnp.bfloat16)
    projection = jnp.dot(attention, w_out, preferred_element_type=jnp.float32)
    return (tile_rows.astype(jnp.float32) + projection).astype(jnp.bfloat16)

def reference(tile_embeds, norm_gain, norm_bias, w_qkv, w_out, valid_count):

    def per_slide(packed):
        return one_slide(packed[0], packed[1], norm_gain, norm_bias, w_qkv, w_out)
    return lax.map(per_slide, (tile_embeds, valid_count))
```

```python
import math

import jax
import jax.numpy as jnp
from jax import lax
from jax.experimental import pallas as pl
from jax.experimental.pallas import tpu as pltpu
from jax.sharding import PartitionSpec as P

HEADS = 12
HEAD_DIM = 64
MID = 4
WIDE = 16
SHARDS = 4
STEPS = WIDE // MID
GROUP_HEADS = HEADS // SHARDS
GROUP_WIDTH = GROUP_HEADS * HEAD_DIM
NEG_FILL = -1e30
SCALE = math.log2(math.e) / math.sqrt(HEAD_DIM)
VMEM_LIMIT = 56 * 1024 * 1024


def call(body, out_shape, scratch=(), n_scalar=0, n_in=0, aliases=None):
    specs = [pl.BlockSpec(memory_space=pltpu.SMEM)] * n_scalar + [
        pl.BlockSpec(memory_space=pltpu.VMEM)
    ] * n_in
    outs = jax.tree.map(lambda _: pl.BlockSpec(memory_space=pltpu.VMEM), out_shape)
    return pl.pallas_call(
        body,
        out_shape=out_shape,
        in_specs=specs,
        out_specs=outs,
        scratch_shapes=list(scratch),
        input_output_aliases=aliases or {},
        compiler_params=pltpu.CompilerParams(vmem_limit_bytes=VMEM_LIMIT),
    )


def flip(value, axis, mask):
    pairs = [(source, source ^ mask) for source in range(lax.axis_size(axis))]
    return lax.ppermute(value, axis, pairs)


def residue_order(rows):
    depth = rows // WIDE
    new = lax.broadcasted_iota(jnp.int32, (rows, rows), 0)
    old = lax.broadcasted_iota(jnp.int32, (rows, rows), 1)
    return (old == (new % depth) * WIDE + new // depth).astype(jnp.bfloat16)


def position_order(rows):
    depth = rows // WIDE
    new = lax.broadcasted_iota(jnp.int32, (rows, rows), 0)
    old = lax.broadcasted_iota(jnp.int32, (rows, rows), 1)
    return (old == (new % WIDE) * depth + new // WIDE).astype(jnp.bfloat16)


def matmul(left, right):
    return jnp.dot(left, right, preferred_element_type=jnp.float32)


def matmul_t(left, right):
    return lax.dot_general(
        left, right, (((1,), (1,)), ((), ())), preferred_element_type=jnp.float32
    )


def norm_body(*refs):
    x_refs, gain_ref, bias_ref, out_refs = refs[:SHARDS], refs[SHARDS], refs[SHARDS + 1], refs[SHARDS + 2 :]
    order = residue_order(x_refs[0].shape[0])
    for x_ref, out_ref in zip(x_refs, out_refs):
        floats = x_ref[...].astype(jnp.float32)
        centred = floats - jnp.mean(floats, axis=-1, keepdims=True)
        spread = jnp.mean(centred * centred, axis=-1, keepdims=True)
        normed = (centred * lax.rsqrt(spread + 1e-05) * gain_ref[...] + bias_ref[...]).astype(
            jnp.bfloat16
        )
        out_ref[...] = matmul(order, normed).astype(jnp.bfloat16)


def group_indices():
    shard = lax.axis_index("ctx")
    return shard % SHARDS, shard // SHARDS


def qkv_body(n_mp, shared, *refs):
    normed_refs, refs = refs[:SHARDS], refs[SHARDS:]
    n_weights = 1 + (2 if shared else 1) * (n_mp - 1)
    weight_refs, refs = refs[:n_weights], refs[n_weights:]
    out_refs, sent_ref, whole_ref = refs[:SHARDS], refs[SHARDS], refs[SHARDS + 1]
    member, group = group_indices()
    mp_index = lax.axis_index("mp")
    rows = weight_refs[0].shape[0]

    def put(ref, source, offset):
        start = pl.multiple_of(source * rows + offset, 16)
        whole_ref[pl.ds(start, ref.shape[0]), :] = ref[...]

    put(weight_refs[0], mp_index, 0)
    for apart in range(1, n_mp):
        if shared:
            half = group % 2
            put(weight_refs[2 * apart - 1], mp_index ^ apart, half * (rows // 2))
            put(weight_refs[2 * apart], mp_index ^ apart, (1 - half) * (rows // 2))
        else:
            put(weight_refs[apart], mp_index ^ apart, 0)
    for normed_ref, out_ref in zip(normed_refs, out_refs):
        projected = matmul(normed_ref[...], whole_ref[...]).astype(jnp.bfloat16)
        out_ref[...] = projected.reshape(out_ref.shape)
    depth = out_refs[0].shape[2]
    for index in range(GROUP_HEADS):
        head = member * GROUP_HEADS + index
        low = index * HEAD_DIM
        for shard, out_ref in enumerate(out_refs):
            block = out_ref[head // MID, head % MID]
            key = block[:, GROUP_WIDTH + low : GROUP_WIDTH + low + HEAD_DIM]
            value = block[:, 2 * GROUP_WIDTH + low : 2 * GROUP_WIDTH + low + HEAD_DIM]
            sent_ref[index, shard * depth : (shard + 1) * depth, :] = jnp.concatenate(
                [key, value], axis=1
            )


def branch(query, key, value, allowed):
    score = matmul_t(query, key) * SCALE
    score = jnp.where(allowed, score, NEG_FILL)
    largest = jnp.max(score, axis=-1, keepdims=True)
    weight = jnp.exp2(score - largest)
    total = jnp.sum(weight, axis=-1, keepdims=True)
    return largest, total, matmul(weight.astype(jnp.bfloat16), value)


def merge(one, two):
    top = jnp.maximum(one[0], two[0])
    left = jnp.exp2(one[0] - top)
    right = jnp.exp2(two[0] - top)
    return top, left * one[1] + right * two[1], left * one[2] + right * two[2]


def near_body(valid_ref, *refs):
    qkv_refs, refs = refs[:SHARDS], refs[SHARDS:]
    out_refs, refs = refs[:SHARDS], refs[SHARDS:]
    kept_max, kept_sum, kept_num, all_max, all_sum, all_num = refs
    member, group = group_indices()
    valid = valid_ref[0]
    depth = qkv_refs[0].shape[2]
    rows = WIDE * depth
    key_at = lax.broadcasted_iota(jnp.int32, (1, rows), 1)
    row_at = lax.broadcasted_iota(jnp.int32, (rows, 1), 0)
    bases = [(group * SHARDS + (member ^ apart)) * rows for apart in range(SHARDS)]

    def part(ref, low):
        return ref[...].reshape(rows, -1)[:, low : low + HEAD_DIM]

    for index in range(GROUP_HEADS):
        head = member * GROUP_HEADS + index
        low = index * HEAD_DIM
        offset = head % MID
        for shard, ref in enumerate(qkv_refs):
            block = ref[...].reshape(rows, 3 * GROUP_WIDTH)
            allowed = bases[shard] + (key_at % depth) * WIDE + key_at // depth < valid
            largest, total, number = branch(
                block[:, low : low + HEAD_DIM],
                block[:, GROUP_WIDTH + low : GROUP_WIDTH + low + HEAD_DIM],
                block[:, 2 * GROUP_WIDTH + low : 2 * GROUP_WIDTH + low + HEAD_DIM],
                allowed,
            )
            all_max[shard] = largest.reshape(STEPS, MID, depth, 1)
            all_sum[shard] = total.reshape(STEPS, MID, depth, 1)
            all_num[shard] = number.reshape(STEPS, MID, depth, HEAD_DIM)
        taken = jnp.concatenate(
            [ref[:, offset].reshape(STEPS * depth, 3 * GROUP_WIDTH) for ref in qkv_refs], axis=0
        )
        count = STEPS * depth
        mid_at = lax.broadcasted_iota(jnp.int32, (1, count), 1)
        mid_position = (mid_at % depth) * WIDE + (mid_at // depth) * MID + offset
        allowed = jnp.concatenate([base + mid_position for base in bases], axis=1) < valid
        middle = branch(
            taken[:, low : low + HEAD_DIM],
            taken[:, GROUP_WIDTH + low : GROUP_WIDTH + low + HEAD_DIM],
            taken[:, 2 * GROUP_WIDTH + low : 2 * GROUP_WIDTH + low + HEAD_DIM],
            allowed,
        )
        here = (
            all_max[:, :, offset].reshape(SHARDS * count, 1),
            all_sum[:, :, offset].reshape(SHARDS * count, 1),
            all_num[:, :, offset].reshape(SHARDS * count, HEAD_DIM),
        )
        top, total, number = merge(here, middle)
        all_max[:, :, offset] = top.reshape(SHARDS, STEPS, depth, 1)
        all_sum[:, :, offset] = total.reshape(SHARDS, STEPS, depth, 1)
        all_num[:, :, offset] = number.reshape(SHARDS, STEPS, depth, HEAD_DIM)
        kept_max[index] = all_max[:, head // MID, offset].reshape(SHARDS * depth, 1)
        kept_sum[index] = all_sum[:, head // MID, offset].reshape(SHARDS * depth, 1)
        kept_num[index] = all_num[:, head // MID, offset].reshape(SHARDS * depth, HEAD_DIM)
        for shard, ref in enumerate(out_refs):
            position = bases[shard] + (row_at % depth) * WIDE + row_at // depth
            number = all_num[shard].reshape(rows, HEAD_DIM)
            total = all_sum[shard].reshape(rows, 1)
            attention = jnp.where(position < valid, number / total, 0.0).astype(jnp.bfloat16)
            ref[:, :, :, low : low + HEAD_DIM] = attention.reshape(STEPS, MID, depth, HEAD_DIM)


def far_body(n_groups, valid_ref, *refs):
    qkv_refs, refs = refs[:SHARDS], refs[SHARDS:]
    sent_refs, refs = refs[:n_groups], refs[n_groups:]
    kept_max, kept_sum, kept_num = refs[:3]
    in_refs, out_refs = refs[3 : 3 + SHARDS], refs[3 + SHARDS :]
    member, group = group_indices()
    valid = valid_ref[0]
    depth = qkv_refs[0].shape[2]
    count = SHARDS * depth
    for ref, out_ref in zip(in_refs, out_refs):
        out_ref[...] = ref[...]

    def positions(at, head, apart):
        block = at // depth
        shard = (group ^ apart) * SHARDS + (member ^ block)
        return (shard * depth + at % depth) * WIDE + head

    key_at = lax.broadcasted_iota(jnp.int32, (1, count), 1)
    row_at = lax.broadcasted_iota(jnp.int32, (count, 1), 0)
    for index in range(GROUP_HEADS):
        head = member * GROUP_HEADS + index
        low = index * HEAD_DIM
        query = jnp.concatenate(
            [ref[head // MID, head % MID][:, low : low + HEAD_DIM] for ref in qkv_refs], axis=0
        )
        allowed = (
            jnp.concatenate([positions(key_at, head, apart) for apart in range(n_groups)], axis=1)
            < valid
        )
        both = jnp.concatenate([ref[index] for ref in sent_refs], axis=0)
        slide = branch(query, both[:, :HEAD_DIM], both[:, HEAD_DIM:], allowed)
        _, total, number = merge((kept_max[index], kept_sum[index], kept_num[index]), slide)
        inside = positions(row_at, head, 0) < valid
        attention = jnp.where(inside, number / total, 0.0).astype(jnp.bfloat16)
        for shard, ref in enumerate(out_refs):
            ref[head // MID, head % MID, :, low : low + HEAD_DIM] = attention[
                shard * depth : (shard + 1) * depth
            ]


def gather_body(n_mp, *refs):
    own_ref, pair_refs, out_ref = refs[0], refs[1:-1], refs[-1]
    mp_index = lax.axis_index("mp")
    rows = own_ref.shape[0]
    out_ref[pl.ds(pl.multiple_of(mp_index * rows, 16), rows), :] = own_ref[...]
    for apart in range(1, n_mp):
        if len(pair_refs) == n_mp - 1:
            start = pl.multiple_of((mp_index ^ apart) * rows, 16)
            out_ref[pl.ds(start, rows), :] = pair_refs[apart - 1][...]
        else:
            core = lax.axis_index("ctx") % 2
            half = rows // 2
            for turn in range(2):
                start = (mp_index ^ apart) * rows + (core ^ turn) * half
                out_ref[pl.ds(pl.multiple_of(start, 16), half), :] = pair_refs[
                    2 * (apart - 1) + turn
                ][...]


def out_body(x_ref, *refs):
    part_refs, weight_ref, out_ref = refs[:SHARDS], refs[SHARDS], refs[SHARDS + 1]
    rows = x_ref.shape[0]
    member, _ = group_indices()
    order = position_order(rows)
    total = x_ref[...].astype(jnp.float32)
    update = jnp.zeros(total.shape, jnp.float32)
    for apart, ref in enumerate(part_refs):
        part = matmul(order, ref[...].reshape(rows, GROUP_WIDTH)).astype(jnp.bfloat16)
        start = pl.multiple_of((member ^ apart) * GROUP_WIDTH, GROUP_WIDTH)
        update = update + matmul(part, weight_ref[pl.ds(start, GROUP_WIDTH), :])
    out_ref[...] = (total + update).astype(jnp.bfloat16)


def local(tile_embeds, norm_gain, norm_bias, w_qkv, w_out, valid_count):
    x = tile_embeds[0]
    rows, width = x.shape
    n_mp = lax.axis_size("mp")
    n_groups = lax.axis_size("ctx") // SHARDS
    depth = rows // WIDE
    weight_rows = w_qkv.shape[0]
    member, group = group_indices()
    bf16 = jnp.bfloat16

    def shape(*dims, kind=bf16):
        return jax.ShapeDtypeStruct(dims, kind)

    x_far = flip(x, "ctx", 2)
    chunks = [x, flip(x, "ctx", 1), x_far, flip(x_far, "ctx", 1)]

    mine = jnp.concatenate(
        [
            lax.dynamic_slice(
                w_qkv, (0, part * width + member * GROUP_WIDTH), (weight_rows, GROUP_WIDTH)
            )
            for part in range(3)
        ],
        axis=1,
    )
    shared = n_groups % 2 == 0 and weight_rows % 32 == 0
    weights = [mine]
    if shared:
        half = weight_rows // 2
        piece = lax.dynamic_slice(mine, (group % 2 * half, 0), (half, 3 * GROUP_WIDTH))
        for apart in range(1, n_mp):
            direct = flip(piece, "mp", apart)
            weights += [direct, flip(direct, "ctx", SHARDS)]
    else:
        weights += [flip(mine, "mp", apart) for apart in range(1, n_mp)]

    out_parts = [w_out]
    if weight_rows % 32 == 0:
        half = weight_rows // 2
        piece = lax.dynamic_slice(w_out, (member % 2 * half, 0), (half, width))
        for apart in range(1, n_mp):
            direct = flip(piece, "mp", apart)
            out_parts += [direct, flip(direct, "ctx", 1)]
    else:
        out_parts += [flip(w_out, "mp", apart) for apart in range(1, n_mp)]

    normed = call(norm_body, [shape(rows, width)] * SHARDS, n_in=SHARDS + 2)(
        *chunks, norm_gain.reshape(1, width), norm_bias.reshape(1, width)
    )
    block = shape(STEPS, MID, depth, 3 * GROUP_WIDTH)
    *qkv, sent = call(
        lambda *refs: qkv_body(n_mp, shared, *refs),
        [block] * SHARDS + [shape(GROUP_HEADS, SHARDS * depth, 2 * HEAD_DIM)],
        scratch=[pltpu.VMEM((n_mp * weight_rows, 3 * GROUP_WIDTH), bf16)],
        n_in=SHARDS + len(weights),
    )(*normed, *weights)
    others = [sent] + [flip(sent, "ctx", SHARDS * apart) for apart in range(1, n_groups)]

    f32 = jnp.float32
    part = shape(STEPS, MID, depth, GROUP_WIDTH)
    stats = [
        shape(GROUP_HEADS, SHARDS * depth, 1, kind=f32),
        shape(GROUP_HEADS, SHARDS * depth, 1, kind=f32),
        shape(GROUP_HEADS, SHARDS * depth, HEAD_DIM, kind=f32),
    ]
    near = call(
        near_body,
        [part] * SHARDS + stats,
        scratch=[
            pltpu.VMEM((SHARDS, STEPS, MID, depth, 1), f32),
            pltpu.VMEM((SHARDS, STEPS, MID, depth, 1), f32),
            pltpu.VMEM((SHARDS, STEPS, MID, depth, HEAD_DIM), f32),
        ],
        n_scalar=1,
        n_in=SHARDS,
    )(valid_count, *qkv)
    attention = call(
        lambda *refs: far_body(n_groups, *refs),
        [part] * SHARDS,
        n_scalar=1,
        n_in=SHARDS + n_groups + 3 + SHARDS,
        aliases={1 + SHARDS + n_groups + 3 + shard: shard for shard in range(SHARDS)},
    )(valid_count, *qkv, *others, *near[SHARDS:], *near[:SHARDS])
    received = [attention[0]] + [flip(attention[apart], "ctx", apart) for apart in range(1, SHARDS)]
    whole_out = call(
        lambda *refs: gather_body(n_mp, *refs), shape(width, width), n_in=len(out_parts)
    )(*out_parts)
    return call(out_body, shape(rows, width), n_in=SHARDS + 2)(x, *received, whole_out)[None]


def solution(mesh):
    placed = (P("mp", "ctx", None), P(), P(), P("mp", None), P("mp", None), P("mp"))
    return jax.shard_map(
        local, mesh=mesh, in_specs=placed, out_specs=P("mp", "ctx", None), check_vma=False
    )
```

```python
import math

import jax
import jax.numpy as jnp
from jax import lax
from jax.experimental import pallas as pl
from jax.experimental.pallas import tpu as pltpu
from jax.sharding import PartitionSpec as P

HEADS = 12
HEAD_DIM = 64
MID = 4
WIDE = 16
SHARDS = 4
STEPS = WIDE // MID
GROUP_HEADS = HEADS // SHARDS
GROUP_WIDTH = GROUP_HEADS * HEAD_DIM
NEG_FILL = -1e30
SCALE = math.log2(math.e) / math.sqrt(HEAD_DIM)
VMEM_LIMIT = 24 * 1024 * 1024
LANES = 128


def call(body, out_shape, scratch=(), n_scalar=0, n_in=0, micros=1):
    specs = [pl.BlockSpec(memory_space=pltpu.SMEM)] * n_scalar + [
        pl.BlockSpec(memory_space=pltpu.VMEM)
    ] * n_in
    outs = [pl.BlockSpec(memory_space=pltpu.VMEM) for _ in out_shape]
    return pl.pallas_call(
        body,
        out_shape=out_shape,
        in_specs=specs,
        out_specs=outs,
        scratch_shapes=list(scratch),
        cost_estimate=pl.CostEstimate(
            flops=micros * 1_000_000_000, transcendentals=0, bytes_accessed=micros * 3_000_000
        ),
        compiler_params=pltpu.CompilerParams(vmem_limit_bytes=VMEM_LIMIT),
    )


def near(value):
    return pltpu.with_memory_space_constraint(value, pltpu.VMEM)


def flip(value, axis, mask):
    pairs = [(source, source ^ mask) for source in range(lax.axis_size(axis))]
    return near(lax.ppermute(value, axis, pairs))


def after(value, *earlier):
    return lax.optimization_barrier((value, *earlier))[0]


def place_of(order, rows):
    depth = rows // WIDE
    return order % depth * WIDE + order // depth % STEPS * MID + order // (STEPS * depth)


def to_order(rows):
    new = lax.broadcasted_iota(jnp.int32, (rows, rows), 0)
    old = lax.broadcasted_iota(jnp.int32, (rows, rows), 1)
    return (old == place_of(new, rows)).astype(jnp.bfloat16)


def to_position(rows):
    new = lax.broadcasted_iota(jnp.int32, (rows, rows), 0)
    old = lax.broadcasted_iota(jnp.int32, (rows, rows), 1)
    return (new == place_of(old, rows)).astype(jnp.bfloat16)


def product(left, right, left_axis=1, right_axis=0):
    return lax.dot_general(
        left,
        right,
        (((left_axis,), (right_axis,)), ((), ())),
        preferred_element_type=jnp.float32,
    )


def norm_body(*refs):
    count = len(refs) // 2 - 1
    x_refs, gain_ref, bias_ref, out_refs = refs[:count], refs[count], refs[count + 1], refs[count + 2 :]
    order = to_order(x_refs[0].shape[0])
    gain = gain_ref[...][None, :]
    bias = bias_ref[...][None, :]
    for x_ref, out_ref in zip(x_refs, out_refs):
        floats = x_ref[...].astype(jnp.float32)
        centred = floats - jnp.mean(floats, axis=-1, keepdims=True)
        spread = jnp.mean(centred * centred, axis=-1, keepdims=True)
        normed = (centred * lax.rsqrt(spread + 1e-05) * gain + bias).astype(jnp.bfloat16)
        out_ref[...] = product(order, normed).astype(jnp.bfloat16)


def group_indices():
    shard = lax.axis_index("ctx")
    return shard % SHARDS, shard // SHARDS


def head_slices(index):
    return [
        slice(part * GROUP_WIDTH + index * HEAD_DIM, part * GROUP_WIDTH + (index + 1) * HEAD_DIM)
        for part in range(3)
    ]


def wide_rows(head, rows):
    depth = rows // WIDE
    start = head % MID * (STEPS * depth) + head % WIDE // MID * depth
    return pl.ds(pl.multiple_of(start, depth), depth)


def middle_rows(head, rows):
    count = rows // MID
    return pl.ds(pl.multiple_of(head % MID * count, count), count)


def qkv_body(n_mp, shared, *refs):
    normed_refs, refs = refs[:SHARDS], refs[SHARDS:]
    n_weights = 1 + (2 if shared else 1) * (n_mp - 1)
    weight_refs, refs = refs[:n_weights], refs[n_weights:]
    out_refs, sent_ref, whole_ref = refs[:SHARDS], refs[SHARDS], refs[SHARDS + 1]
    member, group = group_indices()
    mp_index = lax.axis_index("mp")
    rows = weight_refs[0].shape[0]

    def put(ref, source, offset):
        start = pl.multiple_of(source * rows + offset, 16)
        whole_ref[pl.ds(start, ref.shape[0]), :] = ref[...]

    put(weight_refs[0], mp_index, 0)
    for apart in range(1, n_mp):
        if shared:
            half = group % 2
            put(weight_refs[2 * apart - 1], mp_index ^ apart, half * (rows // 2))
            put(weight_refs[2 * apart], mp_index ^ apart, (1 - half) * (rows // 2))
        else:
            put(weight_refs[apart], mp_index ^ apart, 0)
    shard_rows = out_refs[0].shape[0]
    depth = shard_rows // WIDE
    for normed_ref, out_ref in zip(normed_refs, out_refs):
        out_ref[...] = product(normed_ref[...], whole_ref[...]).astype(jnp.bfloat16)
    for index in range(GROUP_HEADS):
        _, key_at, value_at = head_slices(index)
        taken = wide_rows(member * GROUP_HEADS + index, shard_rows)
        for shard, out_ref in enumerate(out_refs):
            sent_ref[index, shard * depth : (shard + 1) * depth, :] = jnp.concatenate(
                [out_ref[taken, key_at], out_ref[taken, value_at]], axis=1
            )


def branch(query, key, value, bias):
    score = product(key, query, 1, 1) * SCALE + bias
    largest = jnp.max(score, axis=0, keepdims=True)
    weight = jnp.exp2(score - largest)
    total = jnp.sum(weight, axis=0, keepdims=True)
    return largest, total, product(value, weight.astype(jnp.bfloat16), 0, 0)


def key_bias(position, valid):
    return jnp.where(position < valid, 0.0, NEG_FILL).astype(jnp.float32)


def merge(one, two):
    top = jnp.maximum(one[0], two[0])
    left = jnp.exp2(one[0] - top)
    right = jnp.exp2(two[0] - top)
    return top, left * one[1] + right * two[1], left * one[2] + right * two[2]


def near_body(valid_ref, *refs):
    qkv_refs, (max_ref, sum_ref, num_ref) = refs[:SHARDS], refs[SHARDS:]
    member, group = group_indices()
    valid = valid_ref[0]
    rows = qkv_refs[0].shape[0]
    count = rows // MID
    bases = [(group * SHARDS + (member ^ apart)) * rows for apart in range(SHARDS)]
    place = place_of(lax.broadcasted_iota(jnp.int32, (rows, LANES), 0), rows)
    lane = lax.broadcasted_iota(jnp.int32, (1, rows), 1)

    def widen(bias):
        return jnp.concatenate([bias] * (rows // LANES), axis=1)

    for shard, ref in enumerate(qkv_refs):
        bias = widen(key_bias(place + bases[shard], valid))
        for index in range(GROUP_HEADS):
            query_at, key_at, value_at = head_slices(index)
            stats = branch(ref[:, query_at], ref[:, key_at], ref[:, value_at], bias)
            max_ref[index, shard], sum_ref[index, shard], num_ref[index, shard] = stats
    entry = lax.broadcasted_iota(jnp.int32, (count, LANES), 0)
    depth = rows // WIDE
    for index in range(GROUP_HEADS):
        head = member * GROUP_HEADS + index
        taken = middle_rows(head, rows)
        query, key, value = (
            jnp.concatenate([ref[taken, at] for ref in qkv_refs], axis=0)
            for at in head_slices(index)
        )
        position = entry % depth * WIDE + entry // depth * MID + head % MID
        bias = widen(
            jnp.concatenate([key_bias(position + base, valid) for base in bases], axis=0)
        )
        middle = branch(query, key, value, bias)
        inside = lane // count == head % MID
        for shard in range(SHARDS):
            largest, total, number = (
                jnp.concatenate([entry[:, shard * count : (shard + 1) * count]] * MID, axis=1)
                for entry in middle
            )
            merged = merge(
                (max_ref[index, shard], sum_ref[index, shard], num_ref[index, shard]),
                (jnp.where(inside, largest, NEG_FILL), total, number),
            )
            max_ref[index, shard], sum_ref[index, shard], num_ref[index, shard] = merged


def far_body(n_groups, valid_ref, *refs):
    qkv_refs, refs = refs[:SHARDS], refs[SHARDS:]
    sent_refs, refs = refs[:n_groups], refs[n_groups:]
    (max_ref, sum_ref, num_ref), out_refs = refs[:3], refs[3:]
    member, group = group_indices()
    valid = valid_ref[0]
    rows = qkv_refs[0].shape[0]
    depth = rows // WIDE
    count = SHARDS * depth
    entry = lax.broadcasted_iota(jnp.int32, (count, count), 0)
    lane = lax.broadcasted_iota(jnp.int32, (1, rows), 1)
    for index in range(GROUP_HEADS):
        head = member * GROUP_HEADS + index
        taken = wide_rows(head, rows)
        query_at = head_slices(index)[0]
        query = jnp.concatenate([ref[taken, query_at] for ref in qkv_refs], axis=0)
        bias = jnp.concatenate(
            [
                key_bias(
                    ((group ^ apart) * SHARDS + (member ^ (entry // depth))) * rows
                    + entry % depth * WIDE
                    + head,
                    valid,
                )
                for apart in range(n_groups)
            ],
            axis=0,
        )
        both = jnp.concatenate([ref[index] for ref in sent_refs], axis=0)
        stats = branch(query, both[:, :HEAD_DIM], both[:, HEAD_DIM:], bias)
        stacked = jnp.concatenate(
            [stats[2], jnp.broadcast_to(stats[0], (8, count)), jnp.broadcast_to(stats[1], (8, count))],
            axis=0,
        )
        stacked = jnp.concatenate(
            [stacked, jnp.zeros((stacked.shape[0], LANES - count), jnp.float32)], axis=1
        )
        block = head % MID * STEPS + head % WIDE // MID
        inside = lane // depth == block
        for shard, out_ref in enumerate(out_refs):
            shift = (block * depth - shard * depth + LANES) % LANES
            moved = jnp.concatenate(
                [pltpu.roll(stacked, shift, 1)] * (rows // LANES), axis=1
            )
            _, total, number = merge(
                (max_ref[index, shard], sum_ref[index, shard], num_ref[index, shard]),
                (
                    jnp.where(inside, moved[HEAD_DIM : HEAD_DIM + 1], NEG_FILL),
                    moved[HEAD_DIM + 8 : HEAD_DIM + 9],
                    moved[:HEAD_DIM],
                ),
            )
            base = (group * SHARDS + (member ^ shard)) * rows
            attention = jnp.where(
                base + place_of(lane, rows) < valid, number * (1.0 / total), 0.0
            )
            out_ref[index * HEAD_DIM : (index + 1) * HEAD_DIM, :] = attention.astype(jnp.bfloat16)


def gather_body(n_mp, *refs):
    own_ref, pair_refs, out_ref = refs[0], refs[1:-1], refs[-1]
    mp_index = lax.axis_index("mp")
    rows = own_ref.shape[0]
    out_ref[pl.ds(pl.multiple_of(mp_index * rows, 16), rows), :] = own_ref[...]
    for apart in range(1, n_mp):
        if len(pair_refs) == n_mp - 1:
            start = pl.multiple_of((mp_index ^ apart) * rows, 16)
            out_ref[pl.ds(start, rows), :] = pair_refs[apart - 1][...]
        else:
            core = lax.axis_index("ctx") % 2
            half = rows // 2
            for turn in range(2):
                start = (mp_index ^ apart) * rows + (core ^ turn) * half
                out_ref[pl.ds(pl.multiple_of(start, 16), half), :] = pair_refs[
                    2 * (apart - 1) + turn
                ][...]


def out_body(x_ref, *refs):
    part_refs, weight_ref, out_ref = refs[:SHARDS], refs[SHARDS], refs[SHARDS + 1]
    rows = x_ref.shape[0]
    member, _ = group_indices()
    order = to_position(rows)
    update = jnp.zeros(x_ref.shape, jnp.float32)
    for apart, ref in enumerate(part_refs):
        part = product(order, ref[...], 1, 1).astype(jnp.bfloat16)
        start = pl.multiple_of((member ^ apart) * GROUP_WIDTH, GROUP_WIDTH)
        update = update + product(part, weight_ref[pl.ds(start, GROUP_WIDTH), :])
    out_ref[...] = (x_ref[...].astype(jnp.float32) + update).astype(jnp.bfloat16)


def local(tile_embeds, norm_gain, norm_bias, w_qkv, w_out, valid_count):
    x = tile_embeds[0]
    rows, width = x.shape
    n_mp = lax.axis_size("mp")
    n_groups = lax.axis_size("ctx") // SHARDS
    depth = rows // WIDE
    weight_rows = w_qkv.shape[0]
    member, group = group_indices()
    bf16, f32 = jnp.bfloat16, jnp.float32
    shape = pltpu.VMEM

    def columns(first, count):
        return jnp.concatenate(
            [
                lax.dynamic_slice(
                    w_qkv, (first, part * width + member * GROUP_WIDTH), (count, GROUP_WIDTH)
                )
                for part in range(3)
            ],
            axis=1,
        )

    mine = columns(0, weight_rows)
    shared = n_groups % 2 == 0 and weight_rows % 32 == 0
    weights = [near(mine)]
    if shared:
        half = weight_rows // 2
        piece = columns(group % 2 * half, half)
        direct = [flip(piece, "mp", apart) for apart in range(1, n_mp)]
        for value in direct:
            weights += [value, flip(value, "ctx", SHARDS)]
    else:
        direct = [flip(mine, "mp", apart) for apart in range(1, n_mp)]
        weights += direct

    x_pair = flip(x, "ctx", 1)
    x_far = flip(x, "ctx", 2)
    chunks = [near(x), x_pair, x_far, flip(after(x_far, direct[0]), "ctx", 1)]

    out_parts = [near(w_out)]
    if weight_rows % 32 == 0:
        half = weight_rows // 2
        piece = lax.dynamic_slice(w_out, (member % 2 * half, 0), (half, width))
        for apart in range(1, n_mp):
            received = flip(after(piece, *direct), "mp", apart)
            out_parts += [received, flip(received, "ctx", 1)]
    else:
        out_parts += [flip(after(w_out, *direct), "mp", apart) for apart in range(1, n_mp)]

    normed = []
    for pair in (chunks[:2], chunks[2:]):
        normed += call(norm_body, [shape((rows, width), bf16)] * 2, n_in=4, micros=2)(
            *pair, near(norm_gain), near(norm_bias)
        )
    *qkv, sent = call(
        lambda *refs: qkv_body(n_mp, shared, *refs),
        [shape((rows, 3 * GROUP_WIDTH), bf16)] * SHARDS
        + [shape((GROUP_HEADS, SHARDS * depth, 2 * HEAD_DIM), bf16)],
        scratch=[pltpu.VMEM((n_mp * weight_rows, 3 * GROUP_WIDTH), bf16)],
        n_in=SHARDS + len(weights),
        micros=3,
    )(*normed, *weights)
    others = [sent] + [flip(sent, "ctx", SHARDS * apart) for apart in range(1, n_groups)]
    stats = call(
        near_body,
        [
            shape((GROUP_HEADS, SHARDS, 1, rows), f32),
            shape((GROUP_HEADS, SHARDS, 1, rows), f32),
            shape((GROUP_HEADS, SHARDS, HEAD_DIM, rows), f32),
        ],
        n_scalar=1,
        n_in=SHARDS,
        micros=5,
    )(valid_count, *qkv)
    attention = call(
        lambda *refs: far_body(n_groups, *refs),
        [shape((GROUP_WIDTH, rows), bf16)] * SHARDS,
        n_scalar=1,
        n_in=SHARDS + n_groups + 3,
        micros=2,
    )(valid_count, *qkv, *others, *stats)
    received = [attention[0]] + [flip(attention[apart], "ctx", apart) for apart in range(1, SHARDS)]
    (whole_out,) = call(
        lambda *refs: gather_body(n_mp, *refs), [shape((width, width), bf16)], n_in=len(out_parts)
    )(*out_parts)
    (out,) = call(
        out_body, [jax.ShapeDtypeStruct((rows, width), bf16)], n_in=SHARDS + 2, micros=2
    )(near(x), *received, whole_out)
    return out[None]


def solution(mesh):
    placed = (P("mp", "ctx", None), P(), P(), P("mp", None), P("mp", None), P("mp"))
    return jax.shard_map(
        local, mesh=mesh, in_specs=placed, out_specs=P("mp", "ctx", None), check_vma=False
    )
```

```python
import math

import jax
import jax.numpy as jnp
from jax import lax
from jax.experimental import pallas as pl
from jax.experimental.pallas import tpu as pltpu
from jax.sharding import PartitionSpec as P

HEADS = 12
HEAD_DIM = 64
MID = 4
WIDE = 16
SHARDS = 4
STEPS = WIDE // MID
GROUP_HEADS = HEADS // SHARDS
GROUP_WIDTH = GROUP_HEADS * HEAD_DIM
NEG_FILL = -1e30
SCALE = math.log2(math.e) / math.sqrt(HEAD_DIM)
VMEM_LIMIT = 24 * 1024 * 1024
LANES = 128


def call(body, out_shape, scratch=(), n_scalar=0, n_in=0, micros=1):
    specs = [pl.BlockSpec(memory_space=pltpu.SMEM)] * n_scalar + [
        pl.BlockSpec(memory_space=pltpu.VMEM)
    ] * n_in
    outs = [pl.BlockSpec(memory_space=pltpu.VMEM) for _ in out_shape]
    return pl.pallas_call(
        body,
        out_shape=out_shape,
        in_specs=specs,
        out_specs=outs,
        scratch_shapes=list(scratch),
        cost_estimate=pl.CostEstimate(
            flops=micros * 100_000_000_000, transcendentals=0, bytes_accessed=micros * 300_000_000
        ),
        compiler_params=pltpu.CompilerParams(vmem_limit_bytes=VMEM_LIMIT),
    )


def near(value):
    return pltpu.with_memory_space_constraint(value, pltpu.VMEM)


def flip(value, axis, mask):
    pairs = [(source, source ^ mask) for source in range(lax.axis_size(axis))]
    return near(lax.ppermute(value, axis, pairs))


def after(value, *earlier):
    return lax.optimization_barrier((value, *earlier))[0]


def place_of(order, rows):
    depth = rows // WIDE
    return order % depth * WIDE + order // depth % STEPS * MID + order // (STEPS * depth)


def to_order(rows):
    new = lax.broadcasted_iota(jnp.int32, (rows, rows), 0)
    old = lax.broadcasted_iota(jnp.int32, (rows, rows), 1)
    return (old == place_of(new, rows)).astype(jnp.bfloat16)


def to_position(rows):
    new = lax.broadcasted_iota(jnp.int32, (rows, rows), 0)
    old = lax.broadcasted_iota(jnp.int32, (rows, rows), 1)
    return (new == place_of(old, rows)).astype(jnp.bfloat16)


def product(left, right, left_axis=1, right_axis=0):
    return lax.dot_general(
        left,
        right,
        (((left_axis,), (right_axis,)), ((), ())),
        preferred_element_type=jnp.float32,
    )


def norm_body(*refs):
    count = len(refs) // 2 - 1
    x_refs, gain_ref, bias_ref, out_refs = refs[:count], refs[count], refs[count + 1], refs[count + 2 :]
    order = to_order(x_refs[0].shape[0])
    gain = gain_ref[...][None, :]
    bias = bias_ref[...][None, :]
    for x_ref, out_ref in zip(x_refs, out_refs):
        floats = x_ref[...].astype(jnp.float32)
        centred = floats - jnp.mean(floats, axis=-1, keepdims=True)
        spread = jnp.mean(centred * centred, axis=-1, keepdims=True)
        normed = (centred * lax.rsqrt(spread + 1e-05) * gain + bias).astype(jnp.bfloat16)
        out_ref[...] = product(order, normed).astype(jnp.bfloat16)


def group_indices():
    shard = lax.axis_index("ctx")
    return shard % SHARDS, shard // SHARDS


def head_slice(index, part=0):
    low = part * GROUP_WIDTH + index * HEAD_DIM
    return slice(low, low + HEAD_DIM)


def pair_slices(index):
    return head_slice(index, 0), head_slice(index, 1)


def wide_rows(head, rows):
    depth = rows // WIDE
    start = head % MID * (STEPS * depth) + head % WIDE // MID * depth
    return pl.ds(pl.multiple_of(start, depth), depth)


def middle_rows(head, rows):
    count = rows // MID
    return pl.ds(pl.multiple_of(head % MID * count, count), count)


def assemble(whole_ref, refs, sources):
    width = whole_ref.shape[1]
    for ref, source in zip(refs, sources):
        rows, wide = ref.shape
        start = wide - width if width == GROUP_WIDTH else 0
        whole_ref[pl.ds(pl.multiple_of(source * rows, 16), rows), :] = ref[:, start : start + width]


def sources(n_mp, turn, shared):
    mp_index = lax.axis_index("mp")
    if shared:
        return [mp_index, mp_index ^ 1, mp_index ^ (2 + turn), mp_index ^ (3 - turn)]
    return [mp_index ^ apart for apart in range(n_mp)]


def project_body(n_mp, shared, *refs):
    normed_refs, refs = refs[:SHARDS], refs[SHARDS:]
    weight_refs, (*out_refs, whole_ref) = refs[:n_mp], refs[n_mp:]
    _, group = group_indices()
    assemble(whole_ref, weight_refs, sources(n_mp, group % 2, shared))
    for normed_ref, out_ref in zip(normed_refs, out_refs):
        out_ref[...] = product(normed_ref[...], whole_ref[...]).astype(jnp.bfloat16)


def key_value_body(n_mp, shared, *refs):
    *refs, sent_ref, whole_ref = refs
    project_body(n_mp, shared, *refs, whole_ref)
    out_refs = refs[-SHARDS:]
    member, _ = group_indices()
    shard_rows = out_refs[0].shape[0]
    depth = shard_rows // WIDE
    for index in range(GROUP_HEADS):
        taken = wide_rows(member * GROUP_HEADS + index, shard_rows)
        for shard, out_ref in enumerate(out_refs):
            sent_ref[index, shard * depth : (shard + 1) * depth, :] = jnp.concatenate(
                [out_ref[taken, at] for at in pair_slices(index)], axis=1
            )


def branch(query, key, value, bias):
    score = product(key, query, 1, 1) * SCALE + bias
    largest = jnp.max(score, axis=0, keepdims=True)
    weight = jnp.exp2(score - largest)
    total = jnp.sum(weight, axis=0, keepdims=True)
    return largest, total, product(value, weight.astype(jnp.bfloat16), 0, 0)


def key_bias(position, valid):
    return jnp.where(position < valid, 0.0, NEG_FILL).astype(jnp.float32)


def merge(one, two):
    top = jnp.maximum(one[0], two[0])
    left = jnp.exp2(one[0] - top)
    right = jnp.exp2(two[0] - top)
    return top, left * one[1] + right * two[1], left * one[2] + right * two[2]


def near_body(valid_ref, *refs):
    q_refs, refs = refs[:SHARDS], refs[SHARDS:]
    kv_refs, (max_ref, sum_ref, num_ref) = refs[:SHARDS], refs[SHARDS:]
    member, group = group_indices()
    valid = valid_ref[0]
    rows = q_refs[0].shape[0]
    count = rows // MID
    bases = [(group * SHARDS + (member ^ apart)) * rows for apart in range(SHARDS)]
    place = place_of(lax.broadcasted_iota(jnp.int32, (rows, LANES), 0), rows)
    lane = lax.broadcasted_iota(jnp.int32, (1, rows), 1)

    def widen(bias):
        return jnp.concatenate([bias] * (rows // LANES), axis=1)

    for shard, (q_ref, kv_ref) in enumerate(zip(q_refs, kv_refs)):
        bias = widen(key_bias(place + bases[shard], valid))
        for index in range(GROUP_HEADS):
            key_at, value_at = pair_slices(index)
            stats = branch(q_ref[:, head_slice(index)], kv_ref[:, key_at], kv_ref[:, value_at], bias)
            max_ref[index, shard], sum_ref[index, shard], num_ref[index, shard] = stats
    entry = lax.broadcasted_iota(jnp.int32, (count, LANES), 0)
    depth = rows // WIDE
    for index in range(GROUP_HEADS):
        head = member * GROUP_HEADS + index
        taken = middle_rows(head, rows)
        key_at, value_at = pair_slices(index)
        query, key, value = (
            jnp.concatenate([ref[taken, at] for ref in some], axis=0)
            for some, at in ((q_refs, head_slice(index)), (kv_refs, key_at), (kv_refs, value_at))
        )
        position = entry % depth * WIDE + entry // depth * MID + head % MID
        bias = widen(
            jnp.concatenate([key_bias(position + base, valid) for base in bases], axis=0)
        )
        middle = branch(query, key, value, bias)
        inside = lane // count == head % MID
        for shard in range(SHARDS):
            largest, total, number = (
                jnp.concatenate([entry[:, shard * count : (shard + 1) * count]] * MID, axis=1)
                for entry in middle
            )
            merged = merge(
                (max_ref[index, shard], sum_ref[index, shard], num_ref[index, shard]),
                (jnp.where(inside, largest, NEG_FILL), total, number),
            )
            max_ref[index, shard], sum_ref[index, shard], num_ref[index, shard] = merged


def far_body(n_groups, valid_ref, *refs):
    q_refs, refs = refs[:SHARDS], refs[SHARDS:]
    sent_refs, refs = refs[:n_groups], refs[n_groups:]
    (max_ref, sum_ref, num_ref), out_refs = refs[:3], refs[3:]
    member, group = group_indices()
    valid = valid_ref[0]
    rows = q_refs[0].shape[0]
    depth = rows // WIDE
    count = SHARDS * depth
    entry = lax.broadcasted_iota(jnp.int32, (count, count), 0)
    lane = lax.broadcasted_iota(jnp.int32, (1, rows), 1)
    for index in range(GROUP_HEADS):
        head = member * GROUP_HEADS + index
        taken = wide_rows(head, rows)
        query = jnp.concatenate([ref[taken, head_slice(index)] for ref in q_refs], axis=0)
        bias = jnp.concatenate(
            [
                key_bias(
                    ((group ^ apart) * SHARDS + (member ^ (entry // depth))) * rows
                    + entry % depth * WIDE
                    + head,
                    valid,
                )
                for apart in range(n_groups)
            ],
            axis=0,
        )
        both = jnp.concatenate([ref[index] for ref in sent_refs], axis=0)
        stats = branch(query, both[:, :HEAD_DIM], both[:, HEAD_DIM:], bias)
        stacked = jnp.concatenate(
            [stats[2], jnp.broadcast_to(stats[0], (8, count)), jnp.broadcast_to(stats[1], (8, count))],
            axis=0,
        )
        stacked = jnp.concatenate(
            [stacked, jnp.zeros((stacked.shape[0], LANES - count), jnp.float32)], axis=1
        )
        block = head % MID * STEPS + head % WIDE // MID
        inside = lane // depth == block
        for shard, out_ref in enumerate(out_refs):
            shift = (block * depth - shard * depth + LANES) % LANES
            moved = jnp.concatenate(
                [pltpu.roll(stacked, shift, 1)] * (rows // LANES), axis=1
            )
            _, total, number = merge(
                (max_ref[index, shard], sum_ref[index, shard], num_ref[index, shard]),
                (
                    jnp.where(inside, moved[HEAD_DIM : HEAD_DIM + 1], NEG_FILL),
                    moved[HEAD_DIM + 8 : HEAD_DIM + 9],
                    moved[:HEAD_DIM],
                ),
            )
            base = (group * SHARDS + (member ^ shard)) * rows
            attention = jnp.where(
                base + place_of(lane, rows) < valid, number * (1.0 / total), 0.0
            )
            out_ref[index * HEAD_DIM : (index + 1) * HEAD_DIM, :] = attention.astype(jnp.bfloat16)


def gather_body(n_mp, shared, *refs):
    *part_refs, out_ref = refs
    assemble(out_ref, part_refs, sources(n_mp, lax.axis_index("ctx") % 2, shared))


def update_body(*refs):
    *part_refs, weight_ref, base_ref, out_ref = refs
    first = SHARDS // 2 if base_ref.dtype == jnp.float32 else 0
    member, _ = group_indices()
    order = to_position(base_ref.shape[0])
    update = base_ref[...].astype(jnp.float32)
    for apart, ref in enumerate(part_refs):
        part = product(order, ref[...], 1, 1).astype(jnp.bfloat16)
        start = (member ^ (first + apart)) * GROUP_WIDTH
        update = update + product(
            part, weight_ref[pl.ds(pl.multiple_of(start, GROUP_WIDTH), GROUP_WIDTH), :]
        )
    out_ref[...] = update.astype(out_ref.dtype)


def fetch(value, turns, shared, pair_mask, earlier=()):
    n_mp, n_ctx = lax.axis_size("mp"), lax.axis_size("ctx")
    if not shared:
        return [flip(value, "mp", apart) for apart in range(1, n_mp)]
    pairs = [
        (c * n_mp + z, c * n_mp + (z ^ (2 + turns(c)))) for c in range(n_ctx) for z in range(n_mp)
    ]
    direct = near(lax.ppermute(value, ("ctx", "mp"), pairs))
    return [direct, flip(after(direct, *earlier), "ctx", pair_mask)]


def local(tile_embeds, norm_gain, norm_bias, w_qkv, w_out, valid_count):
    x = tile_embeds[0]
    rows, width = x.shape
    n_mp = lax.axis_size("mp")
    n_groups = lax.axis_size("ctx") // SHARDS
    depth = rows // WIDE
    weight_rows = w_qkv.shape[0]
    member, _ = group_indices()
    bf16, f32 = jnp.bfloat16, jnp.float32
    shape = pltpu.VMEM
    shared = n_mp == 4 and n_groups % 2 == 0

    def columns(part):
        start = part * width + member * GROUP_WIDTH
        return lax.dynamic_slice(w_qkv, (0, start), (weight_rows, GROUP_WIDTH))

    key_value = jnp.concatenate([columns(1), columns(2)], axis=1)
    query = columns(0)
    mine = near(jnp.concatenate([key_value, query], axis=1))
    closest = [flip(mine, "mp", 1)] if shared else []
    weights = []
    for value in (key_value, query):
        earlier = [blocks[1 + len(closest)] for blocks in weights]
        others = fetch(near(value), lambda c: c // SHARDS % 2, shared, SHARDS, earlier)
        weights.append([mine] + closest + others)

    x_pair = flip(x, "ctx", 1)
    x_far = flip(x, "ctx", 2)
    x_far = after(x_far, weights[0][2])
    x_last = flip(x_far, "ctx", 1)
    x_own = near(x)
    gain, bias = near(norm_gain), near(norm_bias)
    normed = []
    for pair in ((x_own, x_pair), (x_far, x_last)):
        normed += call(norm_body, [shape((rows, width), bf16)] * 2, n_in=4, micros=1)(
            *pair, gain, bias
        )

    out_weight = after(near(w_out), normed[2])
    out_parts = [out_weight]
    if shared:
        out_parts.append(flip(out_weight, "mp", 1))
    out_parts += fetch(out_weight, lambda c: c % 2, shared, 1)

    *kv, sent = call(
        lambda *refs: key_value_body(n_mp, shared, *refs),
        [shape((rows, 2 * GROUP_WIDTH), bf16)] * SHARDS
        + [shape((GROUP_HEADS, SHARDS * depth, 2 * HEAD_DIM), bf16)],
        scratch=[pltpu.VMEM((width, 2 * GROUP_WIDTH), bf16)],
        n_in=SHARDS + n_mp,
        micros=2,
    )(*normed, *weights[0])
    sents = [sent] + [flip(sent, "ctx", SHARDS * apart) for apart in range(1, n_groups)]
    q = call(
        lambda *refs: project_body(n_mp, shared, *refs),
        [shape((rows, GROUP_WIDTH), bf16)] * SHARDS,
        scratch=[pltpu.VMEM((width, GROUP_WIDTH), bf16)],
        n_in=SHARDS + n_mp,
        micros=1,
    )(*normed, *weights[1])
    stats = call(
        near_body,
        [
            shape((GROUP_HEADS, SHARDS, 1, rows), f32),
            shape((GROUP_HEADS, SHARDS, 1, rows), f32),
            shape((GROUP_HEADS, SHARDS, HEAD_DIM, rows), f32),
        ],
        n_scalar=1,
        n_in=2 * SHARDS,
        micros=50,
    )(valid_count, *q, *kv)
    attention = call(
        lambda *refs: far_body(n_groups, *refs),
        [shape((GROUP_WIDTH, rows), bf16)] * SHARDS,
        n_scalar=1,
        n_in=SHARDS + n_groups + 3,
        micros=1,
    )(valid_count, *q, *sents, *stats)
    received = [attention[0]] + [flip(attention[apart], "ctx", apart) for apart in range(1, SHARDS)]
    (whole_out,) = call(
        lambda *refs: gather_body(n_mp, shared, *refs),
        [shape((width, width), bf16)],
        n_in=n_mp,
    )(*out_parts)
    half = SHARDS // 2
    (partial,) = call(update_body, [shape((rows, width), f32)], n_in=half + 2, micros=1)(
        *received[:half], whole_out, x_own
    )
    (out,) = call(
        update_body, [jax.ShapeDtypeStruct((rows, width), bf16)], n_in=half + 2, micros=1
    )(*received[half:], whole_out, partial)
    return out[None]


def solution(mesh):
    placed = (P("mp", "ctx", None), P(), P(), P("mp", None), P("mp", None), P("mp"))
    return jax.shard_map(
        local, mesh=mesh, in_specs=placed, out_specs=P("mp", "ctx", None), check_vma=False
    )
```

```python
import math

import jax
import jax.numpy as jnp
from jax import lax
from jax.experimental import pallas as pl
from jax.experimental.pallas import tpu as pltpu
from jax.sharding import PartitionSpec as P

HEADS = 12
HEAD_DIM = 64
MID = 4
WIDE = 16
SHARDS = 4
STEPS = WIDE // MID
GROUP_HEADS = HEADS // SHARDS
GROUP_WIDTH = GROUP_HEADS * HEAD_DIM
NEG_FILL = -1e30
SCALE = math.log2(math.e) / math.sqrt(HEAD_DIM)
VMEM_LIMIT = 24 * 1024 * 1024
LANES = 128


def call(body, out_shape, scratch=(), n_scalar=0, n_in=0, micros=1):
    specs = [pl.BlockSpec(memory_space=pltpu.SMEM)] * n_scalar + [
        pl.BlockSpec(memory_space=pltpu.VMEM)
    ] * n_in
    outs = [pl.BlockSpec(memory_space=pltpu.VMEM) for _ in out_shape]
    return pl.pallas_call(
        body,
        out_shape=out_shape,
        in_specs=specs,
        out_specs=outs,
        scratch_shapes=list(scratch),
        cost_estimate=pl.CostEstimate(
            flops=int(micros * 3_000_000_000), transcendentals=0, bytes_accessed=int(micros * 9_000_000)
        ),
        compiler_params=pltpu.CompilerParams(vmem_limit_bytes=VMEM_LIMIT),
    )


def near(value):
    return pltpu.with_memory_space_constraint(value, pltpu.VMEM)


def flip(value, axis, mask):
    pairs = [(source, source ^ mask) for source in range(lax.axis_size(axis))]
    return near(lax.ppermute(value, axis, pairs))


def after(value, *earlier):
    return lax.optimization_barrier((value, *earlier))[0]


def place_of(order, rows):
    depth = rows // WIDE
    return order % depth * WIDE + order // depth % STEPS * MID + order // (STEPS * depth)


def to_order(rows):
    new = lax.broadcasted_iota(jnp.int32, (rows, rows), 0)
    old = lax.broadcasted_iota(jnp.int32, (rows, rows), 1)
    return (old == place_of(new, rows)).astype(jnp.bfloat16)


def to_position(rows):
    new = lax.broadcasted_iota(jnp.int32, (rows, rows), 0)
    old = lax.broadcasted_iota(jnp.int32, (rows, rows), 1)
    return (new == place_of(old, rows)).astype(jnp.bfloat16)


def product(left, right, left_axis=1, right_axis=0):
    return lax.dot_general(
        left,
        right,
        (((left_axis,), (right_axis,)), ((), ())),
        preferred_element_type=jnp.float32,
    )


def norm_body(*refs):
    count = len(refs) // 2 - 1
    x_refs, gain_ref, bias_ref, out_refs = refs[:count], refs[count], refs[count + 1], refs[count + 2 :]
    order = to_order(x_refs[0].shape[0])
    gain = gain_ref[...][None, :]
    bias = bias_ref[...][None, :]
    for x_ref, out_ref in zip(x_refs, out_refs):
        floats = x_ref[...].astype(jnp.float32)
        centred = floats - jnp.mean(floats, axis=-1, keepdims=True)
        spread = jnp.mean(centred * centred, axis=-1, keepdims=True)
        normed = (centred * lax.rsqrt(spread + 1e-05) * gain + bias).astype(jnp.bfloat16)
        out_ref[...] = product(order, normed).astype(jnp.bfloat16)


def group_indices():
    shard = lax.axis_index("ctx")
    return shard % SHARDS, shard // SHARDS


def head_slices(index):
    return [
        slice(part * GROUP_WIDTH + index * HEAD_DIM, part * GROUP_WIDTH + (index + 1) * HEAD_DIM)
        for part in range(3)
    ]


def wide_rows(head, rows):
    depth = rows // WIDE
    start = head % MID * (STEPS * depth) + head % WIDE // MID * depth
    return pl.ds(pl.multiple_of(start, depth), depth)


def middle_rows(head, rows):
    count = rows // MID
    return pl.ds(pl.multiple_of(head % MID * count, count), count)


def assemble(whole_ref, refs, sources):
    for ref, source in zip(refs, sources):
        rows = ref.shape[0]
        whole_ref[pl.ds(pl.multiple_of(source * rows, 16), rows), :] = ref[...]


def sources(n_mp, turn, shared):
    mp_index = lax.axis_index("mp")
    if shared:
        return [mp_index, mp_index ^ 1, mp_index ^ (2 + turn), mp_index ^ (3 - turn)]
    return [mp_index ^ apart for apart in range(n_mp)]


def project_body(n_mp, shared, *refs):
    normed_refs, refs = refs[:SHARDS], refs[SHARDS:]
    weight_refs, (*out_refs, sent_ref, whole_ref) = refs[:n_mp], refs[n_mp:]
    member, group = group_indices()
    assemble(whole_ref, weight_refs, sources(n_mp, group % 2, shared))
    for normed_ref, out_ref in zip(normed_refs, out_refs):
        out_ref[...] = product(normed_ref[...], whole_ref[...]).astype(jnp.bfloat16)
    shard_rows = out_refs[0].shape[0]
    depth = shard_rows // WIDE
    for index in range(GROUP_HEADS):
        _, key_at, value_at = head_slices(index)
        taken = wide_rows(member * GROUP_HEADS + index, shard_rows)
        for shard, out_ref in enumerate(out_refs):
            sent_ref[index, shard * depth : (shard + 1) * depth, :] = jnp.concatenate(
                [out_ref[taken, key_at], out_ref[taken, value_at]], axis=1
            )


def branch(query, key, value, bias):
    score = product(key, query, 1, 1) * SCALE + bias
    largest = jnp.max(score, axis=0, keepdims=True)
    weight = jnp.exp2(score - largest)
    total = jnp.sum(weight, axis=0, keepdims=True)
    return largest, total, product(value, weight.astype(jnp.bfloat16), 0, 0)


def key_bias(position, valid):
    return jnp.where(position < valid, 0.0, NEG_FILL).astype(jnp.float32)


def merge(one, two):
    top = jnp.maximum(one[0], two[0])
    left = jnp.exp2(one[0] - top)
    right = jnp.exp2(two[0] - top)
    return top, left * one[1] + right * two[1], left * one[2] + right * two[2]


def near_body(valid_ref, *refs):
    qkv_refs, (max_ref, sum_ref, num_ref) = refs[:SHARDS], refs[SHARDS:]
    member, group = group_indices()
    valid = valid_ref[0]
    rows = qkv_refs[0].shape[0]
    count = rows // MID
    bases = [(group * SHARDS + (member ^ apart)) * rows for apart in range(SHARDS)]
    place = place_of(lax.broadcasted_iota(jnp.int32, (rows, LANES), 0), rows)
    lane = lax.broadcasted_iota(jnp.int32, (1, rows), 1)

    def widen(bias):
        return jnp.concatenate([bias] * (rows // LANES), axis=1)

    for shard, ref in enumerate(qkv_refs):
        bias = widen(key_bias(place + bases[shard], valid))
        for index in range(GROUP_HEADS):
            stats = branch(*(ref[:, at] for at in head_slices(index)), bias)
            max_ref[index, shard], sum_ref[index, shard], num_ref[index, shard] = stats
    entry = lax.broadcasted_iota(jnp.int32, (count, LANES), 0)
    depth = rows // WIDE
    for index in range(GROUP_HEADS):
        head = member * GROUP_HEADS + index
        taken = middle_rows(head, rows)
        query, key, value = (
            jnp.concatenate([ref[taken, at] for ref in qkv_refs], axis=0)
            for at in head_slices(index)
        )
        position = entry % depth * WIDE + entry // depth * MID + head % MID
        bias = widen(
            jnp.concatenate([key_bias(position + base, valid) for base in bases], axis=0)
        )
        middle = branch(query, key, value, bias)
        inside = lane // count == head % MID
        for shard in range(SHARDS):
            largest, total, number = (
                jnp.concatenate([entry[:, shard * count : (shard + 1) * count]] * MID, axis=1)
                for entry in middle
            )
            merged = merge(
                (max_ref[index, shard], sum_ref[index, shard], num_ref[index, shard]),
                (jnp.where(inside, largest, NEG_FILL), total, number),
            )
            max_ref[index, shard], sum_ref[index, shard], num_ref[index, shard] = merged


def far_body(n_groups, valid_ref, *refs):
    qkv_refs, refs = refs[:SHARDS], refs[SHARDS:]
    sent_refs, refs = refs[:n_groups], refs[n_groups:]
    (max_ref, sum_ref, num_ref), out_refs = refs[:3], refs[3:]
    member, group = group_indices()
    valid = valid_ref[0]
    rows = qkv_refs[0].shape[0]
    depth = rows // WIDE
    count = SHARDS * depth
    entry = lax.broadcasted_iota(jnp.int32, (count, count), 0)
    lane = lax.broadcasted_iota(jnp.int32, (1, rows), 1)
    for index in range(GROUP_HEADS):
        head = member * GROUP_HEADS + index
        taken = wide_rows(head, rows)
        query_at = head_slices(index)[0]
        query = jnp.concatenate([ref[taken, query_at] for ref in qkv_refs], axis=0)
        bias = jnp.concatenate(
            [
                key_bias(
                    ((group ^ apart) * SHARDS + (member ^ (entry // depth))) * rows
                    + entry % depth * WIDE
                    + head,
                    valid,
                )
                for apart in range(n_groups)
            ],
            axis=0,
        )
        both = jnp.concatenate([ref[index] for ref in sent_refs], axis=0)
        stats = branch(query, both[:, :HEAD_DIM], both[:, HEAD_DIM:], bias)
        stacked = jnp.concatenate(
            [stats[2], jnp.broadcast_to(stats[0], (8, count)), jnp.broadcast_to(stats[1], (8, count))],
            axis=0,
        )
        stacked = jnp.concatenate(
            [stacked, jnp.zeros((stacked.shape[0], LANES - count), jnp.float32)], axis=1
        )
        block = head % MID * STEPS + head % WIDE // MID
        inside = lane // depth == block
        for shard, out_ref in enumerate(out_refs):
            shift = (block * depth - shard * depth + LANES) % LANES
            moved = jnp.concatenate(
                [pltpu.roll(stacked, shift, 1)] * (rows // LANES), axis=1
            )
            _, total, number = merge(
                (max_ref[index, shard], sum_ref[index, shard], num_ref[index, shard]),
                (
                    jnp.where(inside, moved[HEAD_DIM : HEAD_DIM + 1], NEG_FILL),
                    moved[HEAD_DIM + 8 : HEAD_DIM + 9],
                    moved[:HEAD_DIM],
                ),
            )
            base = (group * SHARDS + (member ^ shard)) * rows
            attention = jnp.where(
                base + place_of(lane, rows) < valid, number * (1.0 / total), 0.0
            )
            out_ref[index * HEAD_DIM : (index + 1) * HEAD_DIM, :] = attention.astype(jnp.bfloat16)


def gather_body(n_mp, shared, *refs):
    *part_refs, out_ref = refs
    assemble(out_ref, part_refs, sources(n_mp, lax.axis_index("ctx") % 2, shared))


def update_body(*refs):
    *part_refs, weight_ref, base_ref, out_ref = refs
    first = SHARDS // 2 if base_ref.dtype == jnp.float32 else 0
    member, _ = group_indices()
    order = to_position(base_ref.shape[0])
    update = base_ref[...].astype(jnp.float32)
    for apart, ref in enumerate(part_refs):
        part = product(order, ref[...], 1, 1).astype(jnp.bfloat16)
        start = (member ^ (first + apart)) * GROUP_WIDTH
        update = update + product(
            part, weight_ref[pl.ds(pl.multiple_of(start, GROUP_WIDTH), GROUP_WIDTH), :]
        )
    out_ref[...] = update.astype(out_ref.dtype)


def fetch(value, turns, shared, pair_mask, earlier=()):
    n_mp, n_ctx = lax.axis_size("mp"), lax.axis_size("ctx")
    if not shared:
        return [flip(value, "mp", apart) for apart in range(1, n_mp)]
    pairs = [
        (c * n_mp + z, c * n_mp + (z ^ (2 + turns(c)))) for c in range(n_ctx) for z in range(n_mp)
    ]
    direct = near(lax.ppermute(value, ("ctx", "mp"), pairs))
    return [direct, flip(after(direct, *earlier), "ctx", pair_mask)]


def local(tile_embeds, norm_gain, norm_bias, w_qkv, w_out, valid_count):
    x = tile_embeds[0]
    rows, width = x.shape
    n_mp = lax.axis_size("mp")
    n_groups = lax.axis_size("ctx") // SHARDS
    depth = rows // WIDE
    weight_rows = w_qkv.shape[0]
    member, _ = group_indices()
    bf16, f32 = jnp.bfloat16, jnp.float32
    shape = pltpu.VMEM
    shared = n_mp == 4 and n_groups % 2 == 0

    def columns(part):
        start = part * width + member * GROUP_WIDTH
        return lax.dynamic_slice(w_qkv, (0, start), (weight_rows, GROUP_WIDTH))

    mine = near(jnp.concatenate([columns(part) for part in range(3)], axis=1))
    others = fetch(mine, lambda c: c // SHARDS % 2, shared, SHARDS)

    x_pair = flip(x, "ctx", 1)
    x_far = flip(after(x, mine), "ctx", 2)
    weights = [mine] + ([flip(after(mine, x_far), "mp", 1)] if shared else []) + others
    x_far = after(x_far, others[0])
    x_last = flip(x_far, "ctx", 1)
    x_own = near(x)
    gain, bias = near(norm_gain), near(norm_bias)
    normed = []
    for pair in ((x_own, x_pair), (x_far, x_last)):
        normed += call(norm_body, [shape((rows, width), bf16)] * 2, n_in=4, micros=0.01)(
            *pair, gain, bias
        )

    out_weight = after(near(w_out), normed[2])
    out_parts = [out_weight]
    if shared:
        out_parts.append(flip(out_weight, "mp", 1))
    *qkv, sent = call(
        lambda *refs: project_body(n_mp, shared, *refs),
        [shape((rows, 3 * GROUP_WIDTH), bf16)] * SHARDS
        + [shape((GROUP_HEADS, SHARDS * depth, 2 * HEAD_DIM), bf16)],
        scratch=[pltpu.VMEM((width, 3 * GROUP_WIDTH), bf16)],
        n_in=SHARDS + n_mp,
        micros=2,
    )(*normed, *weights)
    sents = [sent] + [flip(sent, "ctx", SHARDS * apart) for apart in range(1, n_groups)]
    stats = call(
        near_body,
        [
            shape((GROUP_HEADS, SHARDS, 1, rows), f32),
            shape((GROUP_HEADS, SHARDS, 1, rows), f32),
            shape((GROUP_HEADS, SHARDS, HEAD_DIM, rows), f32),
        ],
        n_scalar=1,
        n_in=SHARDS,
        micros=5,
    )(valid_count, *qkv)
    out_parts += fetch(out_weight, lambda c: c % 2, shared, 1, stats[:1])
    attention = call(
        lambda *refs: far_body(n_groups, *refs),
        [shape((GROUP_WIDTH, rows), bf16)] * SHARDS,
        n_scalar=1,
        n_in=SHARDS + n_groups + 3,
        micros=1,
    )(valid_count, *qkv, *sents, after(stats[0], *out_parts[:3]), *stats[1:])
    received = [attention[0]] + [flip(attention[apart], "ctx", apart) for apart in range(1, SHARDS)]
    (whole_out,) = call(
        lambda *refs: gather_body(n_mp, shared, *refs),
        [shape((width, width), bf16)],
        n_in=n_mp,
    )(*out_parts)
    half = SHARDS // 2
    (partial,) = call(update_body, [shape((rows, width), f32)], n_in=half + 2, micros=1)(
        *received[:half], whole_out, x_own
    )
    (out,) = call(
        update_body, [jax.ShapeDtypeStruct((rows, width), bf16)], n_in=half + 2, micros=1
    )(*received[half:], whole_out, partial)
    return out[None]


def solution(mesh):
    placed = (P("mp", "ctx", None), P(), P(), P("mp", None), P("mp", None), P("mp"))
    return jax.shard_map(
        local, mesh=mesh, in_specs=placed, out_specs=P("mp", "ctx", None), check_vma=False
    )
```

```python
import math

import jax
import jax.numpy as jnp
from jax import lax
from jax.experimental import pallas as pl
from jax.experimental.pallas import tpu as pltpu
from jax.sharding import PartitionSpec as P

HEADS = 12
HEAD_DIM = 64
MID = 4
WIDE = 16
SHARDS = 4
STEPS = WIDE // MID
GROUP_HEADS = HEADS // SHARDS
GROUP_WIDTH = GROUP_HEADS * HEAD_DIM
NEG_FILL = -1e30
SCALE = math.log2(math.e) / math.sqrt(HEAD_DIM)
VMEM_LIMIT = 24 * 1024 * 1024
LANES = 128


def call(body, out_shape, scratch=(), n_scalar=0, n_in=0, micros=1):
    specs = [pl.BlockSpec(memory_space=pltpu.SMEM)] * n_scalar + [
        pl.BlockSpec(memory_space=pltpu.VMEM)
    ] * n_in
    outs = [pl.BlockSpec(memory_space=pltpu.VMEM) for _ in out_shape]
    return pl.pallas_call(
        body,
        out_shape=out_shape,
        in_specs=specs,
        out_specs=outs,
        scratch_shapes=list(scratch),
        cost_estimate=pl.CostEstimate(
            flops=int(micros * 3_000_000_000), transcendentals=0, bytes_accessed=int(micros * 9_000_000)
        ),
        compiler_params=pltpu.CompilerParams(vmem_limit_bytes=VMEM_LIMIT),
    )


def near(value):
    return pltpu.with_memory_space_constraint(value, pltpu.VMEM)


def flip(value, axis, mask):
    pairs = [(source, source ^ mask) for source in range(lax.axis_size(axis))]
    return near(lax.ppermute(value, axis, pairs))


def after(value, *earlier):
    return lax.optimization_barrier((value, *earlier))[0]


def place_of(order, rows):
    depth = rows // WIDE
    return order % depth * WIDE + order // depth % STEPS * MID + order // (STEPS * depth)


def to_order(rows):
    new = lax.broadcasted_iota(jnp.int32, (rows, rows), 0)
    old = lax.broadcasted_iota(jnp.int32, (rows, rows), 1)
    return (old == place_of(new, rows)).astype(jnp.bfloat16)


def to_position(rows):
    new = lax.broadcasted_iota(jnp.int32, (rows, rows), 0)
    old = lax.broadcasted_iota(jnp.int32, (rows, rows), 1)
    return (new == place_of(old, rows)).astype(jnp.bfloat16)


def product(left, right, left_axis=1, right_axis=0):
    return lax.dot_general(
        left,
        right,
        (((left_axis,), (right_axis,)), ((), ())),
        preferred_element_type=jnp.float32,
    )


def norm_body(*refs):
    count = len(refs) // 2 - 1
    x_refs, gain_ref, bias_ref, out_refs = refs[:count], refs[count], refs[count + 1], refs[count + 2 :]
    order = to_order(x_refs[0].shape[0])
    gain = gain_ref[...][None, :]
    bias = bias_ref[...][None, :]
    for x_ref, out_ref in zip(x_refs, out_refs):
        floats = x_ref[...].astype(jnp.float32)
        centred = floats - jnp.mean(floats, axis=-1, keepdims=True)
        spread = jnp.mean(centred * centred, axis=-1, keepdims=True)
        normed = (centred * lax.rsqrt(spread + 1e-05) * gain + bias).astype(jnp.bfloat16)
        out_ref[...] = product(order, normed).astype(jnp.bfloat16)


def group_indices():
    shard = lax.axis_index("ctx")
    return shard % SHARDS, shard // SHARDS


def head_slices(index):
    return [
        slice(part * GROUP_WIDTH + index * HEAD_DIM, part * GROUP_WIDTH + (index + 1) * HEAD_DIM)
        for part in range(3)
    ]


def wide_rows(head, rows):
    depth = rows // WIDE
    start = head % MID * (STEPS * depth) + head % WIDE // MID * depth
    return pl.ds(pl.multiple_of(start, depth), depth)


def middle_rows(head, rows):
    count = rows // MID
    return pl.ds(pl.multiple_of(head % MID * count, count), count)


def assemble(whole_ref, refs, sources):
    for ref, source in zip(refs, sources):
        rows = ref.shape[0]
        whole_ref[pl.ds(pl.multiple_of(source * rows, 16), rows), :] = ref[...]


def sources(n_mp, turn, shared):
    mp_index = lax.axis_index("mp")
    if shared:
        return [mp_index, mp_index ^ 1, mp_index ^ (2 + turn), mp_index ^ (3 - turn)]
    return [mp_index ^ apart for apart in range(n_mp)]


def project_body(n_mp, shared, *refs):
    normed_refs, refs = refs[:SHARDS], refs[SHARDS:]
    weight_refs, (*out_refs, sent_ref, whole_ref) = refs[:n_mp], refs[n_mp:]
    member, group = group_indices()
    assemble(whole_ref, weight_refs, sources(n_mp, group % 2, shared))
    for normed_ref, out_ref in zip(normed_refs, out_refs):
        out_ref[...] = product(normed_ref[...], whole_ref[...]).astype(jnp.bfloat16)
    shard_rows = out_refs[0].shape[0]
    depth = shard_rows // WIDE
    for index in range(GROUP_HEADS):
        _, key_at, value_at = head_slices(index)
        taken = wide_rows(member * GROUP_HEADS + index, shard_rows)
        for shard, out_ref in enumerate(out_refs):
            sent_ref[index, shard * depth : (shard + 1) * depth, :] = jnp.concatenate(
                [out_ref[taken, key_at], out_ref[taken, value_at]], axis=1
            )


def branch(query, key, value, bias):
    score = product(key, query, 1, 1) * SCALE + bias
    largest = jnp.max(score, axis=0, keepdims=True)
    weight = jnp.exp2(score - largest)
    total = jnp.sum(weight, axis=0, keepdims=True)
    return largest, total, product(value, weight.astype(jnp.bfloat16), 0, 0)


def key_bias(position, valid):
    return jnp.where(position < valid, 0.0, NEG_FILL).astype(jnp.float32)


def merge(one, two):
    top = jnp.maximum(one[0], two[0])
    left = jnp.exp2(one[0] - top)
    right = jnp.exp2(two[0] - top)
    return top, left * one[1] + right * two[1], left * one[2] + right * two[2]


def near_body(valid_ref, *refs):
    qkv_refs, (max_ref, sum_ref, num_ref) = refs[:SHARDS], refs[SHARDS:]
    member, group = group_indices()
    valid = valid_ref[0]
    rows = qkv_refs[0].shape[0]
    count = rows // MID
    bases = [(group * SHARDS + (member ^ apart)) * rows for apart in range(SHARDS)]
    place = place_of(lax.broadcasted_iota(jnp.int32, (rows, LANES), 0), rows)
    lane = lax.broadcasted_iota(jnp.int32, (1, rows), 1)

    def widen(bias):
        return jnp.concatenate([bias] * (rows // LANES), axis=1)

    for shard, ref in enumerate(qkv_refs):
        bias = widen(key_bias(place + bases[shard], valid))
        for index in range(GROUP_HEADS):
            stats = branch(*(ref[:, at] for at in head_slices(index)), bias)
            max_ref[index, shard], sum_ref[index, shard], num_ref[index, shard] = stats
    entry = lax.broadcasted_iota(jnp.int32, (count, LANES), 0)
    depth = rows // WIDE
    for index in range(GROUP_HEADS):
        head = member * GROUP_HEADS + index
        taken = middle_rows(head, rows)
        query, key, value = (
            jnp.concatenate([ref[taken, at] for ref in qkv_refs], axis=0)
            for at in head_slices(index)
        )
        position = entry % depth * WIDE + entry // depth * MID + head % MID
        bias = widen(
            jnp.concatenate([key_bias(position + base, valid) for base in bases], axis=0)
        )
        middle = branch(query, key, value, bias)
        inside = lane // count == head % MID
        for shard in range(SHARDS):
            largest, total, number = (
                jnp.concatenate([entry[:, shard * count : (shard + 1) * count]] * MID, axis=1)
                for entry in middle
            )
            merged = merge(
                (max_ref[index, shard], sum_ref[index, shard], num_ref[index, shard]),
                (jnp.where(inside, largest, NEG_FILL), total, number),
            )
            max_ref[index, shard], sum_ref[index, shard], num_ref[index, shard] = merged


def far_body(n_groups, valid_ref, *refs):
    qkv_refs, refs = refs[:SHARDS], refs[SHARDS:]
    sent_refs, refs = refs[:n_groups], refs[n_groups:]
    (max_ref, sum_ref, num_ref), out_refs = refs[:3], refs[3:]
    member, group = group_indices()
    valid = valid_ref[0]
    rows = qkv_refs[0].shape[0]
    depth = rows // WIDE
    count = SHARDS * depth
    entry = lax.broadcasted_iota(jnp.int32, (count, count), 0)
    lane = lax.broadcasted_iota(jnp.int32, (1, rows), 1)
    for index in range(GROUP_HEADS):
        head = member * GROUP_HEADS + index
        taken = wide_rows(head, rows)
        query_at = head_slices(index)[0]
        query = jnp.concatenate([ref[taken, query_at] for ref in qkv_refs], axis=0)
        bias = jnp.concatenate(
            [
                key_bias(
                    ((group ^ apart) * SHARDS + (member ^ (entry // depth))) * rows
                    + entry % depth * WIDE
                    + head,
                    valid,
                )
                for apart in range(n_groups)
            ],
            axis=0,
        )
        both = jnp.concatenate([ref[index] for ref in sent_refs], axis=0)
        stats = branch(query, both[:, :HEAD_DIM], both[:, HEAD_DIM:], bias)
        stacked = jnp.concatenate(
            [stats[2], jnp.broadcast_to(stats[0], (8, count)), jnp.broadcast_to(stats[1], (8, count))],
            axis=0,
        )
        stacked = jnp.concatenate(
            [stacked, jnp.zeros((stacked.shape[0], LANES - count), jnp.float32)], axis=1
        )
        block = head % MID * STEPS + head % WIDE // MID
        inside = lane // depth == block
        for shard, out_ref in enumerate(out_refs):
            shift = (block * depth - shard * depth + LANES) % LANES
            moved = jnp.concatenate(
                [pltpu.roll(stacked, shift, 1)] * (rows // LANES), axis=1
            )
            _, total, number = merge(
                (max_ref[index, shard], sum_ref[index, shard], num_ref[index, shard]),
                (
                    jnp.where(inside, moved[HEAD_DIM : HEAD_DIM + 1], NEG_FILL),
                    moved[HEAD_DIM + 8 : HEAD_DIM + 9],
                    moved[:HEAD_DIM],
                ),
            )
            base = (group * SHARDS + (member ^ shard)) * rows
            attention = jnp.where(
                base + place_of(lane, rows) < valid, number * (1.0 / total), 0.0
            )
            out_ref[index * HEAD_DIM : (index + 1) * HEAD_DIM, :] = attention.astype(jnp.bfloat16)


def gather_body(n_mp, shared, *refs):
    *part_refs, out_ref = refs
    assemble(out_ref, part_refs, sources(n_mp, lax.axis_index("ctx") % 2, shared))


def update_body(*refs):
    *part_refs, weight_ref, base_ref, out_ref = refs
    first = SHARDS // 2 if base_ref.dtype == jnp.float32 else 0
    member, _ = group_indices()
    order = to_position(base_ref.shape[0])
    update = base_ref[...].astype(jnp.float32)
    for apart, ref in enumerate(part_refs):
        part = product(order, ref[...], 1, 1).astype(jnp.bfloat16)
        start = (member ^ (first + apart)) * GROUP_WIDTH
        update = update + product(
            part, weight_ref[pl.ds(pl.multiple_of(start, GROUP_WIDTH), GROUP_WIDTH), :]
        )
    out_ref[...] = update.astype(out_ref.dtype)


def fetch(value, turns, shared, pair_mask, earlier=()):
    n_mp, n_ctx = lax.axis_size("mp"), lax.axis_size("ctx")
    if not shared:
        return [flip(value, "mp", apart) for apart in range(1, n_mp)]
    pairs = [
        (c * n_mp + z, c * n_mp + (z ^ (2 + turns(c)))) for c in range(n_ctx) for z in range(n_mp)
    ]
    direct = near(lax.ppermute(value, ("ctx", "mp"), pairs))
    return [direct, flip(after(direct, *earlier), "ctx", pair_mask)]


def local(tile_embeds, norm_gain, norm_bias, w_qkv, w_out, valid_count):
    x = tile_embeds[0]
    rows, width = x.shape
    n_mp = lax.axis_size("mp")
    n_groups = lax.axis_size("ctx") // SHARDS
    depth = rows // WIDE
    weight_rows = w_qkv.shape[0]
    member, _ = group_indices()
    bf16, f32 = jnp.bfloat16, jnp.float32
    shape = pltpu.VMEM
    shared = n_mp == 4 and n_groups % 2 == 0

    def columns(part):
        start = part * width + member * GROUP_WIDTH
        return lax.dynamic_slice(w_qkv, (0, start), (weight_rows, GROUP_WIDTH))

    mine = near(jnp.concatenate([columns(part) for part in range(3)], axis=1))
    others = fetch(mine, lambda c: c // SHARDS % 2, shared, SHARDS)

    x_pair = flip(x, "ctx", 1)
    x_far = flip(after(x, mine), "ctx", 2)
    x_last = flip(after(x, mine), "ctx", 3)
    weights = [mine] + ([flip(mine, "mp", 1)] if shared else []) + others
    x_own = near(x)
    gain, bias = near(norm_gain), near(norm_bias)
    normed = []
    for pair in ((x_own, x_pair), (x_far, x_last)):
        normed += call(norm_body, [shape((rows, width), bf16)] * 2, n_in=4, micros=0.01)(
            *pair, gain, bias
        )

    out_weight = after(near(w_out), others[0])
    out_parts = [out_weight]
    if shared:
        out_parts.append(flip(out_weight, "mp", 1))
    *qkv, sent = call(
        lambda *refs: project_body(n_mp, shared, *refs),
        [shape((rows, 3 * GROUP_WIDTH), bf16)] * SHARDS
        + [shape((GROUP_HEADS, SHARDS * depth, 2 * HEAD_DIM), bf16)],
        scratch=[pltpu.VMEM((width, 3 * GROUP_WIDTH), bf16)],
        n_in=SHARDS + n_mp,
        micros=2,
    )(*normed, *weights)
    sents = [sent] + [flip(sent, "ctx", SHARDS * apart) for apart in range(1, n_groups)]
    stats = call(
        near_body,
        [
            shape((GROUP_HEADS, SHARDS, 1, rows), f32),
            shape((GROUP_HEADS, SHARDS, 1, rows), f32),
            shape((GROUP_HEADS, SHARDS, HEAD_DIM, rows), f32),
        ],
        n_scalar=1,
        n_in=SHARDS,
        micros=5,
    )(valid_count, *qkv)
    attention = call(
        lambda *refs: far_body(n_groups, *refs),
        [shape((GROUP_WIDTH, rows), bf16)] * SHARDS,
        n_scalar=1,
        n_in=SHARDS + n_groups + 3,
        micros=1,
    )(valid_count, *qkv, *sents, *stats)
    out_parts += fetch(out_weight, lambda c: c % 2, shared, 1, attention[1:2])
    received = [attention[0]] + [flip(attention[apart], "ctx", apart) for apart in range(1, SHARDS)]
    (whole_out,) = call(
        lambda *refs: gather_body(n_mp, shared, *refs),
        [shape((width, width), bf16)],
        n_in=n_mp,
    )(*out_parts)
    half = SHARDS // 2
    (partial,) = call(update_body, [shape((rows, width), f32)], n_in=half + 2, micros=1)(
        *received[:half], whole_out, x_own
    )
    (out,) = call(
        update_body, [jax.ShapeDtypeStruct((rows, width), bf16)], n_in=half + 2, micros=1
    )(*received[half:], whole_out, partial)
    return out[None]


def solution(mesh):
    placed = (P("mp", "ctx", None), P(), P(), P("mp", None), P("mp", None), P("mp"))
    return jax.shard_map(
        local, mesh=mesh, in_specs=placed, out_specs=P("mp", "ctx", None), check_vma=False
    )
```

```python
import math

import jax
import jax.numpy as jnp
from jax import lax
from jax.experimental import pallas as pl
from jax.experimental.pallas import tpu as pltpu
from jax.sharding import PartitionSpec as P

HEADS = 12
HEAD_DIM = 64
MID = 4
WIDE = 16
SHARDS = 4
STEPS = WIDE // MID
GROUP_HEADS = HEADS // SHARDS
GROUP_WIDTH = GROUP_HEADS * HEAD_DIM
NEG_FILL = -1e30
SCALE = math.log2(math.e) / math.sqrt(HEAD_DIM)
VMEM_LIMIT = 24 * 1024 * 1024
LANES = 128


def call(body, out_shape, scratch=(), n_scalar=0, n_in=0, micros=1):
    specs = [pl.BlockSpec(memory_space=pltpu.SMEM)] * n_scalar + [
        pl.BlockSpec(memory_space=pltpu.VMEM)
    ] * n_in
    outs = [pl.BlockSpec(memory_space=pltpu.VMEM) for _ in out_shape]
    return pl.pallas_call(
        body,
        out_shape=out_shape,
        in_specs=specs,
        out_specs=outs,
        scratch_shapes=list(scratch),
        cost_estimate=pl.CostEstimate(
            flops=int(micros * 3_000_000_000), transcendentals=0, bytes_accessed=int(micros * 9_000_000)
        ),
        compiler_params=pltpu.CompilerParams(vmem_limit_bytes=VMEM_LIMIT),
    )


def near(value):
    return pltpu.with_memory_space_constraint(value, pltpu.VMEM)


def flip(value, axis, mask):
    pairs = [(source, source ^ mask) for source in range(lax.axis_size(axis))]
    return near(lax.ppermute(value, axis, pairs))


def after(value, *earlier):
    return lax.optimization_barrier((value, *earlier))[0]


def place_of(order, rows):
    depth = rows // WIDE
    return order % depth * WIDE + order // depth % STEPS * MID + order // (STEPS * depth)


def to_order(rows):
    new = lax.broadcasted_iota(jnp.int32, (rows, rows), 0)
    old = lax.broadcasted_iota(jnp.int32, (rows, rows), 1)
    return (old == place_of(new, rows)).astype(jnp.bfloat16)


def to_position(rows):
    new = lax.broadcasted_iota(jnp.int32, (rows, rows), 0)
    old = lax.broadcasted_iota(jnp.int32, (rows, rows), 1)
    return (new == place_of(old, rows)).astype(jnp.bfloat16)


def product(left, right, left_axis=1, right_axis=0):
    return lax.dot_general(
        left,
        right,
        (((left_axis,), (right_axis,)), ((), ())),
        preferred_element_type=jnp.float32,
    )


def norm_body(*refs):
    count = len(refs) // 2 - 1
    x_refs, gain_ref, bias_ref, out_refs = refs[:count], refs[count], refs[count + 1], refs[count + 2 :]
    order = to_order(x_refs[0].shape[0])
    gain = gain_ref[...][None, :]
    bias = bias_ref[...][None, :]
    for x_ref, out_ref in zip(x_refs, out_refs):
        floats = x_ref[...].astype(jnp.float32)
        centred = floats - jnp.mean(floats, axis=-1, keepdims=True)
        spread = jnp.mean(centred * centred, axis=-1, keepdims=True)
        normed = (centred * lax.rsqrt(spread + 1e-05) * gain + bias).astype(jnp.bfloat16)
        out_ref[...] = product(order, normed).astype(jnp.bfloat16)


def group_indices():
    shard = lax.axis_index("ctx")
    return shard % SHARDS, shard // SHARDS


def head_slices(index):
    return [
        slice(part * GROUP_WIDTH + index * HEAD_DIM, part * GROUP_WIDTH + (index + 1) * HEAD_DIM)
        for part in range(3)
    ]


def wide_rows(head, rows):
    depth = rows // WIDE
    start = head % MID * (STEPS * depth) + head % WIDE // MID * depth
    return pl.ds(pl.multiple_of(start, depth), depth)


def middle_rows(head, rows):
    count = rows // MID
    return pl.ds(pl.multiple_of(head % MID * count, count), count)


def assemble(whole_ref, refs, sources):
    for ref, source in zip(refs, sources):
        rows = ref.shape[0]
        whole_ref[pl.ds(pl.multiple_of(source * rows, 16), rows), :] = ref[...]


def sources(n_mp, turn, shared):
    mp_index = lax.axis_index("mp")
    if shared:
        return [mp_index, mp_index ^ 1, mp_index ^ (2 + turn), mp_index ^ (3 - turn)]
    return [mp_index ^ apart for apart in range(n_mp)]


def project_body(n_mp, shared, *refs):
    normed_refs, refs = refs[:SHARDS], refs[SHARDS:]
    weight_refs, (*out_refs, sent_ref, whole_ref) = refs[:n_mp], refs[n_mp:]
    member, group = group_indices()
    assemble(whole_ref, weight_refs, sources(n_mp, group % 2, shared))
    for normed_ref, out_ref in zip(normed_refs, out_refs):
        out_ref[...] = product(normed_ref[...], whole_ref[...]).astype(jnp.bfloat16)
    shard_rows = out_refs[0].shape[0]
    depth = shard_rows // WIDE
    for index in range(GROUP_HEADS):
        _, key_at, value_at = head_slices(index)
        taken = wide_rows(member * GROUP_HEADS + index, shard_rows)
        for shard, out_ref in enumerate(out_refs):
            sent_ref[index, shard * depth : (shard + 1) * depth, :] = jnp.concatenate(
                [out_ref[taken, key_at], out_ref[taken, value_at]], axis=1
            )


def branch(query, key, value, bias):
    score = product(key, query, 1, 1) * SCALE + bias
    largest = jnp.max(score, axis=0, keepdims=True)
    weight = jnp.exp2(score - largest)
    total = jnp.sum(weight, axis=0, keepdims=True)
    return largest, total, product(value, weight.astype(jnp.bfloat16), 0, 0)


def key_bias(position, valid):
    return jnp.where(position < valid, 0.0, NEG_FILL).astype(jnp.float32)


def merge(one, two):
    top = jnp.maximum(one[0], two[0])
    left = jnp.exp2(one[0] - top)
    right = jnp.exp2(two[0] - top)
    return top, left * one[1] + right * two[1], left * one[2] + right * two[2]


def near_branches(shards, valid_ref, qkv_refs, max_ref, sum_ref, num_ref):
    member, group = group_indices()
    valid = valid_ref[0]
    rows = qkv_refs[0].shape[0]
    count = rows // MID
    depth = rows // WIDE
    bases = [(group * SHARDS + (member ^ apart)) * rows for apart in range(SHARDS)]
    place = place_of(lax.broadcasted_iota(jnp.int32, (rows, LANES), 0), rows)
    lane = lax.broadcasted_iota(jnp.int32, (1, rows), 1)

    for slot, shard in enumerate(shards):
        ref = qkv_refs[shard]
        bias = jnp.concatenate(
            [key_bias(place + bases[shard], valid)] * (rows // LANES), axis=1
        )
        for index in range(GROUP_HEADS):
            stats = branch(*(ref[:, at] for at in head_slices(index)), bias)
            max_ref[index, slot], sum_ref[index, slot], num_ref[index, slot] = stats
    item = lax.broadcasted_iota(jnp.int32, (count, len(shards) * count), 0)
    for index in range(GROUP_HEADS):
        head = member * GROUP_HEADS + index
        taken = middle_rows(head, rows)
        query, key, value = (
            jnp.concatenate([qkv_refs[shard][taken, at] for shard in some], axis=0)
            for some, at in zip((shards, range(SHARDS), range(SHARDS)), head_slices(index))
        )
        position = item % depth * WIDE + item // depth * MID + head % MID
        bias = jnp.concatenate([key_bias(position + base, valid) for base in bases], axis=0)
        middle = branch(query, key, value, bias)
        inside = lane // count == head % MID
        for slot in range(len(shards)):
            largest, total, number = (
                jnp.concatenate([part[:, slot * count : (slot + 1) * count]] * MID, axis=1)
                for part in middle
            )
            merged = merge(
                (max_ref[index, slot], sum_ref[index, slot], num_ref[index, slot]),
                (jnp.where(inside, largest, NEG_FILL), total, number),
            )
            max_ref[index, slot], sum_ref[index, slot], num_ref[index, slot] = merged


def far_branch(shards, valid_ref, qkv_refs, sent_refs, max_ref, sum_ref, num_ref, out_refs):
    member, group = group_indices()
    valid = valid_ref[0]
    rows = qkv_refs[0].shape[0]
    depth = rows // WIDE
    count = len(shards) * depth
    item = lax.broadcasted_iota(jnp.int32, (SHARDS * depth, count), 0)
    lane = lax.broadcasted_iota(jnp.int32, (1, rows), 1)
    for index in range(GROUP_HEADS):
        head = member * GROUP_HEADS + index
        taken = wide_rows(head, rows)
        query_at = head_slices(index)[0]
        query = jnp.concatenate([qkv_refs[shard][taken, query_at] for shard in shards], axis=0)
        bias = jnp.concatenate(
            [
                key_bias(
                    ((group ^ apart) * SHARDS + (member ^ (item // depth))) * rows
                    + item % depth * WIDE
                    + head,
                    valid,
                )
                for apart in range(len(sent_refs))
            ],
            axis=0,
        )
        both = jnp.concatenate([ref[index] for ref in sent_refs], axis=0)
        stats = branch(query, both[:, :HEAD_DIM], both[:, HEAD_DIM:], bias)
        stacked = jnp.concatenate(
            [stats[2], jnp.broadcast_to(stats[0], (8, count)), jnp.broadcast_to(stats[1], (8, count))],
            axis=0,
        )
        stacked = jnp.concatenate(
            [stacked, jnp.zeros((stacked.shape[0], LANES - count), jnp.float32)], axis=1
        )
        block = head % MID * STEPS + head % WIDE // MID
        inside = lane // depth == block
        for slot, (shard, out_ref) in enumerate(zip(shards, out_refs)):
            shift = (block * depth - slot * depth + LANES) % LANES
            moved = jnp.concatenate([pltpu.roll(stacked, shift, 1)] * (rows // LANES), axis=1)
            _, total, number = merge(
                (max_ref[index, slot], sum_ref[index, slot], num_ref[index, slot]),
                (
                    jnp.where(inside, moved[HEAD_DIM : HEAD_DIM + 1], NEG_FILL),
                    moved[HEAD_DIM + 8 : HEAD_DIM + 9],
                    moved[:HEAD_DIM],
                ),
            )
            base = (group * SHARDS + (member ^ shard)) * rows
            attention = jnp.where(
                base + place_of(lane, rows) < valid, number * (1.0 / total), 0.0
            )
            out_ref[index * HEAD_DIM : (index + 1) * HEAD_DIM, :] = attention.astype(jnp.bfloat16)


def near_body(shards, valid_ref, *refs):
    near_branches(shards, valid_ref, refs[:SHARDS], *refs[SHARDS:])


def far_body(shards, valid_ref, *refs):
    *refs, out_ref = refs
    sent_refs, stat_refs = refs[SHARDS:-3], refs[-3:]
    out_refs = [out_ref.at[slot] for slot in range(len(shards))]
    far_branch(shards, valid_ref, refs[:SHARDS], sent_refs, *stat_refs, out_refs)


def all_body(shards, valid_ref, *refs):
    stat_refs, out_refs = refs[-3:], refs[-len(shards) - 3 : -3]
    sent_refs = refs[SHARDS : -len(shards) - 3]
    near_branches(shards, valid_ref, refs[:SHARDS], *stat_refs)
    far_branch(shards, valid_ref, refs[:SHARDS], sent_refs, *stat_refs, out_refs)


def gather_body(n_mp, shared, *refs):
    *part_refs, out_ref = refs
    assemble(out_ref, part_refs, sources(n_mp, lax.axis_index("ctx") % 2, shared))


def update_body(blocks, *refs):
    *part_refs, weight_ref, base_ref, out_ref = refs
    member, _ = group_indices()
    order = to_position(base_ref.shape[0])
    update = base_ref[...].astype(jnp.float32)
    for (apart, slot), ref in zip(blocks, part_refs):
        part = ref[...] if slot is None else ref[slot]
        part = product(order, part, 1, 1).astype(jnp.bfloat16)
        start = pl.multiple_of((member ^ apart) * GROUP_WIDTH, GROUP_WIDTH)
        update = update + product(part, weight_ref[pl.ds(start, GROUP_WIDTH), :])
    out_ref[...] = update.astype(out_ref.dtype)


def fetch(value, turns, shared, pair_mask, earlier=()):
    n_mp, n_ctx = lax.axis_size("mp"), lax.axis_size("ctx")
    if not shared:
        return [flip(value, "mp", apart) for apart in range(1, n_mp)]
    pairs = [
        (c * n_mp + z, c * n_mp + (z ^ (2 + turns(c)))) for c in range(n_ctx) for z in range(n_mp)
    ]
    direct = near(lax.ppermute(value, ("ctx", "mp"), pairs))
    return [direct, flip(after(direct, *earlier), "ctx", pair_mask)]


def local(tile_embeds, norm_gain, norm_bias, w_qkv, w_out, valid_count):
    x = tile_embeds[0]
    rows, width = x.shape
    n_mp = lax.axis_size("mp")
    n_groups = lax.axis_size("ctx") // SHARDS
    depth = rows // WIDE
    weight_rows = w_qkv.shape[0]
    member, _ = group_indices()
    bf16, f32 = jnp.bfloat16, jnp.float32
    shape = pltpu.VMEM
    shared = n_mp == 4 and n_groups % 2 == 0

    def columns(part):
        start = part * width + member * GROUP_WIDTH
        return lax.dynamic_slice(w_qkv, (0, start), (weight_rows, GROUP_WIDTH))

    mine = near(jnp.concatenate([columns(part) for part in range(3)], axis=1))
    others = fetch(mine, lambda c: c // SHARDS % 2, shared, SHARDS)

    x_pair = flip(after(x, mine), "ctx", 1)
    x_far = flip(after(x, x_pair), "ctx", 2)
    x_last = flip(x_far, "ctx", 1)
    weights = [mine] + ([flip(mine, "mp", 1)] if shared else []) + others
    x_own = near(x)
    gain, bias = near(norm_gain), near(norm_bias)
    normed = []
    for pair in ((x_own, x_pair), (x_far, x_last)):
        normed += call(norm_body, [shape((rows, width), bf16)] * 2, n_in=4, micros=0.01)(
            *pair, gain, bias
        )

    out_weight = after(near(w_out), others[0])
    out_parts = [out_weight]
    if shared:
        out_parts.append(flip(out_weight, "mp", 1))
    *qkv, sent = call(
        lambda *refs: project_body(n_mp, shared, *refs),
        [shape((rows, 3 * GROUP_WIDTH), bf16)] * SHARDS
        + [shape((GROUP_HEADS, SHARDS * depth, 2 * HEAD_DIM), bf16)],
        scratch=[pltpu.VMEM((width, 3 * GROUP_WIDTH), bf16)],
        n_in=SHARDS + n_mp,
        micros=2,
    )(*normed, *weights)
    sents = [sent] + [flip(sent, "ctx", SHARDS * apart) for apart in range(1, n_groups)]
    half = SHARDS // 2
    here, there = range(half), range(half, SHARDS)
    stat_shapes = [
        shape((GROUP_HEADS, half, 1, rows), f32),
        shape((GROUP_HEADS, half, 1, rows), f32),
        shape((GROUP_HEADS, half, HEAD_DIM, rows), f32),
    ]
    stats = call(
        lambda *refs: near_body(there, *refs), stat_shapes, n_scalar=1, n_in=SHARDS, micros=3
    )(valid_count, *qkv)
    (sending,) = call(
        lambda *refs: far_body(there, *refs),
        [shape((half, GROUP_WIDTH, rows), bf16)],
        n_scalar=1,
        n_in=SHARDS + n_groups + 3,
        micros=1,
    )(valid_count, *qkv, *sents, *stats)
    staying = call(
        lambda *refs: all_body(here, *refs),
        [shape((GROUP_WIDTH, rows), bf16)] * half,
        scratch=stat_shapes,
        n_scalar=1,
        n_in=SHARDS + n_groups,
        micros=2,
    )(valid_count, *qkv, after(sents[0], sending), *sents[1:])
    far_part = flip(sending, "ctx", 2)
    out_parts += fetch(out_weight, lambda c: c % 2, shared, 1, staying[:1])
    (whole_out,) = call(
        lambda *refs: gather_body(n_mp, shared, *refs),
        [shape((width, width), bf16)],
        n_in=n_mp,
        micros=0.001,
    )(*out_parts)
    total = x_own
    pair_part = flip(staying[1], "ctx", 1)
    last_part = flip(after(far_part, pair_part), "ctx", 1)
    steps = [
        ([(0, None), (1, None)], [staying[0], pair_part], shape((rows, width), f32)),
        ([(2, 0)], [far_part], shape((rows, width), f32)),
        ([(3, 1)], [last_part], jax.ShapeDtypeStruct((rows, width), bf16)),
    ]
    for blocks, operands, out_shape in steps:
        (total,) = call(
            lambda *refs, blocks=blocks: update_body(blocks, *refs),
            [out_shape],
            n_in=len(operands) + 2,
            micros=0.001,
        )(*operands, whole_out, total)
    return total[None]


def solution(mesh):
    placed = (P("mp", "ctx", None), P(), P(), P("mp", None), P("mp", None), P("mp"))
    return jax.shard_map(
        local, mesh=mesh, in_specs=placed, out_specs=P("mp", "ctx", None), check_vma=False
    )
```

```python
import math

import jax
import jax.numpy as jnp
from jax import lax
from jax.experimental import pallas as pl
from jax.experimental.pallas import tpu as pltpu
from jax.sharding import PartitionSpec as P

HEADS = 12
HEAD_DIM = 64
MID = 4
WIDE = 16
SHARDS = 4
STEPS = WIDE // MID
GROUP_HEADS = HEADS // SHARDS
GROUP_WIDTH = GROUP_HEADS * HEAD_DIM
NEG_FILL = -1e30
SCALE = math.log2(math.e) / math.sqrt(HEAD_DIM)
VMEM_LIMIT = 24 * 1024 * 1024
LANES = 128


def call(body, out_shape, scratch=(), n_scalar=0, n_in=0, micros=1):
    specs = [pl.BlockSpec(memory_space=pltpu.SMEM)] * n_scalar + [
        pl.BlockSpec(memory_space=pltpu.VMEM)
    ] * n_in
    outs = [pl.BlockSpec(memory_space=pltpu.VMEM) for _ in out_shape]
    return pl.pallas_call(
        body,
        out_shape=out_shape,
        in_specs=specs,
        out_specs=outs,
        scratch_shapes=list(scratch),
        cost_estimate=pl.CostEstimate(
            flops=int(micros * 3_000_000_000), transcendentals=0, bytes_accessed=int(micros * 9_000_000)
        ),
        compiler_params=pltpu.CompilerParams(vmem_limit_bytes=VMEM_LIMIT),
    )


def near(value):
    return pltpu.with_memory_space_constraint(value, pltpu.VMEM)


def flip(value, axis, mask):
    pairs = [(source, source ^ mask) for source in range(lax.axis_size(axis))]
    return near(lax.ppermute(value, axis, pairs))


def after(value, *earlier):
    return lax.optimization_barrier((value, *earlier))[0]


def place_of(order, rows):
    depth = rows // WIDE
    return order % depth * WIDE + order // depth % STEPS * MID + order // (STEPS * depth)


def to_order(rows):
    new = lax.broadcasted_iota(jnp.int32, (rows, rows), 0)
    old = lax.broadcasted_iota(jnp.int32, (rows, rows), 1)
    return (old == place_of(new, rows)).astype(jnp.bfloat16)


def to_position(rows):
    new = lax.broadcasted_iota(jnp.int32, (rows, rows), 0)
    old = lax.broadcasted_iota(jnp.int32, (rows, rows), 1)
    return (new == place_of(old, rows)).astype(jnp.bfloat16)


def product(left, right, left_axis=1, right_axis=0):
    return lax.dot_general(
        left,
        right,
        (((left_axis,), (right_axis,)), ((), ())),
        preferred_element_type=jnp.float32,
    )


def norm_body(*refs):
    count = len(refs) // 2 - 1
    x_refs, gain_ref, bias_ref, out_refs = refs[:count], refs[count], refs[count + 1], refs[count + 2 :]
    order = to_order(x_refs[0].shape[0])
    gain = gain_ref[...][None, :]
    bias = bias_ref[...][None, :]
    for x_ref, out_ref in zip(x_refs, out_refs):
        floats = x_ref[...].astype(jnp.float32)
        centred = floats - jnp.mean(floats, axis=-1, keepdims=True)
        spread = jnp.mean(centred * centred, axis=-1, keepdims=True)
        normed = (centred * lax.rsqrt(spread + 1e-05) * gain + bias).astype(jnp.bfloat16)
        out_ref[...] = product(order, normed).astype(jnp.bfloat16)


def group_indices():
    shard = lax.axis_index("ctx")
    return shard % SHARDS, shard // SHARDS


def head_slices(index):
    return [
        slice(part * GROUP_WIDTH + index * HEAD_DIM, part * GROUP_WIDTH + (index + 1) * HEAD_DIM)
        for part in range(3)
    ]


def wide_rows(head, rows):
    depth = rows // WIDE
    start = head % MID * (STEPS * depth) + head % WIDE // MID * depth
    return pl.ds(pl.multiple_of(start, depth), depth)


def middle_rows(head, rows):
    count = rows // MID
    return pl.ds(pl.multiple_of(head % MID * count, count), count)


def assemble(whole_ref, refs, sources):
    for ref, source in zip(refs, sources):
        rows = ref.shape[0]
        whole_ref[pl.ds(pl.multiple_of(source * rows, 16), rows), :] = ref[...]


def sources(n_mp, turn, shared):
    mp_index = lax.axis_index("mp")
    if shared:
        return [mp_index, mp_index ^ 1, mp_index ^ (2 + turn), mp_index ^ (3 - turn)]
    return [mp_index ^ apart for apart in range(n_mp)]


def project_body(n_mp, shared, *refs):
    normed_refs, refs = refs[:SHARDS], refs[SHARDS:]
    weight_refs, (*out_refs, sent_ref, whole_ref) = refs[:n_mp], refs[n_mp:]
    member, group = group_indices()
    assemble(whole_ref, weight_refs, sources(n_mp, group % 2, shared))
    for normed_ref, out_ref in zip(normed_refs, out_refs):
        out_ref[...] = product(normed_ref[...], whole_ref[...]).astype(jnp.bfloat16)
    shard_rows = out_refs[0].shape[0]
    depth = shard_rows // WIDE
    for index in range(GROUP_HEADS):
        _, key_at, value_at = head_slices(index)
        taken = wide_rows(member * GROUP_HEADS + index, shard_rows)
        for shard, out_ref in enumerate(out_refs):
            sent_ref[index, shard * depth : (shard + 1) * depth, :] = jnp.concatenate(
                [out_ref[taken, key_at], out_ref[taken, value_at]], axis=1
            )


def branch(query, key, value, bias):
    score = product(key, query, 1, 1) * SCALE + bias
    largest = jnp.max(score, axis=0, keepdims=True)
    weight = jnp.exp2(score - largest)
    total = jnp.sum(weight, axis=0, keepdims=True)
    return largest, total, product(value, weight.astype(jnp.bfloat16), 0, 0)


def key_bias(position, valid):
    return jnp.where(position < valid, 0.0, NEG_FILL).astype(jnp.float32)


def merge(one, two):
    top = jnp.maximum(one[0], two[0])
    left = jnp.exp2(one[0] - top)
    right = jnp.exp2(two[0] - top)
    return top, left * one[1] + right * two[1], left * one[2] + right * two[2]


def near_branches(shards, valid_ref, qkv_refs, max_ref, sum_ref, num_ref):
    member, group = group_indices()
    valid = valid_ref[0]
    rows = qkv_refs[0].shape[0]
    count = rows // MID
    depth = rows // WIDE
    bases = [(group * SHARDS + (member ^ apart)) * rows for apart in range(SHARDS)]
    place = place_of(lax.broadcasted_iota(jnp.int32, (rows, LANES), 0), rows)
    lane = lax.broadcasted_iota(jnp.int32, (1, rows), 1)

    for slot, shard in enumerate(shards):
        ref = qkv_refs[shard]
        bias = jnp.concatenate(
            [key_bias(place + bases[shard], valid)] * (rows // LANES), axis=1
        )
        for index in range(GROUP_HEADS):
            stats = branch(*(ref[:, at] for at in head_slices(index)), bias)
            max_ref[index, slot], sum_ref[index, slot], num_ref[index, slot] = stats
    item = lax.broadcasted_iota(jnp.int32, (count, len(shards) * count), 0)
    for index in range(GROUP_HEADS):
        head = member * GROUP_HEADS + index
        taken = middle_rows(head, rows)
        query, key, value = (
            jnp.concatenate([qkv_refs[shard][taken, at] for shard in some], axis=0)
            for some, at in zip((shards, range(SHARDS), range(SHARDS)), head_slices(index))
        )
        position = item % depth * WIDE + item // depth * MID + head % MID
        bias = jnp.concatenate([key_bias(position + base, valid) for base in bases], axis=0)
        middle = branch(query, key, value, bias)
        inside = lane // count == head % MID
        for slot in range(len(shards)):
            largest, total, number = (
                jnp.concatenate([part[:, slot * count : (slot + 1) * count]] * MID, axis=1)
                for part in middle
            )
            merged = merge(
                (max_ref[index, slot], sum_ref[index, slot], num_ref[index, slot]),
                (jnp.where(inside, largest, NEG_FILL), total, number),
            )
            max_ref[index, slot], sum_ref[index, slot], num_ref[index, slot] = merged


def far_branch(shards, valid_ref, qkv_refs, sent_refs, max_ref, sum_ref, num_ref, out_refs):
    member, group = group_indices()
    valid = valid_ref[0]
    rows = qkv_refs[0].shape[0]
    depth = rows // WIDE
    count = len(shards) * depth
    item = lax.broadcasted_iota(jnp.int32, (SHARDS * depth, count), 0)
    lane = lax.broadcasted_iota(jnp.int32, (1, rows), 1)
    for index in range(GROUP_HEADS):
        head = member * GROUP_HEADS + index
        taken = wide_rows(head, rows)
        query_at = head_slices(index)[0]
        query = jnp.concatenate([qkv_refs[shard][taken, query_at] for shard in shards], axis=0)
        bias = jnp.concatenate(
            [
                key_bias(
                    ((group ^ apart) * SHARDS + (member ^ (item // depth))) * rows
                    + item % depth * WIDE
                    + head,
                    valid,
                )
                for apart in range(len(sent_refs))
            ],
            axis=0,
        )
        both = jnp.concatenate([ref[index] for ref in sent_refs], axis=0)
        stats = branch(query, both[:, :HEAD_DIM], both[:, HEAD_DIM:], bias)
        stacked = jnp.concatenate(
            [stats[2], jnp.broadcast_to(stats[0], (8, count)), jnp.broadcast_to(stats[1], (8, count))],
            axis=0,
        )
        stacked = jnp.concatenate(
            [stacked, jnp.zeros((stacked.shape[0], LANES - count), jnp.float32)], axis=1
        )
        block = head % MID * STEPS + head % WIDE // MID
        inside = lane // depth == block
        for slot, (shard, out_ref) in enumerate(zip(shards, out_refs)):
            shift = (block * depth - slot * depth + LANES) % LANES
            moved = jnp.concatenate([pltpu.roll(stacked, shift, 1)] * (rows // LANES), axis=1)
            _, total, number = merge(
                (max_ref[index, slot], sum_ref[index, slot], num_ref[index, slot]),
                (
                    jnp.where(inside, moved[HEAD_DIM : HEAD_DIM + 1], NEG_FILL),
                    moved[HEAD_DIM + 8 : HEAD_DIM + 9],
                    moved[:HEAD_DIM],
                ),
            )
            base = (group * SHARDS + (member ^ shard)) * rows
            attention = jnp.where(
                base + place_of(lane, rows) < valid, number * (1.0 / total), 0.0
            )
            out_ref[index * HEAD_DIM : (index + 1) * HEAD_DIM, :] = attention.astype(jnp.bfloat16)


def near_body(shards, valid_ref, *refs):
    near_branches(shards, valid_ref, refs[:SHARDS], *refs[SHARDS:])


def far_body(shards, valid_ref, *refs):
    *refs, out_ref = refs
    sent_refs, stat_refs = refs[SHARDS:-3], refs[-3:]
    out_refs = [out_ref.at[slot] for slot in range(len(shards))]
    far_branch(shards, valid_ref, refs[:SHARDS], sent_refs, *stat_refs, out_refs)


def all_body(shards, valid_ref, *refs):
    stat_refs, out_refs = refs[-3:], refs[-len(shards) - 3 : -3]
    sent_refs = refs[SHARDS : -len(shards) - 3]
    near_branches(shards, valid_ref, refs[:SHARDS], *stat_refs)
    far_branch(shards, valid_ref, refs[:SHARDS], sent_refs, *stat_refs, out_refs)


def gather_body(n_mp, shared, *refs):
    *part_refs, out_ref, order_ref = refs
    order_ref[...] = to_position(order_ref.shape[0])
    assemble(out_ref, part_refs, sources(n_mp, lax.axis_index("ctx") % 2, shared))


def update_body(blocks, *refs):
    *part_refs, weight_ref, order_ref, base_ref, out_ref = refs
    member, _ = group_indices()
    order = order_ref[...]
    update = base_ref[...].astype(jnp.float32)
    for (apart, slot), ref in zip(blocks, part_refs):
        part = ref[...] if slot is None else ref[slot]
        part = product(order, part, 1, 1).astype(jnp.bfloat16)
        start = pl.multiple_of((member ^ apart) * GROUP_WIDTH, GROUP_WIDTH)
        update = update + product(part, weight_ref[pl.ds(start, GROUP_WIDTH), :])
    out_ref[...] = update.astype(out_ref.dtype)


def fetch(value, turns, shared):
    n_mp, n_ctx = lax.axis_size("mp"), lax.axis_size("ctx")
    if not shared:
        return [flip(value, "mp", apart) for apart in range(1, n_mp)]
    pairs = [
        (c * n_mp + z, c * n_mp + (z ^ (2 + turns(c)))) for c in range(n_ctx) for z in range(n_mp)
    ]
    return [flip(value, "mp", 1), near(lax.ppermute(value, ("ctx", "mp"), pairs))]


def exchange(blocks, shared, mask, *earlier):
    if not shared:
        return blocks
    return blocks + [flip(after(blocks[-1], *earlier), "ctx", mask)]


def local(tile_embeds, norm_gain, norm_bias, w_qkv, w_out, valid_count):
    x = tile_embeds[0]
    rows, width = x.shape
    n_mp = lax.axis_size("mp")
    n_groups = lax.axis_size("ctx") // SHARDS
    depth = rows // WIDE
    weight_rows = w_qkv.shape[0]
    member, _ = group_indices()
    bf16, f32 = jnp.bfloat16, jnp.float32
    shape = pltpu.VMEM
    shared = n_mp == 4 and n_groups % 2 == 0

    def columns(part):
        start = part * width + member * GROUP_WIDTH
        return lax.dynamic_slice(w_qkv, (0, start), (weight_rows, GROUP_WIDTH))

    mine = near(jnp.concatenate([columns(part) for part in range(3)], axis=1))
    fetched = fetch(mine, lambda c: c // SHARDS % 2, shared)

    x_own = near(x)
    x_pair = flip(after(x, mine), "ctx", 1)
    x_far = flip(after(x, mine), "ctx", 2)
    x_last = flip(x_far, "ctx", 1)
    gain, bias = near(norm_gain), near(norm_bias)

    def normalized(one, two, micros):
        return call(norm_body, [shape((rows, width), bf16)] * 2, n_in=4, micros=micros)(
            one, two, gain, bias
        )

    normed = normalized(x_own, x_pair, 1)
    weights = [mine] + exchange(fetched, shared, SHARDS, normed[0])
    normed += normalized(x_far, x_last, 0.01)

    out_weight = after(near(w_out), x_last)
    out_fetched = fetch(out_weight, lambda c: c % 2, shared)

    *qkv, sent = call(
        lambda *refs: project_body(n_mp, shared, *refs),
        [shape((rows, 3 * GROUP_WIDTH), bf16)] * SHARDS
        + [shape((GROUP_HEADS, SHARDS * depth, 2 * HEAD_DIM), bf16)],
        scratch=[pltpu.VMEM((width, 3 * GROUP_WIDTH), bf16)],
        n_in=SHARDS + n_mp,
        micros=2,
    )(*normed, *weights)
    sents = [sent] + [flip(sent, "ctx", SHARDS * apart) for apart in range(1, n_groups)]
    half = SHARDS // 2
    here, there = range(half), range(half, SHARDS)
    stat_shapes = [
        shape((GROUP_HEADS, half, 1, rows), f32),
        shape((GROUP_HEADS, half, 1, rows), f32),
        shape((GROUP_HEADS, half, HEAD_DIM, rows), f32),
    ]
    stats = call(
        lambda *refs: near_body(there, *refs), stat_shapes, n_scalar=1, n_in=SHARDS, micros=3
    )(valid_count, *qkv)
    (sending,) = call(
        lambda *refs: far_body(there, *refs),
        [shape((half, GROUP_WIDTH, rows), bf16)],
        n_scalar=1,
        n_in=SHARDS + n_groups + 3,
        micros=1,
    )(valid_count, *qkv, *sents, *stats)
    staying = call(
        lambda *refs: all_body(here, *refs),
        [shape((GROUP_WIDTH, rows), bf16)] * half,
        scratch=stat_shapes,
        n_scalar=1,
        n_in=SHARDS + n_groups,
        micros=2,
    )(valid_count, *qkv, after(sents[0], sending), *sents[1:])
    far_part = flip(sending, "ctx", 2)
    out_parts = [out_weight] + exchange(out_fetched, shared, 1, staying[0])
    whole_out, order = call(
        lambda *refs: gather_body(n_mp, shared, *refs),
        [shape((width, width), bf16), shape((rows, rows), bf16)],
        n_in=n_mp,
        micros=0.001,
    )(*out_parts)
    total = x_own
    pair_part = flip(staying[1], "ctx", 1)
    last_part = flip(after(far_part, pair_part), "ctx", 1)
    steps = [
        ([(0, None)], [staying[0]], shape((rows, width), f32)),
        ([(1, None), (2, 0)], [pair_part, far_part], shape((rows, width), f32)),
        ([(3, 1)], [last_part], jax.ShapeDtypeStruct((rows, width), bf16)),
    ]
    for blocks, operands, out_shape in steps:
        (total,) = call(
            lambda *refs, blocks=blocks: update_body(blocks, *refs),
            [out_shape],
            n_in=len(operands) + 3,
            micros=0.001,
        )(*operands, whole_out, order, total)
    return total[None]


def solution(mesh):
    placed = (P("mp", "ctx", None), P(), P(), P("mp", None), P("mp", None), P("mp"))
    return jax.shard_map(
        local, mesh=mesh, in_specs=placed, out_specs=P("mp", "ctx", None), check_vma=False
    )
```

```python
import math

import jax
import jax.numpy as jnp
from jax import lax
from jax.experimental import pallas as pl
from jax.experimental.pallas import tpu as pltpu
from jax.sharding import PartitionSpec as P

HEADS = 12
HEAD_DIM = 64
MID = 4
WIDE = 16
SHARDS = 4
STEPS = WIDE // MID
GROUP_HEADS = HEADS // SHARDS
GROUP_WIDTH = GROUP_HEADS * HEAD_DIM
NEG_FILL = -1e30
SCALE = math.log2(math.e) / math.sqrt(HEAD_DIM)
VMEM_LIMIT = 24 * 1024 * 1024
LANES = 128


def call(body, out_shape, scratch=(), n_scalar=0, n_in=0, micros=1):
    specs = [pl.BlockSpec(memory_space=pltpu.SMEM)] * n_scalar + [
        pl.BlockSpec(memory_space=pltpu.VMEM)
    ] * n_in
    outs = [pl.BlockSpec(memory_space=pltpu.VMEM) for _ in out_shape]
    return pl.pallas_call(
        body,
        out_shape=out_shape,
        in_specs=specs,
        out_specs=outs,
        scratch_shapes=list(scratch),
        cost_estimate=pl.CostEstimate(
            flops=int(micros * 3_000_000_000), transcendentals=0, bytes_accessed=int(micros * 9_000_000)
        ),
        compiler_params=pltpu.CompilerParams(vmem_limit_bytes=VMEM_LIMIT),
    )


def near(value):
    return pltpu.with_memory_space_constraint(value, pltpu.VMEM)


def flip(value, axis, mask):
    pairs = [(source, source ^ mask) for source in range(lax.axis_size(axis))]
    return near(lax.ppermute(value, axis, pairs))


def after(value, *earlier):
    return lax.optimization_barrier((value, *earlier))[0]


def place_of(order, rows):
    depth = rows // WIDE
    return order % depth * WIDE + order // depth % STEPS * MID + order // (STEPS * depth)


def to_order(rows):
    new = lax.broadcasted_iota(jnp.int32, (rows, rows), 0)
    old = lax.broadcasted_iota(jnp.int32, (rows, rows), 1)
    return (old == place_of(new, rows)).astype(jnp.bfloat16)


def to_position(rows):
    new = lax.broadcasted_iota(jnp.int32, (rows, rows), 0)
    old = lax.broadcasted_iota(jnp.int32, (rows, rows), 1)
    return (new == place_of(old, rows)).astype(jnp.bfloat16)


def product(left, right, left_axis=1, right_axis=0):
    return lax.dot_general(
        left,
        right,
        (((left_axis,), (right_axis,)), ((), ())),
        preferred_element_type=jnp.float32,
    )


def norm_body(*refs):
    count = len(refs) // 2 - 1
    x_refs, gain_ref, bias_ref, out_refs = refs[:count], refs[count], refs[count + 1], refs[count + 2 :]
    order = to_order(x_refs[0].shape[0])
    gain = gain_ref[...][None, :]
    bias = bias_ref[...][None, :]
    for x_ref, out_ref in zip(x_refs, out_refs):
        floats = x_ref[...].astype(jnp.float32)
        centred = floats - jnp.mean(floats, axis=-1, keepdims=True)
        spread = jnp.mean(centred * centred, axis=-1, keepdims=True)
        normed = (centred * lax.rsqrt(spread + 1e-05) * gain + bias).astype(jnp.bfloat16)
        ordered = product(order, normed).astype(jnp.bfloat16)
        blocks, _, width = out_ref.shape
        for block in range(blocks):
            out_ref[block] = ordered[:, block * width : (block + 1) * width]


def group_indices():
    shard = lax.axis_index("ctx")
    return shard % SHARDS, shard // SHARDS


def head_slices(index):
    return [
        slice(part * GROUP_WIDTH + index * HEAD_DIM, part * GROUP_WIDTH + (index + 1) * HEAD_DIM)
        for part in range(3)
    ]


def wide_rows(head, rows):
    depth = rows // WIDE
    start = head % MID * (STEPS * depth) + head % WIDE // MID * depth
    return pl.ds(pl.multiple_of(start, depth), depth)


def middle_rows(head, rows):
    count = rows // MID
    return pl.ds(pl.multiple_of(head % MID * count, count), count)


def assemble(whole_ref, refs, sources):
    for ref, source in zip(refs, sources):
        rows = ref.shape[0]
        whole_ref[pl.ds(pl.multiple_of(source * rows, 16), rows), :] = ref[...]


def sources(n_mp, turn, shared):
    mp_index = lax.axis_index("mp")
    if shared:
        return [mp_index, mp_index ^ 1, mp_index ^ (2 + turn), mp_index ^ (3 - turn)]
    return [mp_index ^ apart for apart in range(n_mp)]


def project_body(blocks, *refs):
    _, group = group_indices()
    normed_refs, refs = refs[:SHARDS], refs[SHARDS:]
    n_mp, shared, some = blocks
    weight_refs, refs = refs[: len(some)], refs[len(some) :]
    base_refs, out_refs = refs[:-SHARDS], refs[-SHARDS:]
    origin = sources(n_mp, group % 2, shared)
    for shard, (normed_ref, out_ref) in enumerate(zip(normed_refs, out_refs)):
        total = base_refs[shard][...] if base_refs else 0.0
        for block, weight_ref in zip(some, weight_refs):
            total = total + product(normed_ref[origin[block]], weight_ref[...])
        out_ref[...] = total.astype(out_ref.dtype)


def project_last_body(blocks, *refs):
    *refs, sent_ref = refs
    project_body(blocks, *refs)
    out_refs = refs[-SHARDS:]
    member, _ = group_indices()
    shard_rows = out_refs[0].shape[0]
    depth = shard_rows // WIDE
    for index in range(GROUP_HEADS):
        _, key_at, value_at = head_slices(index)
        taken = wide_rows(member * GROUP_HEADS + index, shard_rows)
        for shard, out_ref in enumerate(out_refs):
            sent_ref[index, shard * depth : (shard + 1) * depth, :] = jnp.concatenate(
                [out_ref[taken, key_at], out_ref[taken, value_at]], axis=1
            )


def attend(items):
    scores = [product(key, query, 1, 1) for query, key, _, _ in items]
    weights = []
    for score, (_, _, _, bias) in zip(scores, items):
        score = score * SCALE + bias
        largest = jnp.max(score, axis=0, keepdims=True)
        weight = jnp.exp2(score - largest)
        weights.append((largest, jnp.sum(weight, axis=0, keepdims=True), weight.astype(jnp.bfloat16)))
    return [
        (largest, total, product(value, weight, 0, 0))
        for (largest, total, weight), (_, _, value, _) in zip(weights, items)
    ]


def key_bias(position, valid):
    return jnp.where(position < valid, 0.0, NEG_FILL).astype(jnp.float32)


def merge(one, two):
    top = jnp.maximum(one[0], two[0])
    left = jnp.exp2(one[0] - top)
    right = jnp.exp2(two[0] - top)
    return top, left * one[1] + right * two[1], left * one[2] + right * two[2]


def near_body(valid_ref, *refs):
    qkv_refs, (max_ref, sum_ref, num_ref) = refs[:SHARDS], refs[SHARDS:]
    member, group = group_indices()
    valid = valid_ref[0]
    rows = qkv_refs[0].shape[0]
    count = rows // MID
    depth = rows // WIDE
    bases = [(group * SHARDS + (member ^ apart)) * rows for apart in range(SHARDS)]
    place = place_of(lax.broadcasted_iota(jnp.int32, (rows, LANES), 0), rows)
    lane = lax.broadcasted_iota(jnp.int32, (1, rows), 1)

    def widen(bias):
        return jnp.concatenate([bias] * (rows // LANES), axis=1)

    items = []
    for base, ref in zip(bases, qkv_refs):
        bias = widen(key_bias(place + base, valid))
        for index in range(GROUP_HEADS):
            items.append((*(ref[:, at] for at in head_slices(index)), bias))
    item = lax.broadcasted_iota(jnp.int32, (count, LANES), 0)
    for index in range(GROUP_HEADS):
        head = member * GROUP_HEADS + index
        taken = middle_rows(head, rows)
        position = item % depth * WIDE + item // depth * MID + head % MID
        bias = jnp.concatenate([key_bias(position + base, valid) for base in bases], axis=0)
        items.append(
            (
                *(
                    jnp.concatenate([ref[taken, at] for ref in qkv_refs], axis=0)
                    for at in head_slices(index)
                ),
                widen(bias),
            )
        )
    stats = attend(items)
    for index in range(GROUP_HEADS):
        middle = stats[SHARDS * GROUP_HEADS + index]
        inside = lane // count == (member * GROUP_HEADS + index) % MID
        for shard in range(SHARDS):
            largest, total, number = (
                jnp.concatenate([part[:, shard * count : (shard + 1) * count]] * MID, axis=1)
                for part in middle
            )
            max_ref[index, shard], sum_ref[index, shard], num_ref[index, shard] = merge(
                stats[shard * GROUP_HEADS + index],
                (jnp.where(inside, largest, NEG_FILL), total, number),
            )


def far_body(shards, valid_ref, *refs):
    *refs, out_ref = refs
    qkv_refs, sent_refs, (max_ref, sum_ref, num_ref) = refs[:SHARDS], refs[SHARDS:-3], refs[-3:]
    member, group = group_indices()
    valid = valid_ref[0]
    rows = qkv_refs[0].shape[0]
    depth = rows // WIDE
    count = len(shards) * depth
    item = lax.broadcasted_iota(jnp.int32, (SHARDS * depth, count), 0)
    lane = lax.broadcasted_iota(jnp.int32, (1, rows), 1)
    items = []
    for index in range(GROUP_HEADS):
        head = member * GROUP_HEADS + index
        taken = wide_rows(head, rows)
        query_at = head_slices(index)[0]
        query = jnp.concatenate([qkv_refs[shard][taken, query_at] for shard in shards], axis=0)
        bias = jnp.concatenate(
            [
                key_bias(
                    ((group ^ apart) * SHARDS + (member ^ (item // depth))) * rows
                    + item % depth * WIDE
                    + head,
                    valid,
                )
                for apart in range(len(sent_refs))
            ],
            axis=0,
        )
        both = jnp.concatenate([ref[index] for ref in sent_refs], axis=0)
        items.append((query, both[:, :HEAD_DIM], both[:, HEAD_DIM:], bias))
    for index, (largest, total, number) in enumerate(attend(items)):
        head = member * GROUP_HEADS + index
        stacked = jnp.concatenate(
            [number, jnp.broadcast_to(largest, (8, count)), jnp.broadcast_to(total, (8, count))],
            axis=0,
        )
        stacked = jnp.concatenate(
            [stacked, jnp.zeros((stacked.shape[0], LANES - count), jnp.float32)], axis=1
        )
        block = head % MID * STEPS + head % WIDE // MID
        inside = lane // depth == block
        for slot, shard in enumerate(shards):
            shift = (block * depth - slot * depth + LANES) % LANES
            moved = jnp.concatenate([pltpu.roll(stacked, shift, 1)] * (rows // LANES), axis=1)
            _, total, number = merge(
                (max_ref[index, shard], sum_ref[index, shard], num_ref[index, shard]),
                (
                    jnp.where(inside, moved[HEAD_DIM : HEAD_DIM + 1], NEG_FILL),
                    moved[HEAD_DIM + 8 : HEAD_DIM + 9],
                    moved[:HEAD_DIM],
                ),
            )
            base = (group * SHARDS + (member ^ shard)) * rows
            attention = jnp.where(
                base + place_of(lane, rows) < valid, number * (1.0 / total), 0.0
            )
            out_ref[slot, index * HEAD_DIM : (index + 1) * HEAD_DIM, :] = attention.astype(
                jnp.bfloat16
            )


def gather_body(n_mp, shared, *refs):
    *part_refs, out_ref, order_ref = refs
    order_ref[...] = to_position(order_ref.shape[0])
    assemble(out_ref, part_refs, sources(n_mp, lax.axis_index("ctx") % 2, shared))


def update_body(blocks, *refs):
    *part_refs, weight_ref, order_ref, base_ref, out_ref = refs
    member, _ = group_indices()
    order = order_ref[...]
    update = base_ref[...].astype(jnp.float32)
    for (apart, slot), ref in zip(blocks, part_refs):
        part = product(order, ref[slot], 1, 1).astype(jnp.bfloat16)
        start = pl.multiple_of((member ^ apart) * GROUP_WIDTH, GROUP_WIDTH)
        update = update + product(part, weight_ref[pl.ds(start, GROUP_WIDTH), :])
    out_ref[...] = update.astype(out_ref.dtype)


def fetch(value, turns, shared):
    n_mp, n_ctx = lax.axis_size("mp"), lax.axis_size("ctx")
    if not shared:
        return [flip(value, "mp", apart) for apart in range(1, n_mp)]
    pairs = [
        (c * n_mp + z, c * n_mp + (z ^ (2 + turns(c)))) for c in range(n_ctx) for z in range(n_mp)
    ]
    return [flip(value, "mp", 1), near(lax.ppermute(value, ("ctx", "mp"), pairs))]


def exchange(blocks, shared, mask, *earlier):
    if not shared:
        return blocks
    return blocks + [flip(after(blocks[-1], *earlier), "ctx", mask)]


def local(tile_embeds, norm_gain, norm_bias, w_qkv, w_out, valid_count):
    x = tile_embeds[0]
    rows, width = x.shape
    n_mp = lax.axis_size("mp")
    n_groups = lax.axis_size("ctx") // SHARDS
    depth = rows // WIDE
    weight_rows = w_qkv.shape[0]
    member, _ = group_indices()
    bf16, f32 = jnp.bfloat16, jnp.float32
    shape = pltpu.VMEM
    shared = n_mp == 4 and n_groups % 2 == 0

    def columns(part):
        start = part * width + member * GROUP_WIDTH
        return lax.dynamic_slice(w_qkv, (0, start), (weight_rows, GROUP_WIDTH))

    mine = near(jnp.concatenate([columns(part) for part in range(3)], axis=1))
    fetched = fetch(mine, lambda c: c // SHARDS % 2, shared)

    x_own = near(x)
    x_pair = flip(after(x, mine), "ctx", 1)
    x_far = flip(after(x, mine), "ctx", 2)
    x_last = flip(x_far, "ctx", 1)
    gain, bias = near(norm_gain), near(norm_bias)

    def normalized(one, two, micros):
        blocks = shape((n_mp, rows, weight_rows), bf16)
        return call(norm_body, [blocks] * 2, n_in=4, micros=micros)(
            one, two, gain, bias
        )

    normed = normalized(x_own, x_pair, 3)
    weights = [mine] + exchange(fetched, shared, SHARDS, normed[0])
    normed += normalized(x_far, x_last, 0.01)

    out_weight = after(near(w_out), normed[2])
    out_fetched = fetch(out_weight, lambda c: c % 2, shared)

    early = range(n_mp - 1)
    partial = call(
        lambda *refs: project_body((n_mp, shared, early), *refs),
        [shape((rows, 3 * GROUP_WIDTH), f32)] * SHARDS,
        n_in=SHARDS + len(early),
        micros=1,
    )(*normed, *weights[:-1])
    *qkv, sent = call(
        lambda *refs: project_last_body((n_mp, shared, [n_mp - 1]), *refs),
        [shape((rows, 3 * GROUP_WIDTH), bf16)] * SHARDS
        + [shape((GROUP_HEADS, SHARDS * depth, 2 * HEAD_DIM), bf16)],
        n_in=2 * SHARDS + 1,
        micros=1,
    )(*normed, weights[-1], *partial)
    sents = [sent] + [flip(sent, "ctx", SHARDS * apart) for apart in range(1, n_groups)]
    stats = call(
        near_body,
        [
            shape((GROUP_HEADS, SHARDS, 1, rows), f32),
            shape((GROUP_HEADS, SHARDS, 1, rows), f32),
            shape((GROUP_HEADS, SHARDS, HEAD_DIM, rows), f32),
        ],
        n_scalar=1,
        n_in=SHARDS,
        micros=20,
    )(valid_count, *qkv)

    half = SHARDS // 2

    def finished(shards, sent_parts, micros):
        return call(
            lambda *refs: far_body(shards, *refs),
            [shape((half, GROUP_WIDTH, rows), bf16)],
            n_scalar=1,
            n_in=SHARDS + n_groups + 3,
            micros=micros,
        )(valid_count, *qkv, *sent_parts, *stats)[0]

    sending = finished(range(half, SHARDS), sents, 1)
    staying = finished(range(half), [after(sents[0], sending, *out_fetched)] + sents[1:], 5)
    far_part = flip(sending, "ctx", 2)
    pair_part = flip(staying, "ctx", 1)
    out_parts = [out_weight] + exchange(out_fetched, shared, 1, sending)
    whole_out, order = call(
        lambda *refs: gather_body(n_mp, shared, *refs),
        [shape((width, width), bf16), shape((rows, rows), bf16)],
        n_in=n_mp,
        micros=0.001,
    )(*out_parts)
    total = x_own
    last_part = flip(after(far_part, pair_part), "ctx", 1)
    steps = [
        ([(0, 0), (1, 1)], [staying, pair_part], shape((rows, width), f32)),
        ([(2, 0)], [far_part], shape((rows, width), f32)),
        ([(3, 1)], [last_part], jax.ShapeDtypeStruct((rows, width), bf16)),
    ]
    for blocks, operands, out_shape in steps:
        (total,) = call(
            lambda *refs, blocks=blocks: update_body(blocks, *refs),
            [out_shape],
            n_in=len(operands) + 3,
            micros=0.001,
        )(*operands, whole_out, order, total)
    return total[None]


def solution(mesh):
    placed = (P("mp", "ctx", None), P(), P(), P("mp", None), P("mp", None), P("mp"))
    return jax.shard_map(
        local, mesh=mesh, in_specs=placed, out_specs=P("mp", "ctx", None), check_vma=False
    )
```

```python
import math

import jax
import jax.numpy as jnp
from jax import lax
from jax.experimental import pallas as pl
from jax.experimental.pallas import tpu as pltpu
from jax.sharding import PartitionSpec as P

HEADS = 12
HEAD_DIM = 64
MID = 4
WIDE = 16
SHARDS = 4
STEPS = WIDE // MID
GROUP_HEADS = HEADS // SHARDS
GROUP_WIDTH = GROUP_HEADS * HEAD_DIM
NEG_FILL = -1e30
SCALE = math.log2(math.e) / math.sqrt(HEAD_DIM)
VMEM_LIMIT = 24 * 1024 * 1024
LANES = 128


def call(body, out_shape, scratch=(), n_scalar=0, n_in=0, micros=1):
    specs = [pl.BlockSpec(memory_space=pltpu.SMEM)] * n_scalar + [
        pl.BlockSpec(memory_space=pltpu.VMEM)
    ] * n_in
    outs = [pl.BlockSpec(memory_space=pltpu.VMEM) for _ in out_shape]
    return pl.pallas_call(
        body,
        out_shape=out_shape,
        in_specs=specs,
        out_specs=outs,
        scratch_shapes=list(scratch),
        cost_estimate=pl.CostEstimate(
            flops=int(micros * 3_000_000_000), transcendentals=0, bytes_accessed=int(micros * 9_000_000)
        ),
        compiler_params=pltpu.CompilerParams(vmem_limit_bytes=VMEM_LIMIT),
    )


def near(value):
    return pltpu.with_memory_space_constraint(value, pltpu.VMEM)


def flip(value, axis, mask):
    pairs = [(source, source ^ mask) for source in range(lax.axis_size(axis))]
    return near(lax.ppermute(value, axis, pairs))


def after(value, *earlier):
    return lax.optimization_barrier((value, *earlier))[0]


def place_of(order, rows):
    depth = rows // WIDE
    return order % depth * WIDE + order // depth % STEPS * MID + order // (STEPS * depth)


def to_order(rows):
    new = lax.broadcasted_iota(jnp.int32, (rows, rows), 0)
    old = lax.broadcasted_iota(jnp.int32, (rows, rows), 1)
    return (old == place_of(new, rows)).astype(jnp.bfloat16)


def to_position(rows):
    new = lax.broadcasted_iota(jnp.int32, (rows, rows), 0)
    old = lax.broadcasted_iota(jnp.int32, (rows, rows), 1)
    return (new == place_of(old, rows)).astype(jnp.bfloat16)


def product(left, right, left_axis=1, right_axis=0):
    return lax.dot_general(
        left,
        right,
        (((left_axis,), (right_axis,)), ((), ())),
        preferred_element_type=jnp.float32,
    )


def norm_body(*refs):
    count = len(refs) // 2 - 1
    x_refs, gain_ref, bias_ref, out_refs = refs[:count], refs[count], refs[count + 1], refs[count + 2 :]
    order = to_order(x_refs[0].shape[0])
    gain = gain_ref[...][None, :]
    bias = bias_ref[...][None, :]
    for x_ref, out_ref in zip(x_refs, out_refs):
        floats = x_ref[...].astype(jnp.float32)
        centred = floats - jnp.mean(floats, axis=-1, keepdims=True)
        spread = jnp.mean(centred * centred, axis=-1, keepdims=True)
        normed = (centred * lax.rsqrt(spread + 1e-05) * gain + bias).astype(jnp.bfloat16)
        ordered = product(order, normed).astype(jnp.bfloat16)
        blocks, _, width = out_ref.shape
        for block in range(blocks):
            out_ref[block] = ordered[:, block * width : (block + 1) * width]


def group_indices():
    shard = lax.axis_index("ctx")
    return shard % SHARDS, shard // SHARDS


def head_slices(index):
    return [
        slice(part * GROUP_WIDTH + index * HEAD_DIM, part * GROUP_WIDTH + (index + 1) * HEAD_DIM)
        for part in range(3)
    ]


def wide_rows(head, rows):
    depth = rows // WIDE
    start = head % MID * (STEPS * depth) + head % WIDE // MID * depth
    return pl.ds(pl.multiple_of(start, depth), depth)


def middle_rows(head, rows):
    count = rows // MID
    return pl.ds(pl.multiple_of(head % MID * count, count), count)


def assemble(whole_ref, refs, sources):
    for ref, source in zip(refs, sources):
        rows = ref.shape[0]
        whole_ref[pl.ds(pl.multiple_of(source * rows, 16), rows), :] = ref[...]


def sources(n_mp, turn, shared):
    mp_index = lax.axis_index("mp")
    if shared:
        return [mp_index, mp_index ^ 1, mp_index ^ (2 + turn), mp_index ^ (3 - turn)]
    return [mp_index ^ apart for apart in range(n_mp)]


def project_body(blocks, *refs):
    _, group = group_indices()
    normed_refs, refs = refs[:SHARDS], refs[SHARDS:]
    n_mp, shared, some = blocks
    weight_refs, refs = refs[: len(some)], refs[len(some) :]
    base_refs, out_refs = refs[:-SHARDS], refs[-SHARDS:]
    origin = sources(n_mp, group % 2, shared)
    for shard, (normed_ref, out_ref) in enumerate(zip(normed_refs, out_refs)):
        total = base_refs[shard][...] if base_refs else 0.0
        for block, weight_ref in zip(some, weight_refs):
            total = total + product(normed_ref[origin[block]], weight_ref[...])
        out_ref[...] = total.astype(out_ref.dtype)


def project_last_body(blocks, *refs):
    *refs, sent_ref = refs
    project_body(blocks, *refs)
    out_refs = refs[-SHARDS:]
    member, _ = group_indices()
    shard_rows = out_refs[0].shape[0]
    depth = shard_rows // WIDE
    for index in range(GROUP_HEADS):
        _, key_at, value_at = head_slices(index)
        taken = wide_rows(member * GROUP_HEADS + index, shard_rows)
        for shard, out_ref in enumerate(out_refs):
            sent_ref[index, shard * depth : (shard + 1) * depth, :] = jnp.concatenate(
                [out_ref[taken, key_at], out_ref[taken, value_at]], axis=1
            )


def attend(items):
    scores = [product(key, query, 1, 1) for query, key, _, _ in items]
    weights = []
    for score, (_, _, _, bias) in zip(scores, items):
        score = score * SCALE + bias
        largest = jnp.max(score, axis=0, keepdims=True)
        weight = jnp.exp2(score - largest)
        weights.append((largest, jnp.sum(weight, axis=0, keepdims=True), weight.astype(jnp.bfloat16)))
    return [
        (largest, total, product(value, weight, 0, 0))
        for (largest, total, weight), (_, _, value, _) in zip(weights, items)
    ]


def key_bias(position, valid):
    return jnp.where(position < valid, 0.0, NEG_FILL).astype(jnp.float32)


def merge(one, two):
    top = jnp.maximum(one[0], two[0])
    left = jnp.exp2(one[0] - top)
    right = jnp.exp2(two[0] - top)
    return top, left * one[1] + right * two[1], left * one[2] + right * two[2]


def near_body(valid_ref, *refs):
    qkv_refs, (max_ref, sum_ref, num_ref) = refs[:SHARDS], refs[SHARDS:]
    member, group = group_indices()
    valid = valid_ref[0]
    rows = qkv_refs[0].shape[0]
    count = rows // MID
    depth = rows // WIDE
    bases = [(group * SHARDS + (member ^ apart)) * rows for apart in range(SHARDS)]
    place = place_of(lax.broadcasted_iota(jnp.int32, (rows, LANES), 0), rows)
    lane = lax.broadcasted_iota(jnp.int32, (1, rows), 1)

    def widen(bias):
        return jnp.concatenate([bias] * (rows // LANES), axis=1)

    items = []
    for base, ref in zip(bases, qkv_refs):
        bias = widen(key_bias(place + base, valid))
        for index in range(GROUP_HEADS):
            items.append((*(ref[:, at] for at in head_slices(index)), bias))
    item = lax.broadcasted_iota(jnp.int32, (count, LANES), 0)
    for index in range(GROUP_HEADS):
        head = member * GROUP_HEADS + index
        taken = middle_rows(head, rows)
        position = item % depth * WIDE + item // depth * MID + head % MID
        bias = jnp.concatenate([key_bias(position + base, valid) for base in bases], axis=0)
        items.append(
            (
                *(
                    jnp.concatenate([ref[taken, at] for ref in qkv_refs], axis=0)
                    for at in head_slices(index)
                ),
                widen(bias),
            )
        )
    stats = attend(items)
    for index in range(GROUP_HEADS):
        middle = stats[SHARDS * GROUP_HEADS + index]
        inside = lane // count == (member * GROUP_HEADS + index) % MID
        for shard in range(SHARDS):
            largest, total, number = (
                jnp.concatenate([part[:, shard * count : (shard + 1) * count]] * MID, axis=1)
                for part in middle
            )
            max_ref[index, shard], sum_ref[index, shard], num_ref[index, shard] = merge(
                stats[shard * GROUP_HEADS + index],
                (jnp.where(inside, largest, NEG_FILL), total, number),
            )


def far_body(shards, valid_ref, *refs):
    *refs, out_ref = refs
    qkv_refs, sent_refs, (max_ref, sum_ref, num_ref) = refs[:SHARDS], refs[SHARDS:-3], refs[-3:]
    member, group = group_indices()
    valid = valid_ref[0]
    rows = qkv_refs[0].shape[0]
    depth = rows // WIDE
    count = len(shards) * depth
    item = lax.broadcasted_iota(jnp.int32, (SHARDS * depth, count), 0)
    lane = lax.broadcasted_iota(jnp.int32, (1, rows), 1)
    items = []
    for index in range(GROUP_HEADS):
        head = member * GROUP_HEADS + index
        taken = wide_rows(head, rows)
        query_at = head_slices(index)[0]
        query = jnp.concatenate([qkv_refs[shard][taken, query_at] for shard in shards], axis=0)
        bias = jnp.concatenate(
            [
                key_bias(
                    ((group ^ apart) * SHARDS + (member ^ (item // depth))) * rows
                    + item % depth * WIDE
                    + head,
                    valid,
                )
                for apart in range(len(sent_refs))
            ],
            axis=0,
        )
        both = jnp.concatenate([ref[index] for ref in sent_refs], axis=0)
        items.append((query, both[:, :HEAD_DIM], both[:, HEAD_DIM:], bias))
    for index, (largest, total, number) in enumerate(attend(items)):
        head = member * GROUP_HEADS + index
        stacked = jnp.concatenate(
            [number, jnp.broadcast_to(largest, (8, count)), jnp.broadcast_to(total, (8, count))],
            axis=0,
        )
        stacked = jnp.concatenate(
            [stacked, jnp.zeros((stacked.shape[0], LANES - count), jnp.float32)], axis=1
        )
        block = head % MID * STEPS + head % WIDE // MID
        inside = lane // depth == block
        for slot, shard in enumerate(shards):
            shift = (block * depth - slot * depth + LANES) % LANES
            moved = jnp.concatenate([pltpu.roll(stacked, shift, 1)] * (rows // LANES), axis=1)
            _, total, number = merge(
                (max_ref[index, shard], sum_ref[index, shard], num_ref[index, shard]),
                (
                    jnp.where(inside, moved[HEAD_DIM : HEAD_DIM + 1], NEG_FILL),
                    moved[HEAD_DIM + 8 : HEAD_DIM + 9],
                    moved[:HEAD_DIM],
                ),
            )
            base = (group * SHARDS + (member ^ shard)) * rows
            attention = jnp.where(
                base + place_of(lane, rows) < valid, number * (1.0 / total), 0.0
            )
            out_ref[slot, index * HEAD_DIM : (index + 1) * HEAD_DIM, :] = attention.astype(
                jnp.bfloat16
            )


def gather_body(n_mp, shared, *refs):
    *part_refs, out_ref, order_ref = refs
    order_ref[...] = to_position(order_ref.shape[0])
    member, group = group_indices()
    origin = sources(n_mp, group % 2, shared)
    rows = part_refs[0].shape[0]
    starts = [source * rows for source in origin]
    if shared:
        core, half = member % 2, rows // 2
        starts = starts[:1] + [
            start + side * half for side in (core, 1 - core) for start in starts[1:]
        ]
    for ref, start in zip(part_refs, starts):
        out_ref[pl.ds(pl.multiple_of(start, 16), ref.shape[0]), :] = ref[...]


def update_body(blocks, *refs):
    *part_refs, weight_ref, order_ref, base_ref, out_ref = refs
    member, _ = group_indices()
    order = order_ref[...]
    update = base_ref[...].astype(jnp.float32)
    for (apart, slot), ref in zip(blocks, part_refs):
        part = product(order, ref[slot], 1, 1).astype(jnp.bfloat16)
        start = pl.multiple_of((member ^ apart) * GROUP_WIDTH, GROUP_WIDTH)
        update = update + product(part, weight_ref[pl.ds(start, GROUP_WIDTH), :])
    out_ref[...] = update.astype(out_ref.dtype)


def fetch(value, turns, shared):
    n_mp, n_ctx = lax.axis_size("mp"), lax.axis_size("ctx")
    if not shared:
        return [flip(value, "mp", apart) for apart in range(1, n_mp)]
    pairs = [
        (c * n_mp + z, c * n_mp + (z ^ (2 + turns(c)))) for c in range(n_ctx) for z in range(n_mp)
    ]
    return [flip(value, "mp", 1), near(lax.ppermute(value, ("ctx", "mp"), pairs))]


def exchange(blocks, shared, mask, *earlier):
    if not shared:
        return blocks
    return blocks + [flip(after(blocks[-1], *earlier), "ctx", mask)]


def local(tile_embeds, norm_gain, norm_bias, w_qkv, w_out, valid_count):
    x = tile_embeds[0]
    rows, width = x.shape
    n_mp = lax.axis_size("mp")
    n_groups = lax.axis_size("ctx") // SHARDS
    depth = rows // WIDE
    weight_rows = w_qkv.shape[0]
    member, _ = group_indices()
    bf16, f32 = jnp.bfloat16, jnp.float32
    shape = pltpu.VMEM
    shared = n_mp == 4 and n_groups % 2 == 0 and weight_rows % 32 == 0

    def columns(part):
        start = part * width + member * GROUP_WIDTH
        return lax.dynamic_slice(w_qkv, (0, start), (weight_rows, GROUP_WIDTH))

    mine = near(jnp.concatenate([columns(part) for part in range(3)], axis=1))
    fetched = fetch(mine, lambda c: c // SHARDS % 2, shared)

    x_own = near(x)
    x_pair = flip(after(x, mine), "ctx", 1)
    x_far = flip(after(x, mine), "ctx", 2)
    x_last = flip(x_far, "ctx", 1)
    gain, bias = near(norm_gain), near(norm_bias)

    def normalized(one, two, micros):
        blocks = shape((n_mp, rows, weight_rows), bf16)
        return call(norm_body, [blocks] * 2, n_in=4, micros=micros)(
            one, two, gain, bias
        )

    normed = normalized(x_own, x_pair, 3)
    weights = [mine] + exchange(fetched, shared, SHARDS, normed[0])
    normed += normalized(x_far, x_last, 0.01)

    out_own = near(w_out)
    out_weight = w_out
    if shared:
        size = weight_rows // 2
        out_weight = lax.dynamic_slice(w_out, (member % 2 * size, 0), (size, width))
    out_weight = after(near(out_weight), normed[2])
    out_fetched = fetch(out_weight, lambda c: c // SHARDS % 2, shared)

    early = range(n_mp - 1)
    partial = call(
        lambda *refs: project_body((n_mp, shared, early), *refs),
        [shape((rows, 3 * GROUP_WIDTH), f32)] * SHARDS,
        n_in=SHARDS + len(early),
        micros=1,
    )(*normed, *weights[:-1])
    *qkv, sent = call(
        lambda *refs: project_last_body((n_mp, shared, [n_mp - 1]), *refs),
        [shape((rows, 3 * GROUP_WIDTH), bf16)] * SHARDS
        + [shape((GROUP_HEADS, SHARDS * depth, 2 * HEAD_DIM), bf16)],
        n_in=2 * SHARDS + 1,
        micros=1,
    )(*normed, weights[-1], *partial)
    sents = [sent] + [flip(sent, "ctx", SHARDS * apart) for apart in range(1, n_groups)]
    stats = call(
        near_body,
        [
            shape((GROUP_HEADS, SHARDS, 1, rows), f32),
            shape((GROUP_HEADS, SHARDS, 1, rows), f32),
            shape((GROUP_HEADS, SHARDS, HEAD_DIM, rows), f32),
        ],
        n_scalar=1,
        n_in=SHARDS,
        micros=1,
    )(valid_count, *qkv)

    half = SHARDS // 2

    def finished(shards, sent_parts, micros):
        return call(
            lambda *refs: far_body(shards, *refs),
            [shape((half, GROUP_WIDTH, rows), bf16)],
            n_scalar=1,
            n_in=SHARDS + n_groups + 3,
            micros=micros,
        )(valid_count, *qkv, *sent_parts, *stats)[0]

    sending = finished(range(half, SHARDS), sents, 1)
    last_fetched = out_fetched[-1]
    staying = finished(range(half), [after(sents[0], sending, last_fetched)] + sents[1:], 0.01)
    far_part = flip(sending, "ctx", 2)
    pair_part = flip(staying, "ctx", 1)
    out_blocks = exchange(out_fetched, shared, SHARDS, stats[0])
    out_parts = [out_own] + out_blocks
    if shared:
        out_parts += [flip(after(value, sending), "ctx", 1) for value in out_blocks]
    whole_out, order = call(
        lambda *refs: gather_body(n_mp, shared, *refs),
        [shape((width, width), bf16), shape((rows, rows), bf16)],
        n_in=len(out_parts),
        micros=0.001,
    )(*out_parts)
    total = x_own
    last_part = flip(after(far_part, pair_part, whole_out), "ctx", 1)
    steps = [
        ([(0, 0), (1, 1)], [staying, pair_part], shape((rows, width), f32)),
        ([(2, 0)], [far_part], shape((rows, width), f32)),
        ([(3, 1)], [last_part], jax.ShapeDtypeStruct((rows, width), bf16)),
    ]
    for blocks, operands, out_shape in steps:
        (total,) = call(
            lambda *refs, blocks=blocks: update_body(blocks, *refs),
            [out_shape],
            n_in=len(operands) + 3,
            micros=0.001,
        )(*operands, whole_out, order, total)
    return total[None]


def solution(mesh):
    placed = (P("mp", "ctx", None), P(), P(), P("mp", None), P("mp", None), P("mp"))
    return jax.shard_map(
        local, mesh=mesh, in_specs=placed, out_specs=P("mp", "ctx", None), check_vma=False
    )
```

```python
import math

import jax
import jax.numpy as jnp
from jax import lax
from jax.experimental import pallas as pl
from jax.experimental.pallas import tpu as pltpu
from jax.sharding import PartitionSpec as P

HEADS = 12
HEAD_DIM = 64
MID = 4
WIDE = 16
SHARDS = 4
STEPS = WIDE // MID
GROUP_HEADS = HEADS // SHARDS
GROUP_WIDTH = GROUP_HEADS * HEAD_DIM
NEG_FILL = -1e30
SCALE = math.log2(math.e) / math.sqrt(HEAD_DIM)
VMEM_LIMIT = 24 * 1024 * 1024
LANES = 128


def call(body, out_shape, scratch=(), n_scalar=0, n_in=0, micros=1):
    specs = [pl.BlockSpec(memory_space=pltpu.SMEM)] * n_scalar + [
        pl.BlockSpec(memory_space=pltpu.VMEM)
    ] * n_in
    outs = [pl.BlockSpec(memory_space=pltpu.VMEM) for _ in out_shape]
    return pl.pallas_call(
        body,
        out_shape=out_shape,
        in_specs=specs,
        out_specs=outs,
        scratch_shapes=list(scratch),
        cost_estimate=pl.CostEstimate(
            flops=int(micros * 3_000_000_000), transcendentals=0, bytes_accessed=int(micros * 9_000_000)
        ),
        compiler_params=pltpu.CompilerParams(vmem_limit_bytes=VMEM_LIMIT),
    )


def near(value):
    return pltpu.with_memory_space_constraint(value, pltpu.VMEM)


def flip(value, axis, mask):
    pairs = [(source, source ^ mask) for source in range(lax.axis_size(axis))]
    return near(lax.ppermute(value, axis, pairs))


def after(value, *earlier):
    return lax.optimization_barrier((value, *earlier))[0]


def place_of(order, rows):
    depth = rows // WIDE
    return order % depth * WIDE + order // depth % STEPS * MID + order // (STEPS * depth)


def to_order(rows):
    new = lax.broadcasted_iota(jnp.int32, (rows, rows), 0)
    old = lax.broadcasted_iota(jnp.int32, (rows, rows), 1)
    return (old == place_of(new, rows)).astype(jnp.bfloat16)


def to_position(rows):
    new = lax.broadcasted_iota(jnp.int32, (rows, rows), 0)
    old = lax.broadcasted_iota(jnp.int32, (rows, rows), 1)
    return (new == place_of(old, rows)).astype(jnp.bfloat16)


def product(left, right, left_axis=1, right_axis=0):
    return lax.dot_general(
        left,
        right,
        (((left_axis,), (right_axis,)), ((), ())),
        preferred_element_type=jnp.float32,
    )


def norm_body(*refs):
    count = len(refs) // 2 - 1
    x_refs, gain_ref, bias_ref, out_refs = refs[:count], refs[count], refs[count + 1], refs[count + 2 :]
    order = to_order(x_refs[0].shape[0])
    gain = gain_ref[...][None, :]
    bias = bias_ref[...][None, :]
    for x_ref, out_ref in zip(x_refs, out_refs):
        floats = x_ref[...].astype(jnp.float32)
        centred = floats - jnp.mean(floats, axis=-1, keepdims=True)
        spread = jnp.mean(centred * centred, axis=-1, keepdims=True)
        normed = (centred * lax.rsqrt(spread + 1e-05) * gain + bias).astype(jnp.bfloat16)
        ordered = product(order, normed).astype(jnp.bfloat16)
        blocks, _, width = out_ref.shape
        for block in range(blocks):
            out_ref[block] = ordered[:, block * width : (block + 1) * width]


def group_indices():
    shard = lax.axis_index("ctx")
    return shard % SHARDS, shard // SHARDS


def head_slices(index):
    return [
        slice(part * GROUP_WIDTH + index * HEAD_DIM, part * GROUP_WIDTH + (index + 1) * HEAD_DIM)
        for part in range(3)
    ]


def wide_rows(head, rows):
    depth = rows // WIDE
    start = head % MID * (STEPS * depth) + head % WIDE // MID * depth
    return pl.ds(pl.multiple_of(start, depth), depth)


def middle_rows(head, rows):
    count = rows // MID
    return pl.ds(pl.multiple_of(head % MID * count, count), count)


def assemble(whole_ref, refs, sources):
    for ref, source in zip(refs, sources):
        rows = ref.shape[0]
        whole_ref[pl.ds(pl.multiple_of(source * rows, 16), rows), :] = ref[...]


def sources(n_mp, turn, shared):
    mp_index = lax.axis_index("mp")
    if shared:
        return [mp_index, mp_index ^ 1, mp_index ^ (2 + turn), mp_index ^ (3 - turn)]
    return [mp_index ^ apart for apart in range(n_mp)]


def project_body(blocks, *refs):
    _, group = group_indices()
    normed_refs, refs = refs[:SHARDS], refs[SHARDS:]
    n_mp, shared, some = blocks
    weight_refs, refs = refs[: len(some)], refs[len(some) :]
    base_refs, out_refs = refs[:-SHARDS], refs[-SHARDS:]
    origin = sources(n_mp, group % 2, shared)
    for shard, (normed_ref, out_ref) in enumerate(zip(normed_refs, out_refs)):
        total = base_refs[shard][...] if base_refs else 0.0
        for (block, first), weight_ref in zip(some, weight_refs):
            columns = slice(first, first + weight_ref.shape[0])
            total = total + product(normed_ref[origin[block], :, columns], weight_ref[...])
        out_ref[...] = total.astype(out_ref.dtype)


def project_last_body(blocks, *refs):
    *refs, sent_ref = refs
    project_body(blocks, *refs)
    out_refs = refs[-SHARDS:]
    member, _ = group_indices()
    shard_rows = out_refs[0].shape[0]
    depth = shard_rows // WIDE
    for index in range(GROUP_HEADS):
        _, key_at, value_at = head_slices(index)
        taken = wide_rows(member * GROUP_HEADS + index, shard_rows)
        for shard, out_ref in enumerate(out_refs):
            sent_ref[index, shard * depth : (shard + 1) * depth, :] = jnp.concatenate(
                [out_ref[taken, key_at], out_ref[taken, value_at]], axis=1
            )


def attend(items):
    scores = [product(key, query, 1, 1) for query, key, _, _ in items]
    weights = []
    for score, (_, _, _, bias) in zip(scores, items):
        score = score * SCALE + bias
        largest = jnp.max(score, axis=0, keepdims=True)
        weight = jnp.exp2(score - largest)
        weights.append((largest, jnp.sum(weight, axis=0, keepdims=True), weight.astype(jnp.bfloat16)))
    return [
        (largest, total, product(value, weight, 0, 0))
        for (largest, total, weight), (_, _, value, _) in zip(weights, items)
    ]


def key_bias(position, valid):
    return jnp.where(position < valid, 0.0, NEG_FILL).astype(jnp.float32)


def merge(one, two):
    top = jnp.maximum(one[0], two[0])
    left = jnp.exp2(one[0] - top)
    right = jnp.exp2(two[0] - top)
    return top, left * one[1] + right * two[1], left * one[2] + right * two[2]


def near_body(valid_ref, *refs):
    qkv_refs, (max_ref, sum_ref, num_ref) = refs[:SHARDS], refs[SHARDS:]
    member, group = group_indices()
    valid = valid_ref[0]
    rows = qkv_refs[0].shape[0]
    count = rows // MID
    depth = rows // WIDE
    bases = [(group * SHARDS + (member ^ apart)) * rows for apart in range(SHARDS)]
    place = place_of(lax.broadcasted_iota(jnp.int32, (rows, LANES), 0), rows)
    lane = lax.broadcasted_iota(jnp.int32, (1, rows), 1)

    def widen(bias):
        return jnp.concatenate([bias] * (rows // LANES), axis=1)

    items = []
    for base, ref in zip(bases, qkv_refs):
        bias = widen(key_bias(place + base, valid))
        for index in range(GROUP_HEADS):
            items.append((*(ref[:, at] for at in head_slices(index)), bias))
    item = lax.broadcasted_iota(jnp.int32, (count, LANES), 0)
    for index in range(GROUP_HEADS):
        head = member * GROUP_HEADS + index
        taken = middle_rows(head, rows)
        position = item % depth * WIDE + item // depth * MID + head % MID
        bias = jnp.concatenate([key_bias(position + base, valid) for base in bases], axis=0)
        items.append(
            (
                *(
                    jnp.concatenate([ref[taken, at] for ref in qkv_refs], axis=0)
                    for at in head_slices(index)
                ),
                widen(bias),
            )
        )
    stats = attend(items)
    for index in range(GROUP_HEADS):
        middle = stats[SHARDS * GROUP_HEADS + index]
        inside = lane // count == (member * GROUP_HEADS + index) % MID
        for shard in range(SHARDS):
            largest, total, number = (
                jnp.concatenate([part[:, shard * count : (shard + 1) * count]] * MID, axis=1)
                for part in middle
            )
            max_ref[index, shard], sum_ref[index, shard], num_ref[index, shard] = merge(
                stats[shard * GROUP_HEADS + index],
                (jnp.where(inside, largest, NEG_FILL), total, number),
            )


def far_body(shards, valid_ref, *refs):
    *refs, out_ref = refs
    qkv_refs, sent_refs, (max_ref, sum_ref, num_ref) = refs[:SHARDS], refs[SHARDS:-3], refs[-3:]
    member, group = group_indices()
    valid = valid_ref[0]
    rows = qkv_refs[0].shape[0]
    depth = rows // WIDE
    count = len(shards) * depth
    item = lax.broadcasted_iota(jnp.int32, (SHARDS * depth, count), 0)
    lane = lax.broadcasted_iota(jnp.int32, (1, rows), 1)
    items = []
    for index in range(GROUP_HEADS):
        head = member * GROUP_HEADS + index
        taken = wide_rows(head, rows)
        query_at = head_slices(index)[0]
        query = jnp.concatenate([qkv_refs[shard][taken, query_at] for shard in shards], axis=0)
        bias = jnp.concatenate(
            [
                key_bias(
                    ((group ^ apart) * SHARDS + (member ^ (item // depth))) * rows
                    + item % depth * WIDE
                    + head,
                    valid,
                )
                for apart in range(len(sent_refs))
            ],
            axis=0,
        )
        both = jnp.concatenate([ref[index] for ref in sent_refs], axis=0)
        items.append((query, both[:, :HEAD_DIM], both[:, HEAD_DIM:], bias))
    for index, (largest, total, number) in enumerate(attend(items)):
        head = member * GROUP_HEADS + index
        stacked = jnp.concatenate(
            [number, jnp.broadcast_to(largest, (8, count)), jnp.broadcast_to(total, (8, count))],
            axis=0,
        )
        stacked = jnp.concatenate(
            [stacked, jnp.zeros((stacked.shape[0], LANES - count), jnp.float32)], axis=1
        )
        block = head % MID * STEPS + head % WIDE // MID
        inside = lane // depth == block
        for slot, shard in enumerate(shards):
            shift = (block * depth - slot * depth + LANES) % LANES
            moved = jnp.concatenate([pltpu.roll(stacked, shift, 1)] * (rows // LANES), axis=1)
            _, total, number = merge(
                (max_ref[index, shard], sum_ref[index, shard], num_ref[index, shard]),
                (
                    jnp.where(inside, moved[HEAD_DIM : HEAD_DIM + 1], NEG_FILL),
                    moved[HEAD_DIM + 8 : HEAD_DIM + 9],
                    moved[:HEAD_DIM],
                ),
            )
            base = (group * SHARDS + (member ^ shard)) * rows
            attention = jnp.where(
                base + place_of(lane, rows) < valid, number * (1.0 / total), 0.0
            )
            out_ref[slot, index * HEAD_DIM : (index + 1) * HEAD_DIM, :] = attention.astype(
                jnp.bfloat16
            )


def gather_body(n_mp, shared, *refs):
    *part_refs, out_ref, order_ref = refs
    order_ref[...] = to_position(order_ref.shape[0])
    member, group = group_indices()
    origin = sources(n_mp, group % 2, shared)
    rows = part_refs[0].shape[0]
    starts = [source * rows for source in origin]
    if shared:
        core, half = member % 2, rows // 2
        starts = starts[:1] + [
            start + side * half for side in (core, 1 - core) for start in starts[1:]
        ]
    for ref, start in zip(part_refs, starts):
        out_ref[pl.ds(pl.multiple_of(start, 16), ref.shape[0]), :] = ref[...]


def update_body(blocks, *refs):
    *part_refs, weight_ref, order_ref, base_ref, out_ref = refs
    member, _ = group_indices()
    order = order_ref[...]
    update = base_ref[...].astype(jnp.float32)
    for (apart, slot), ref in zip(blocks, part_refs):
        part = product(order, ref[slot], 1, 1).astype(jnp.bfloat16)
        start = pl.multiple_of((member ^ apart) * GROUP_WIDTH, GROUP_WIDTH)
        update = update + product(part, weight_ref[pl.ds(start, GROUP_WIDTH), :])
    out_ref[...] = update.astype(out_ref.dtype)


def fetch_far(value, turns):
    n_mp, n_ctx = lax.axis_size("mp"), lax.axis_size("ctx")
    pairs = [
        (c * n_mp + z, c * n_mp + (z ^ (2 + turns(c)))) for c in range(n_ctx) for z in range(n_mp)
    ]
    return near(lax.ppermute(value, ("ctx", "mp"), pairs))


def local(tile_embeds, norm_gain, norm_bias, w_qkv, w_out, valid_count):
    x = tile_embeds[0]
    rows, width = x.shape
    n_mp = lax.axis_size("mp")
    n_groups = lax.axis_size("ctx") // SHARDS
    depth = rows // WIDE
    weight_rows = w_qkv.shape[0]
    member, _ = group_indices()
    bf16, f32 = jnp.bfloat16, jnp.float32
    shape = pltpu.VMEM
    shared = n_mp == 4 and n_groups % 2 == 0 and weight_rows % 32 == 0

    def columns(part):
        start = part * width + member * GROUP_WIDTH
        return lax.dynamic_slice(w_qkv, (0, start), (weight_rows, GROUP_WIDTH))

    chosen = jnp.concatenate([columns(part) for part in range(3)], axis=1)
    mine = near(chosen)
    parity = lambda c: c // SHARDS % 2
    cut = weight_rows // 3
    if shared:
        pieces = [fetch_far(near(part), parity) for part in (chosen[:cut], chosen[cut:])]

    x_own = near(x)
    x_pair = flip(after(x, mine), "ctx", 1)
    x_far = flip(after(x, mine), "ctx", 2)
    x_last = flip(x_far, "ctx", 1)
    if shared:
        closest = flip(after(mine, x_far), "mp", 1)
    gain, bias = near(norm_gain), near(norm_bias)

    def normalized(one, two, micros):
        blocks = shape((n_mp, rows, weight_rows), bf16)
        return call(norm_body, [blocks] * 2, n_in=4, micros=micros)(
            one, two, gain, bias
        )

    normed = normalized(x_own, x_pair, 1)
    if shared:
        swapped = [flip(after(pieces[0]), "ctx", SHARDS)]
        swapped.append(flip(after(pieces[1], normed[0]), "ctx", SHARDS))
        weights = [mine, closest, *pieces, *swapped]
        blocks = [(0, 0), (1, 0), (2, 0), (2, cut), (3, 0), (3, cut)]
    else:
        weights = [mine] + [flip(mine, "mp", apart) for apart in range(1, n_mp)]
        blocks = [(apart, 0) for apart in range(n_mp)]
    normed += normalized(x_far, x_last, 1)

    out_own = near(w_out)
    out_weight = w_out
    if shared:
        size = weight_rows // 2
        out_weight = lax.dynamic_slice(w_out, (member % 2 * size, 0), (size, width))
    out_weight = after(near(out_weight), x_last)
    if shared:
        out_fetched = [flip(out_weight, "mp", 1), fetch_far(out_weight, parity)]
    else:
        out_fetched = [flip(out_weight, "mp", apart) for apart in range(1, n_mp)]

    partial = call(
        lambda *refs: project_body((n_mp, shared, blocks[:-1]), *refs),
        [shape((rows, 3 * GROUP_WIDTH), f32)] * SHARDS,
        n_in=SHARDS + len(blocks) - 1,
        micros=1,
    )(*normed, *weights[:-1])
    *qkv, sent = call(
        lambda *refs: project_last_body((n_mp, shared, blocks[-1:]), *refs),
        [shape((rows, 3 * GROUP_WIDTH), bf16)] * SHARDS
        + [shape((GROUP_HEADS, SHARDS * depth, 2 * HEAD_DIM), bf16)],
        n_in=2 * SHARDS + 1,
        micros=1,
    )(*normed, weights[-1], *partial)
    sents = [sent] + [flip(sent, "ctx", SHARDS * apart) for apart in range(1, n_groups)]
    stats = call(
        near_body,
        [
            shape((GROUP_HEADS, SHARDS, 1, rows), f32),
            shape((GROUP_HEADS, SHARDS, 1, rows), f32),
            shape((GROUP_HEADS, SHARDS, HEAD_DIM, rows), f32),
        ],
        n_scalar=1,
        n_in=SHARDS,
        micros=20,
    )(valid_count, *qkv)

    half = SHARDS // 2

    def finished(shards, sent_parts, micros):
        return call(
            lambda *refs: far_body(shards, *refs),
            [shape((half, GROUP_WIDTH, rows), bf16)],
            n_scalar=1,
            n_in=SHARDS + n_groups + 3,
            micros=micros,
        )(valid_count, *qkv, *sent_parts, *stats)[0]

    sending = finished(range(half, SHARDS), sents, 1)
    last_fetched = out_fetched[-1]
    staying = finished(range(half), [after(sents[0], sending, last_fetched)] + sents[1:], 0.01)
    far_part = flip(sending, "ctx", 2)
    pair_part = flip(staying, "ctx", 1)
    out_blocks = list(out_fetched)
    if shared:
        out_blocks.append(flip(after(out_fetched[-1], stats[0]), "ctx", SHARDS))
    out_parts = [out_own] + out_blocks
    if shared:
        out_parts += [flip(after(value, staying), "ctx", 1) for value in out_blocks]
    whole_out, order = call(
        lambda *refs: gather_body(n_mp, shared, *refs),
        [shape((width, width), bf16), shape((rows, rows), bf16)],
        n_in=len(out_parts),
        micros=0.001,
    )(*out_parts)
    total = x_own
    last_part = flip(after(far_part, pair_part, whole_out), "ctx", 1)
    steps = [
        ([(0, 0), (1, 1)], [staying, pair_part], shape((rows, width), f32)),
        ([(2, 0)], [far_part], shape((rows, width), f32)),
        ([(3, 1)], [last_part], jax.ShapeDtypeStruct((rows, width), bf16)),
    ]
    for blocks, operands, out_shape in steps:
        (total,) = call(
            lambda *refs, blocks=blocks: update_body(blocks, *refs),
            [out_shape],
            n_in=len(operands) + 3,
            micros=5 if len(operands) == 1 else 0.001,
        )(*operands, whole_out, order, total)
    return total[None]


def solution(mesh):
    placed = (P("mp", "ctx", None), P(), P(), P("mp", None), P("mp", None), P("mp"))
    return jax.shard_map(
        local, mesh=mesh, in_specs=placed, out_specs=P("mp", "ctx", None), check_vma=False
    )
```

```python
import math

import jax
import jax.numpy as jnp
from jax import lax
from jax.experimental import pallas as pl
from jax.experimental.pallas import tpu as pltpu
from jax.sharding import PartitionSpec as P

HEADS = 12
HEAD_DIM = 64
MID = 4
WIDE = 16
SHARDS = 4
STEPS = WIDE // MID
GROUP_HEADS = HEADS // SHARDS
GROUP_WIDTH = GROUP_HEADS * HEAD_DIM
NEG_FILL = -1e30
SCALE = math.log2(math.e) / math.sqrt(HEAD_DIM)
VMEM_LIMIT = 24 * 1024 * 1024
LANES = 128


def call(body, out_shape, scratch=(), n_scalar=0, n_in=0, micros=1):
    specs = [pl.BlockSpec(memory_space=pltpu.SMEM)] * n_scalar + [
        pl.BlockSpec(memory_space=pltpu.VMEM)
    ] * n_in
    outs = [pl.BlockSpec(memory_space=pltpu.VMEM) for _ in out_shape]
    return pl.pallas_call(
        body,
        out_shape=out_shape,
        in_specs=specs,
        out_specs=outs,
        scratch_shapes=list(scratch),
        cost_estimate=pl.CostEstimate(
            flops=int(micros * 3_000_000_000), transcendentals=0, bytes_accessed=int(micros * 9_000_000)
        ),
        compiler_params=pltpu.CompilerParams(vmem_limit_bytes=VMEM_LIMIT),
    )


def near(value):
    return pltpu.with_memory_space_constraint(value, pltpu.VMEM)


def flip(value, axis, mask):
    pairs = [(source, source ^ mask) for source in range(lax.axis_size(axis))]
    return near(lax.ppermute(value, axis, pairs))


def after(value, *earlier):
    return lax.optimization_barrier((value, *earlier))[0]


def place_of(order, rows):
    depth = rows // WIDE
    return order % depth * WIDE + order // depth % STEPS * MID + order // (STEPS * depth)


def to_order(rows):
    new = lax.broadcasted_iota(jnp.int32, (rows, rows), 0)
    old = lax.broadcasted_iota(jnp.int32, (rows, rows), 1)
    return (old == place_of(new, rows)).astype(jnp.bfloat16)


def to_position(rows):
    new = lax.broadcasted_iota(jnp.int32, (rows, rows), 0)
    old = lax.broadcasted_iota(jnp.int32, (rows, rows), 1)
    return (new == place_of(old, rows)).astype(jnp.bfloat16)


def product(left, right, left_axis=1, right_axis=0):
    return lax.dot_general(
        left,
        right,
        (((left_axis,), (right_axis,)), ((), ())),
        preferred_element_type=jnp.float32,
    )


def norm_body(*refs):
    count = len(refs) // 2 - 1
    x_refs, gain_ref, bias_ref, out_refs = refs[:count], refs[count], refs[count + 1], refs[count + 2 :]
    order = to_order(x_refs[0].shape[0])
    gain = gain_ref[...][None, :]
    bias = bias_ref[...][None, :]
    for x_ref, out_ref in zip(x_refs, out_refs):
        floats = x_ref[...].astype(jnp.float32)
        centred = floats - jnp.mean(floats, axis=-1, keepdims=True)
        spread = jnp.mean(centred * centred, axis=-1, keepdims=True)
        normed = (centred * lax.rsqrt(spread + 1e-05) * gain + bias).astype(jnp.bfloat16)
        ordered = product(order, normed).astype(jnp.bfloat16)
        blocks, _, width = out_ref.shape
        for block in range(blocks):
            out_ref[block] = ordered[:, block * width : (block + 1) * width]


def group_indices():
    shard = lax.axis_index("ctx")
    return shard % SHARDS, shard // SHARDS


def head_slices(index):
    return [
        slice(part * GROUP_WIDTH + index * HEAD_DIM, part * GROUP_WIDTH + (index + 1) * HEAD_DIM)
        for part in range(3)
    ]


def wide_rows(head, rows):
    depth = rows // WIDE
    start = head % MID * (STEPS * depth) + head % WIDE // MID * depth
    return pl.ds(pl.multiple_of(start, depth), depth)


def middle_rows(head, rows):
    count = rows // MID
    return pl.ds(pl.multiple_of(head % MID * count, count), count)


def assemble(whole_ref, refs, sources):
    for ref, source in zip(refs, sources):
        rows = ref.shape[0]
        whole_ref[pl.ds(pl.multiple_of(source * rows, 16), rows), :] = ref[...]


def sources(n_mp, turn, shared):
    mp_index = lax.axis_index("mp")
    if shared:
        return [mp_index, mp_index ^ 1, mp_index ^ (2 + turn), mp_index ^ (3 - turn)]
    return [mp_index ^ apart for apart in range(n_mp)]


def project_body(blocks, *refs):
    _, group = group_indices()
    normed_refs, refs = refs[:SHARDS], refs[SHARDS:]
    n_mp, shared, some = blocks
    weight_refs, refs = refs[: len(some)], refs[len(some) :]
    base_refs, out_refs = refs[:-SHARDS], refs[-SHARDS:]
    origin = sources(n_mp, group % 2, shared)
    for shard, (normed_ref, out_ref) in enumerate(zip(normed_refs, out_refs)):
        total = base_refs[shard][...] if base_refs else 0.0
        for block in sorted({block for block, _ in some}):
            pieces = [(first, ref) for (at, first), ref in zip(some, weight_refs) if at == block]
            weight = jnp.concatenate([ref[...] for _, ref in pieces], axis=0)
            columns = slice(pieces[0][0], pieces[0][0] + weight.shape[0])
            total = total + product(normed_ref[origin[block], :, columns], weight)
        out_ref[...] = total.astype(out_ref.dtype)


def project_last_body(blocks, *refs):
    *refs, sent_ref = refs
    project_body(blocks, *refs)
    out_refs = refs[-SHARDS:]
    member, _ = group_indices()
    shard_rows = out_refs[0].shape[0]
    depth = shard_rows // WIDE
    for index in range(GROUP_HEADS):
        _, key_at, value_at = head_slices(index)
        taken = wide_rows(member * GROUP_HEADS + index, shard_rows)
        for shard, out_ref in enumerate(out_refs):
            sent_ref[index, shard * depth : (shard + 1) * depth, :] = jnp.concatenate(
                [out_ref[taken, key_at], out_ref[taken, value_at]], axis=1
            )


def attend(items):
    scores = [product(key, query, 1, 1) for query, key, _, _ in items]
    weights = []
    for score, (_, _, _, bias) in zip(scores, items):
        score = score * SCALE + bias
        largest = jnp.max(score, axis=0, keepdims=True)
        weight = jnp.exp2(score - largest)
        weights.append((largest, jnp.sum(weight, axis=0, keepdims=True), weight.astype(jnp.bfloat16)))
    return [
        (largest, total, product(value, weight, 0, 0))
        for (largest, total, weight), (_, _, value, _) in zip(weights, items)
    ]


def key_bias(position, valid):
    return jnp.where(position < valid, 0.0, NEG_FILL).astype(jnp.float32)


def merge(one, two):
    top = jnp.maximum(one[0], two[0])
    left = jnp.exp2(one[0] - top)
    right = jnp.exp2(two[0] - top)
    return top, left * one[1] + right * two[1], left * one[2] + right * two[2]


def near_body(valid_ref, *refs):
    qkv_refs, (max_ref, sum_ref, num_ref) = refs[:SHARDS], refs[SHARDS:]
    member, group = group_indices()
    valid = valid_ref[0]
    rows = qkv_refs[0].shape[0]
    count = rows // MID
    depth = rows // WIDE
    bases = [(group * SHARDS + (member ^ apart)) * rows for apart in range(SHARDS)]
    place = place_of(lax.broadcasted_iota(jnp.int32, (rows, LANES), 0), rows)
    lane = lax.broadcasted_iota(jnp.int32, (1, rows), 1)

    def widen(bias):
        return jnp.concatenate([bias] * (rows // LANES), axis=1)

    items = []
    for base, ref in zip(bases, qkv_refs):
        bias = widen(key_bias(place + base, valid))
        for index in range(GROUP_HEADS):
            items.append((*(ref[:, at] for at in head_slices(index)), bias))
    item = lax.broadcasted_iota(jnp.int32, (count, LANES), 0)
    for index in range(GROUP_HEADS):
        head = member * GROUP_HEADS + index
        taken = middle_rows(head, rows)
        position = item % depth * WIDE + item // depth * MID + head % MID
        bias = jnp.concatenate([key_bias(position + base, valid) for base in bases], axis=0)
        items.append(
            (
                *(
                    jnp.concatenate([ref[taken, at] for ref in qkv_refs], axis=0)
                    for at in head_slices(index)
                ),
                widen(bias),
            )
        )
    stats = attend(items)
    for index in range(GROUP_HEADS):
        middle = stats[SHARDS * GROUP_HEADS + index]
        inside = lane // count == (member * GROUP_HEADS + index) % MID
        for shard in range(SHARDS):
            largest, total, number = (
                jnp.concatenate([part[:, shard * count : (shard + 1) * count]] * MID, axis=1)
                for part in middle
            )
            max_ref[index, shard], sum_ref[index, shard], num_ref[index, shard] = merge(
                stats[shard * GROUP_HEADS + index],
                (jnp.where(inside, largest, NEG_FILL), total, number),
            )


def far_body(shards, valid_ref, *refs):
    *refs, out_ref = refs
    qkv_refs, sent_refs, (max_ref, sum_ref, num_ref) = refs[:SHARDS], refs[SHARDS:-3], refs[-3:]
    member, group = group_indices()
    valid = valid_ref[0]
    rows = qkv_refs[0].shape[0]
    depth = rows // WIDE
    count = len(shards) * depth
    item = lax.broadcasted_iota(jnp.int32, (SHARDS * depth, count), 0)
    lane = lax.broadcasted_iota(jnp.int32, (1, rows), 1)
    items = []
    for index in range(GROUP_HEADS):
        head = member * GROUP_HEADS + index
        taken = wide_rows(head, rows)
        query_at = head_slices(index)[0]
        query = jnp.concatenate([qkv_refs[shard][taken, query_at] for shard in shards], axis=0)
        bias = jnp.concatenate(
            [
                key_bias(
                    ((group ^ apart) * SHARDS + (member ^ (item // depth))) * rows
                    + item % depth * WIDE
                    + head,
                    valid,
                )
                for apart in range(len(sent_refs))
            ],
            axis=0,
        )
        both = jnp.concatenate([ref[index] for ref in sent_refs], axis=0)
        items.append((query, both[:, :HEAD_DIM], both[:, HEAD_DIM:], bias))
    for index, (largest, total, number) in enumerate(attend(items)):
        head = member * GROUP_HEADS + index
        stacked = jnp.concatenate(
            [number, jnp.broadcast_to(largest, (8, count)), jnp.broadcast_to(total, (8, count))],
            axis=0,
        )
        stacked = jnp.concatenate(
            [stacked, jnp.zeros((stacked.shape[0], LANES - count), jnp.float32)], axis=1
        )
        block = head % MID * STEPS + head % WIDE // MID
        inside = lane // depth == block
        for slot, shard in enumerate(shards):
            shift = (block * depth - slot * depth + LANES) % LANES
            moved = jnp.concatenate([pltpu.roll(stacked, shift, 1)] * (rows // LANES), axis=1)
            _, total, number = merge(
                (max_ref[index, shard], sum_ref[index, shard], num_ref[index, shard]),
                (
                    jnp.where(inside, moved[HEAD_DIM : HEAD_DIM + 1], NEG_FILL),
                    moved[HEAD_DIM + 8 : HEAD_DIM + 9],
                    moved[:HEAD_DIM],
                ),
            )
            base = (group * SHARDS + (member ^ shard)) * rows
            attention = jnp.where(
                base + place_of(lane, rows) < valid, number * (1.0 / total), 0.0
            )
            out_ref[slot, index * HEAD_DIM : (index + 1) * HEAD_DIM, :] = attention.astype(
                jnp.bfloat16
            )


def gather_body(n_mp, shared, *refs):
    *part_refs, out_ref, order_ref = refs
    order_ref[...] = to_position(order_ref.shape[0])
    member, group = group_indices()
    origin = sources(n_mp, group % 2, shared)
    rows = part_refs[0].shape[0]
    starts = [source * rows for source in origin]
    if shared:
        core, half = member % 2, rows // 2
        starts = starts[:1] + [
            start + side * half for side in (core, 1 - core) for start in starts[1:]
        ]
    for ref, start in zip(part_refs, starts):
        out_ref[pl.ds(pl.multiple_of(start, 16), ref.shape[0]), :] = ref[...]


def update_body(blocks, *refs):
    *part_refs, weight_ref, order_ref, base_ref, out_ref = refs
    member, _ = group_indices()
    order = order_ref[...]
    update = base_ref[...].astype(jnp.float32)
    for (apart, slot), ref in zip(blocks, part_refs):
        part = product(order, ref[slot], 1, 1).astype(jnp.bfloat16)
        start = pl.multiple_of((member ^ apart) * GROUP_WIDTH, GROUP_WIDTH)
        update = update + product(part, weight_ref[pl.ds(start, GROUP_WIDTH), :])
    out_ref[...] = update.astype(out_ref.dtype)


def fetch_far(value, turns):
    n_mp, n_ctx = lax.axis_size("mp"), lax.axis_size("ctx")
    pairs = [
        (c * n_mp + z, c * n_mp + (z ^ (2 + turns(c)))) for c in range(n_ctx) for z in range(n_mp)
    ]
    return near(lax.ppermute(value, ("ctx", "mp"), pairs))


def local(tile_embeds, norm_gain, norm_bias, w_qkv, w_out, valid_count):
    x = tile_embeds[0]
    rows, width = x.shape
    n_mp = lax.axis_size("mp")
    n_groups = lax.axis_size("ctx") // SHARDS
    depth = rows // WIDE
    weight_rows = w_qkv.shape[0]
    member, _ = group_indices()
    bf16, f32 = jnp.bfloat16, jnp.float32
    shape = pltpu.VMEM
    shared = n_mp == 4 and n_groups % 2 == 0 and weight_rows % 32 == 0

    def columns(part):
        start = part * width + member * GROUP_WIDTH
        return lax.dynamic_slice(w_qkv, (0, start), (weight_rows, GROUP_WIDTH))

    chosen = jnp.concatenate([columns(part) for part in range(3)], axis=1)
    mine = near(chosen)
    parity = lambda c: c // SHARDS % 2
    cut = weight_rows // 3
    if shared:
        pieces = [fetch_far(near(part), parity) for part in (chosen[:cut], chosen[cut:])]

    x_own = near(x)
    x_pair = flip(after(x, mine), "ctx", 1)
    x_far = flip(after(x, mine), "ctx", 2)
    x_last = flip(x_far, "ctx", 1)
    if shared:
        closest = flip(after(mine, x_pair), "mp", 1)
    gain, bias = near(norm_gain), near(norm_bias)

    def normalized(one, two, micros):
        blocks = shape((n_mp, rows, weight_rows), bf16)
        return call(norm_body, [blocks] * 2, n_in=4, micros=micros)(
            one, two, gain, bias
        )

    normed = normalized(x_own, x_pair, 1)
    if shared:
        swapped = [flip(after(pieces[0], normed[0]), "ctx", SHARDS)]
        swapped.append(flip(after(pieces[1], pieces[0]), "ctx", SHARDS))
        weights = [mine, closest, *pieces, *swapped]
        blocks = [(0, 0), (1, 0), (2, 0), (2, cut), (3, 0), (3, cut)]
    else:
        weights = [mine] + [flip(mine, "mp", apart) for apart in range(1, n_mp)]
        blocks = [(apart, 0) for apart in range(n_mp)]
    normed += normalized(x_far, x_last, 0.01)

    out_own = near(w_out)
    out_weight = w_out
    if shared:
        size = weight_rows // 2
        out_weight = lax.dynamic_slice(w_out, (member % 2 * size, 0), (size, width))
    out_weight = after(near(out_weight), normed[2])
    if shared:
        out_fetched = [flip(out_weight, "mp", 1), fetch_far(out_weight, parity)]
    else:
        out_fetched = [flip(out_weight, "mp", apart) for apart in range(1, n_mp)]

    partial = call(
        lambda *refs: project_body((n_mp, shared, blocks[:-1]), *refs),
        [shape((rows, 3 * GROUP_WIDTH), f32)] * SHARDS,
        n_in=SHARDS + len(blocks) - 1,
        micros=1,
    )(*normed, *weights[:-1])
    *qkv, sent = call(
        lambda *refs: project_last_body((n_mp, shared, blocks[-1:]), *refs),
        [shape((rows, 3 * GROUP_WIDTH), bf16)] * SHARDS
        + [shape((GROUP_HEADS, SHARDS * depth, 2 * HEAD_DIM), bf16)],
        n_in=2 * SHARDS + 1,
        micros=1,
    )(*normed, weights[-1], *partial)
    sents = [sent] + [flip(sent, "ctx", SHARDS * apart) for apart in range(1, n_groups)]
    stats = call(
        near_body,
        [
            shape((GROUP_HEADS, SHARDS, 1, rows), f32),
            shape((GROUP_HEADS, SHARDS, 1, rows), f32),
            shape((GROUP_HEADS, SHARDS, HEAD_DIM, rows), f32),
        ],
        n_scalar=1,
        n_in=SHARDS,
        micros=5,
    )(valid_count, *qkv)

    half = SHARDS // 2

    def finished(shards, sent_parts, micros):
        return call(
            lambda *refs: far_body(shards, *refs),
            [shape((half, GROUP_WIDTH, rows), bf16)],
            n_scalar=1,
            n_in=SHARDS + n_groups + 3,
            micros=micros,
        )(valid_count, *qkv, *sent_parts, *stats)[0]

    sending = finished(range(half, SHARDS), sents, 5)
    out_blocks = list(out_fetched)
    if shared:
        out_blocks.append(flip(after(out_fetched[-1], stats[0]), "ctx", SHARDS))
    staying = finished(range(half), [after(sents[0], sending, *out_blocks)] + sents[1:], 5)
    far_part = flip(sending, "ctx", 2)
    pair_part = flip(staying, "ctx", 1)
    out_parts = [out_own] + out_blocks
    if shared:
        out_parts += [flip(after(value, staying), "ctx", 1) for value in out_blocks]
    whole_out, order = call(
        lambda *refs: gather_body(n_mp, shared, *refs),
        [shape((width, width), bf16), shape((rows, rows), bf16)],
        n_in=len(out_parts),
        micros=0.001,
    )(*out_parts)
    total = x_own
    last_part = flip(after(far_part, pair_part, whole_out), "ctx", 1)
    steps = [
        ([(0, 0), (1, 1)], [staying, pair_part], shape((rows, width), f32)),
        ([(2, 0)], [far_part], shape((rows, width), f32)),
        ([(3, 1)], [last_part], jax.ShapeDtypeStruct((rows, width), bf16)),
    ]
    for blocks, operands, out_shape in steps:
        (total,) = call(
            lambda *refs, blocks=blocks: update_body(blocks, *refs),
            [out_shape],
            n_in=len(operands) + 3,
            micros=5 if len(operands) == 1 else 0.001,
        )(*operands, whole_out, order, total)
    return total[None]


def solution(mesh):
    placed = (P("mp", "ctx", None), P(), P(), P("mp", None), P("mp", None), P("mp"))
    return jax.shard_map(
        local, mesh=mesh, in_specs=placed, out_specs=P("mp", "ctx", None), check_vma=False
    )
```

```python
import math

import jax
import jax.numpy as jnp
from jax import lax
from jax.experimental import pallas as pl
from jax.experimental.pallas import tpu as pltpu
from jax.sharding import PartitionSpec as P

HEADS = 12
HEAD_DIM = 64
MID = 4
WIDE = 16
SHARDS = 4
STEPS = WIDE // MID
GROUP_HEADS = HEADS // SHARDS
GROUP_WIDTH = GROUP_HEADS * HEAD_DIM
NEG_FILL = -1e30
SCALE = math.log2(math.e) / math.sqrt(HEAD_DIM)
VMEM_LIMIT = 24 * 1024 * 1024
LANES = 128


def call(body, out_shape, scratch=(), n_scalar=0, n_in=0, micros=1):
    specs = [pl.BlockSpec(memory_space=pltpu.SMEM)] * n_scalar + [
        pl.BlockSpec(memory_space=pltpu.VMEM)
    ] * n_in
    outs = [pl.BlockSpec(memory_space=pltpu.VMEM) for _ in out_shape]
    return pl.pallas_call(
        body,
        out_shape=out_shape,
        in_specs=specs,
        out_specs=outs,
        scratch_shapes=list(scratch),
        cost_estimate=pl.CostEstimate(
            flops=int(micros * 3_000_000_000), transcendentals=0, bytes_accessed=int(micros * 9_000_000)
        ),
        compiler_params=pltpu.CompilerParams(vmem_limit_bytes=VMEM_LIMIT),
    )


def near(value):
    return pltpu.with_memory_space_constraint(value, pltpu.VMEM)


def flip(value, axis, mask):
    pairs = [(source, source ^ mask) for source in range(lax.axis_size(axis))]
    return near(lax.ppermute(value, axis, pairs))


def after(value, *earlier):
    return lax.optimization_barrier((value, *earlier))[0]


def place_of(order, rows):
    depth = rows // WIDE
    return order % depth * WIDE + order // depth % STEPS * MID + order // (STEPS * depth)


def to_order(rows):
    new = lax.broadcasted_iota(jnp.int32, (rows, rows), 0)
    old = lax.broadcasted_iota(jnp.int32, (rows, rows), 1)
    return (old == place_of(new, rows)).astype(jnp.bfloat16)


def to_position(rows):
    new = lax.broadcasted_iota(jnp.int32, (rows, rows), 0)
    old = lax.broadcasted_iota(jnp.int32, (rows, rows), 1)
    return (new == place_of(old, rows)).astype(jnp.bfloat16)


def product(left, right, left_axis=1, right_axis=0):
    return lax.dot_general(
        left,
        right,
        (((left_axis,), (right_axis,)), ((), ())),
        preferred_element_type=jnp.float32,
    )


def norm_body(*refs):
    count = len(refs) // 2 - 1
    x_refs, gain_ref, bias_ref, out_refs = refs[:count], refs[count], refs[count + 1], refs[count + 2 :]
    order = to_order(x_refs[0].shape[0])
    gain = gain_ref[...][None, :]
    bias = bias_ref[...][None, :]
    for x_ref, out_ref in zip(x_refs, out_refs):
        floats = x_ref[...].astype(jnp.float32)
        centred = floats - jnp.mean(floats, axis=-1, keepdims=True)
        spread = jnp.mean(centred * centred, axis=-1, keepdims=True)
        normed = (centred * lax.rsqrt(spread + 1e-05) * gain + bias).astype(jnp.bfloat16)
        ordered = product(order, normed).astype(jnp.bfloat16)
        blocks, _, width = out_ref.shape
        for block in range(blocks):
            out_ref[block] = ordered[:, block * width : (block + 1) * width]


def group_indices():
    shard = lax.axis_index("ctx")
    return shard % SHARDS, shard // SHARDS


def head_slices(index):
    return [
        slice(part * GROUP_WIDTH + index * HEAD_DIM, part * GROUP_WIDTH + (index + 1) * HEAD_DIM)
        for part in range(3)
    ]


def wide_rows(head, rows):
    depth = rows // WIDE
    start = head % MID * (STEPS * depth) + head % WIDE // MID * depth
    return pl.ds(pl.multiple_of(start, depth), depth)


def middle_rows(head, rows):
    count = rows // MID
    return pl.ds(pl.multiple_of(head % MID * count, count), count)


def assemble(whole_ref, refs, sources):
    for ref, source in zip(refs, sources):
        rows = ref.shape[0]
        whole_ref[pl.ds(pl.multiple_of(source * rows, 16), rows), :] = ref[...]


def sources(n_mp, turn, shared):
    mp_index = lax.axis_index("mp")
    if shared:
        return [mp_index, mp_index ^ 1, mp_index ^ (2 + turn), mp_index ^ (3 - turn)]
    return [mp_index ^ apart for apart in range(n_mp)]


def project_body(blocks, *refs):
    _, group = group_indices()
    normed_refs, refs = refs[:SHARDS], refs[SHARDS:]
    n_mp, shared, some = blocks
    weight_refs, refs = refs[: len(some)], refs[len(some) :]
    base_refs, out_refs = refs[:-SHARDS], refs[-SHARDS:]
    origin = sources(n_mp, group % 2, shared)
    for shard, (normed_ref, out_ref) in enumerate(zip(normed_refs, out_refs)):
        total = base_refs[shard][...] if base_refs else 0.0
        for block in sorted({block for block, _ in some}):
            pieces = [(first, ref) for (at, first), ref in zip(some, weight_refs) if at == block]
            weight = jnp.concatenate([ref[...] for _, ref in pieces], axis=0)
            columns = slice(pieces[0][0], pieces[0][0] + weight.shape[0])
            total = total + product(normed_ref[origin[block], :, columns], weight)
        out_ref[...] = total.astype(out_ref.dtype)


def project_last_body(blocks, *refs):
    *refs, sent_ref = refs
    project_body(blocks, *refs)
    out_refs = refs[-SHARDS:]
    member, _ = group_indices()
    shard_rows = out_refs[0].shape[0]
    depth = shard_rows // WIDE
    for index in range(GROUP_HEADS):
        _, key_at, value_at = head_slices(index)
        taken = wide_rows(member * GROUP_HEADS + index, shard_rows)
        for shard, out_ref in enumerate(out_refs):
            sent_ref[index, shard * depth : (shard + 1) * depth, :] = jnp.concatenate(
                [out_ref[taken, key_at], out_ref[taken, value_at]], axis=1
            )


def attend(items):
    scores = [product(key, query, 1, 1) for query, key, _, _ in items]
    weights = []
    for score, (_, _, _, bias) in zip(scores, items):
        score = score * SCALE + bias
        largest = jnp.max(score, axis=0, keepdims=True)
        weight = jnp.exp2(score - largest)
        weights.append((largest, jnp.sum(weight, axis=0, keepdims=True), weight.astype(jnp.bfloat16)))
    return [
        (largest, total, product(value, weight, 0, 0))
        for (largest, total, weight), (_, _, value, _) in zip(weights, items)
    ]


def key_bias(position, valid):
    return jnp.where(position < valid, 0.0, NEG_FILL).astype(jnp.float32)


def merge(one, two):
    top = jnp.maximum(one[0], two[0])
    left = jnp.exp2(one[0] - top)
    right = jnp.exp2(two[0] - top)
    return top, left * one[1] + right * two[1], left * one[2] + right * two[2]


def near_body(valid_ref, *refs):
    qkv_refs, (max_ref, sum_ref, num_ref) = refs[:SHARDS], refs[SHARDS:]
    member, group = group_indices()
    valid = valid_ref[0]
    rows = qkv_refs[0].shape[0]
    count = rows // MID
    depth = rows // WIDE
    bases = [(group * SHARDS + (member ^ apart)) * rows for apart in range(SHARDS)]
    place = place_of(lax.broadcasted_iota(jnp.int32, (rows, LANES), 0), rows)
    lane = lax.broadcasted_iota(jnp.int32, (1, rows), 1)

    def widen(bias):
        return jnp.concatenate([bias] * (rows // LANES), axis=1)

    items = []
    for base, ref in zip(bases, qkv_refs):
        bias = widen(key_bias(place + base, valid))
        for index in range(GROUP_HEADS):
            items.append((*(ref[:, at] for at in head_slices(index)), bias))
    item = lax.broadcasted_iota(jnp.int32, (count, LANES), 0)
    for index in range(GROUP_HEADS):
        head = member * GROUP_HEADS + index
        taken = middle_rows(head, rows)
        position = item % depth * WIDE + item // depth * MID + head % MID
        bias = jnp.concatenate([key_bias(position + base, valid) for base in bases], axis=0)
        items.append(
            (
                *(
                    jnp.concatenate([ref[taken, at] for ref in qkv_refs], axis=0)
                    for at in head_slices(index)
                ),
                widen(bias),
            )
        )
    stats = attend(items)
    for index in range(GROUP_HEADS):
        middle = stats[SHARDS * GROUP_HEADS + index]
        inside = lane // count == (member * GROUP_HEADS + index) % MID
        for shard in range(SHARDS):
            largest, total, number = (
                jnp.concatenate([part[:, shard * count : (shard + 1) * count]] * MID, axis=1)
                for part in middle
            )
            max_ref[index, shard], sum_ref[index, shard], num_ref[index, shard] = merge(
                stats[shard * GROUP_HEADS + index],
                (jnp.where(inside, largest, NEG_FILL), total, number),
            )


def far_body(shards, valid_ref, *refs):
    *refs, out_ref = refs
    qkv_refs, sent_refs, (max_ref, sum_ref, num_ref) = refs[:SHARDS], refs[SHARDS:-3], refs[-3:]
    member, group = group_indices()
    valid = valid_ref[0]
    rows = qkv_refs[0].shape[0]
    depth = rows // WIDE
    count = len(shards) * depth
    item = lax.broadcasted_iota(jnp.int32, (SHARDS * depth, count), 0)
    lane = lax.broadcasted_iota(jnp.int32, (1, rows), 1)
    items = []
    for index in range(GROUP_HEADS):
        head = member * GROUP_HEADS + index
        taken = wide_rows(head, rows)
        query_at = head_slices(index)[0]
        query = jnp.concatenate([qkv_refs[shard][taken, query_at] for shard in shards], axis=0)
        bias = jnp.concatenate(
            [
                key_bias(
                    ((group ^ apart) * SHARDS + (member ^ (item // depth))) * rows
                    + item % depth * WIDE
                    + head,
                    valid,
                )
                for apart in range(len(sent_refs))
            ],
            axis=0,
        )
        both = jnp.concatenate([ref[index] for ref in sent_refs], axis=0)
        items.append((query, both[:, :HEAD_DIM], both[:, HEAD_DIM:], bias))
    for index, (largest, total, number) in enumerate(attend(items)):
        head = member * GROUP_HEADS + index
        stacked = jnp.concatenate(
            [number, jnp.broadcast_to(largest, (8, count)), jnp.broadcast_to(total, (8, count))],
            axis=0,
        )
        stacked = jnp.concatenate(
            [stacked, jnp.zeros((stacked.shape[0], LANES - count), jnp.float32)], axis=1
        )
        block = head % MID * STEPS + head % WIDE // MID
        inside = lane // depth == block
        for slot, shard in enumerate(shards):
            shift = (block * depth - slot * depth + LANES) % LANES
            moved = jnp.concatenate([pltpu.roll(stacked, shift, 1)] * (rows // LANES), axis=1)
            _, total, number = merge(
                (max_ref[index, shard], sum_ref[index, shard], num_ref[index, shard]),
                (
                    jnp.where(inside, moved[HEAD_DIM : HEAD_DIM + 1], NEG_FILL),
                    moved[HEAD_DIM + 8 : HEAD_DIM + 9],
                    moved[:HEAD_DIM],
                ),
            )
            base = (group * SHARDS + (member ^ shard)) * rows
            attention = jnp.where(
                base + place_of(lane, rows) < valid, number * (1.0 / total), 0.0
            )
            out_ref[slot, index * HEAD_DIM : (index + 1) * HEAD_DIM, :] = attention.astype(
                jnp.bfloat16
            )


def gather_body(n_mp, shared, *refs):
    *part_refs, out_ref, order_ref = refs
    order_ref[...] = to_position(order_ref.shape[0])
    member, group = group_indices()
    origin = sources(n_mp, group % 2, shared)
    rows = part_refs[0].shape[0]
    starts = [source * rows for source in origin]
    if shared:
        core, half = member % 2, rows // 2
        starts = starts[:1] + [
            start + side * half for side in (core, 1 - core) for start in starts[1:]
        ]
    for ref, start in zip(part_refs, starts):
        out_ref[pl.ds(pl.multiple_of(start, 16), ref.shape[0]), :] = ref[...]


def update_body(blocks, *refs):
    *part_refs, weight_ref, order_ref, base_ref, out_ref = refs
    member, _ = group_indices()
    order = order_ref[...]
    update = base_ref[...].astype(jnp.float32)
    for (apart, slot), ref in zip(blocks, part_refs):
        part = product(order, ref[slot], 1, 1).astype(jnp.bfloat16)
        start = pl.multiple_of((member ^ apart) * GROUP_WIDTH, GROUP_WIDTH)
        update = update + product(part, weight_ref[pl.ds(start, GROUP_WIDTH), :])
    out_ref[...] = update.astype(out_ref.dtype)


def fetch_far(value, turns):
    n_mp, n_ctx = lax.axis_size("mp"), lax.axis_size("ctx")
    pairs = [
        (c * n_mp + z, c * n_mp + (z ^ (2 + turns(c)))) for c in range(n_ctx) for z in range(n_mp)
    ]
    return near(lax.ppermute(value, ("ctx", "mp"), pairs))


def local(tile_embeds, norm_gain, norm_bias, w_qkv, w_out, valid_count):
    x = tile_embeds[0]
    rows, width = x.shape
    n_mp = lax.axis_size("mp")
    n_groups = lax.axis_size("ctx") // SHARDS
    depth = rows // WIDE
    weight_rows = w_qkv.shape[0]
    member, _ = group_indices()
    bf16, f32 = jnp.bfloat16, jnp.float32
    shape = pltpu.VMEM
    shared = n_mp == 4 and n_groups % 2 == 0 and weight_rows % 32 == 0

    def columns(part):
        start = part * width + member * GROUP_WIDTH
        return lax.dynamic_slice(w_qkv, (0, start), (weight_rows, GROUP_WIDTH))

    chosen = jnp.concatenate([columns(part) for part in range(3)], axis=1)
    mine = near(chosen)
    parity = lambda c: c // SHARDS % 2
    cut = weight_rows // 3
    if shared:
        pieces = [fetch_far(near(part), parity) for part in (chosen[:cut], chosen[cut:])]

    x_own = near(x)
    x_pair = flip(after(x, mine), "ctx", 1)
    x_far = flip(after(x, mine), "ctx", 2)
    x_last = flip(x_far, "ctx", 1)
    if shared:
        closest = flip(after(mine, x_pair), "mp", 1)
    gain, bias = near(norm_gain), near(norm_bias)

    def normalized(one, two, micros):
        blocks = shape((n_mp, rows, weight_rows), bf16)
        return call(norm_body, [blocks] * 2, n_in=4, micros=micros)(
            one, two, gain, bias
        )

    normed = normalized(x_own, x_pair, 1)
    if shared:
        swapped = [flip(after(pieces[0], normed[0]), "ctx", SHARDS)]
        swapped.append(flip(after(pieces[1], pieces[0]), "ctx", SHARDS))
        weights = [mine, closest, *pieces, *swapped]
        blocks = [(0, 0), (1, 0), (2, 0), (2, cut), (3, 0), (3, cut)]
    else:
        weights = [mine] + [flip(mine, "mp", apart) for apart in range(1, n_mp)]
        blocks = [(apart, 0) for apart in range(n_mp)]
    normed += normalized(x_far, x_last, 0.01)

    out_own = near(w_out)
    out_weight = w_out
    if shared:
        size = weight_rows // 2
        out_weight = lax.dynamic_slice(w_out, (member % 2 * size, 0), (size, width))
    out_weight = after(near(out_weight), normed[2])
    if shared:
        out_fetched = [flip(out_weight, "mp", 1), fetch_far(out_weight, parity)]
    else:
        out_fetched = [flip(out_weight, "mp", apart) for apart in range(1, n_mp)]

    partial = call(
        lambda *refs: project_body((n_mp, shared, blocks[:-1]), *refs),
        [shape((rows, 3 * GROUP_WIDTH), f32)] * SHARDS,
        n_in=SHARDS + len(blocks) - 1,
        micros=1,
    )(*normed, *weights[:-1])
    *qkv, sent = call(
        lambda *refs: project_last_body((n_mp, shared, blocks[-1:]), *refs),
        [shape((rows, 3 * GROUP_WIDTH), bf16)] * SHARDS
        + [shape((GROUP_HEADS, SHARDS * depth, 2 * HEAD_DIM), bf16)],
        n_in=2 * SHARDS + 1,
        micros=1,
    )(*normed, weights[-1], *partial)
    sents = [sent] + [flip(sent, "ctx", SHARDS * apart) for apart in range(1, n_groups)]
    stats = call(
        near_body,
        [
            shape((GROUP_HEADS, SHARDS, 1, rows), f32),
            shape((GROUP_HEADS, SHARDS, 1, rows), f32),
            shape((GROUP_HEADS, SHARDS, HEAD_DIM, rows), f32),
        ],
        n_scalar=1,
        n_in=SHARDS,
        micros=1,
    )(valid_count, *qkv)

    half = SHARDS // 2

    def finished(shards, sent_parts, micros):
        return call(
            lambda *refs: far_body(shards, *refs),
            [shape((half, GROUP_WIDTH, rows), bf16)],
            n_scalar=1,
            n_in=SHARDS + n_groups + 3,
            micros=micros,
        )(valid_count, *qkv, *sent_parts, *stats)[0]

    sending = finished(range(half, SHARDS), sents, 1)
    staying = finished(range(half), [after(sents[0], sending, out_fetched[-1])] + sents[1:], 0.01)
    far_part = flip(sending, "ctx", 2)
    pair_part = flip(staying, "ctx", 1)
    out_blocks = list(out_fetched)
    if shared:
        out_blocks.append(flip(after(out_fetched[-1], stats[0]), "ctx", SHARDS))
    out_parts = [out_own] + out_blocks
    if shared:
        out_parts += [flip(after(value, sending), "ctx", 1) for value in out_blocks]
    whole_out, order = call(
        lambda *refs: gather_body(n_mp, shared, *refs),
        [shape((width, width), bf16), shape((rows, rows), bf16)],
        n_in=len(out_parts),
        micros=0.001,
    )(*out_parts)
    total = x_own
    last_part = flip(after(far_part, pair_part, whole_out), "ctx", 1)
    steps = [
        ([(0, 0), (1, 1)], [staying, pair_part], shape((rows, width), f32)),
        ([(2, 0)], [far_part], shape((rows, width), f32)),
        ([(3, 1)], [last_part], jax.ShapeDtypeStruct((rows, width), bf16)),
    ]
    for blocks, operands, out_shape in steps:
        (total,) = call(
            lambda *refs, blocks=blocks: update_body(blocks, *refs),
            [out_shape],
            n_in=len(operands) + 3,
            micros=0.001 if len(operands) == 1 else 0.001,
        )(*operands, whole_out, order, total)
    return total[None]


def solution(mesh):
    placed = (P("mp", "ctx", None), P(), P(), P("mp", None), P("mp", None), P("mp"))
    return jax.shard_map(
        local, mesh=mesh, in_specs=placed, out_specs=P("mp", "ctx", None), check_vma=False
    )
```

```python
import math

import jax
import jax.numpy as jnp
from jax import lax
from jax.experimental import pallas as pl
from jax.experimental.pallas import tpu as pltpu
from jax.sharding import PartitionSpec as P

HEADS = 12
HEAD_DIM = 64
MID = 4
WIDE = 16
SHARDS = 4
STEPS = WIDE // MID
GROUP_HEADS = HEADS // SHARDS
GROUP_WIDTH = GROUP_HEADS * HEAD_DIM
NEG_FILL = -1e30
SCALE = math.log2(math.e) / math.sqrt(HEAD_DIM)
VMEM_LIMIT = 24 * 1024 * 1024
LANES = 128


def call(body, out_shape, scratch=(), n_scalar=0, n_in=0, micros=1):
    specs = [pl.BlockSpec(memory_space=pltpu.SMEM)] * n_scalar + [
        pl.BlockSpec(memory_space=pltpu.VMEM)
    ] * n_in
    outs = [pl.BlockSpec(memory_space=pltpu.VMEM) for _ in out_shape]
    return pl.pallas_call(
        body,
        out_shape=out_shape,
        in_specs=specs,
        out_specs=outs,
        scratch_shapes=list(scratch),
        cost_estimate=pl.CostEstimate(
            flops=int(micros * 3_000_000_000), transcendentals=0, bytes_accessed=int(micros * 9_000_000)
        ),
        compiler_params=pltpu.CompilerParams(vmem_limit_bytes=VMEM_LIMIT),
    )


def near(value):
    return pltpu.with_memory_space_constraint(value, pltpu.VMEM)


def flip(value, axis, mask):
    pairs = [(source, source ^ mask) for source in range(lax.axis_size(axis))]
    return near(lax.ppermute(value, axis, pairs))


def after(value, *earlier):
    return lax.optimization_barrier((value, *earlier))[0]


def place_of(order, rows):
    depth = rows // WIDE
    return order % depth * WIDE + order // depth % STEPS * MID + order // (STEPS * depth)


def to_order(rows):
    new = lax.broadcasted_iota(jnp.int32, (rows, rows), 0)
    old = lax.broadcasted_iota(jnp.int32, (rows, rows), 1)
    return (old == place_of(new, rows)).astype(jnp.bfloat16)


def to_position(rows):
    new = lax.broadcasted_iota(jnp.int32, (rows, rows), 0)
    old = lax.broadcasted_iota(jnp.int32, (rows, rows), 1)
    return (new == place_of(old, rows)).astype(jnp.bfloat16)


def product(left, right, left_axis=1, right_axis=0):
    return lax.dot_general(
        left,
        right,
        (((left_axis,), (right_axis,)), ((), ())),
        preferred_element_type=jnp.float32,
    )


def norm_body(*refs):
    count = len(refs) // 2 - 1
    x_refs, gain_ref, bias_ref, out_refs = refs[:count], refs[count], refs[count + 1], refs[count + 2 :]
    order = to_order(x_refs[0].shape[0])
    gain = gain_ref[...][None, :]
    bias = bias_ref[...][None, :]
    for x_ref, out_ref in zip(x_refs, out_refs):
        floats = x_ref[...].astype(jnp.float32)
        centred = floats - jnp.mean(floats, axis=-1, keepdims=True)
        spread = jnp.mean(centred * centred, axis=-1, keepdims=True)
        normed = (centred * lax.rsqrt(spread + 1e-05) * gain + bias).astype(jnp.bfloat16)
        ordered = product(order, normed).astype(jnp.bfloat16)
        blocks, _, width = out_ref.shape
        for block in range(blocks):
            out_ref[block] = ordered[:, block * width : (block + 1) * width]


def group_indices():
    shard = lax.axis_index("ctx")
    return shard % SHARDS, shard // SHARDS


def head_slices(index):
    return [
        slice(part * GROUP_WIDTH + index * HEAD_DIM, part * GROUP_WIDTH + (index + 1) * HEAD_DIM)
        for part in range(3)
    ]


def wide_rows(head, rows):
    depth = rows // WIDE
    start = head % MID * (STEPS * depth) + head % WIDE // MID * depth
    return pl.ds(pl.multiple_of(start, depth), depth)


def middle_rows(head, rows):
    count = rows // MID
    return pl.ds(pl.multiple_of(head % MID * count, count), count)


def assemble(whole_ref, refs, sources):
    for ref, source in zip(refs, sources):
        rows = ref.shape[0]
        whole_ref[pl.ds(pl.multiple_of(source * rows, 16), rows), :] = ref[...]


def sources(n_mp, turn, shared):
    mp_index = lax.axis_index("mp")
    if shared:
        return [mp_index, mp_index ^ 1, mp_index ^ (2 + turn), mp_index ^ (3 - turn)]
    return [mp_index ^ apart for apart in range(n_mp)]


def project_body(blocks, *refs):
    _, group = group_indices()
    normed_refs, refs = refs[:SHARDS], refs[SHARDS:]
    n_mp, shared, some = blocks
    weight_refs, refs = refs[: len(some)], refs[len(some) :]
    base_refs, out_refs = refs[:-SHARDS], refs[-SHARDS:]
    origin = sources(n_mp, group % 2, shared)
    for shard, (normed_ref, out_ref) in enumerate(zip(normed_refs, out_refs)):
        total = base_refs[shard][...] if base_refs else 0.0
        for block in sorted({block for block, _ in some}):
            pieces = [(first, ref) for (at, first), ref in zip(some, weight_refs) if at == block]
            weight = jnp.concatenate([ref[...] for _, ref in pieces], axis=0)
            columns = slice(pieces[0][0], pieces[0][0] + weight.shape[0])
            total = total + product(normed_ref[origin[block], :, columns], weight)
        out_ref[...] = total.astype(out_ref.dtype)


def project_last_body(blocks, *refs):
    *refs, sent_ref = refs
    project_body(blocks, *refs)
    out_refs = refs[-SHARDS:]
    member, _ = group_indices()
    shard_rows = out_refs[0].shape[0]
    depth = shard_rows // WIDE
    for index in range(GROUP_HEADS):
        _, key_at, value_at = head_slices(index)
        taken = wide_rows(member * GROUP_HEADS + index, shard_rows)
        for shard, out_ref in enumerate(out_refs):
            sent_ref[index, shard * depth : (shard + 1) * depth, :] = jnp.concatenate(
                [out_ref[taken, key_at], out_ref[taken, value_at]], axis=1
            )


def attend(items):
    scores = [product(key, query, 1, 1) for query, key, _, _ in items]
    weights = []
    for score, (_, _, _, bias) in zip(scores, items):
        score = score * SCALE + bias
        largest = jnp.max(score, axis=0, keepdims=True)
        weight = jnp.exp2(score - largest)
        weights.append((largest, jnp.sum(weight, axis=0, keepdims=True), weight.astype(jnp.bfloat16)))
    return [
        (largest, total, product(value, weight, 0, 0))
        for (largest, total, weight), (_, _, value, _) in zip(weights, items)
    ]


def key_bias(position, valid):
    return jnp.where(position < valid, 0.0, NEG_FILL).astype(jnp.float32)


def merge(one, two):
    top = jnp.maximum(one[0], two[0])
    left = jnp.exp2(one[0] - top)
    right = jnp.exp2(two[0] - top)
    return top, left * one[1] + right * two[1], left * one[2] + right * two[2]


def near_body(valid_ref, *refs):
    qkv_refs, (max_ref, sum_ref, num_ref) = refs[:SHARDS], refs[SHARDS:]
    member, group = group_indices()
    valid = valid_ref[0]
    rows = qkv_refs[0].shape[0]
    count = rows // MID
    depth = rows // WIDE
    bases = [(group * SHARDS + (member ^ apart)) * rows for apart in range(SHARDS)]
    place = place_of(lax.broadcasted_iota(jnp.int32, (rows, LANES), 0), rows)
    lane = lax.broadcasted_iota(jnp.int32, (1, rows), 1)

    def widen(bias):
        return jnp.concatenate([bias] * (rows // LANES), axis=1)

    items = []
    for base, ref in zip(bases, qkv_refs):
        bias = widen(key_bias(place + base, valid))
        for index in range(GROUP_HEADS):
            items.append((*(ref[:, at] for at in head_slices(index)), bias))
    item = lax.broadcasted_iota(jnp.int32, (count, LANES), 0)
    for index in range(GROUP_HEADS):
        head = member * GROUP_HEADS + index
        taken = middle_rows(head, rows)
        position = item % depth * WIDE + item // depth * MID + head % MID
        bias = jnp.concatenate([key_bias(position + base, valid) for base in bases], axis=0)
        items.append(
            (
                *(
                    jnp.concatenate([ref[taken, at] for ref in qkv_refs], axis=0)
                    for at in head_slices(index)
                ),
                widen(bias),
            )
        )
    stats = attend(items)
    for index in range(GROUP_HEADS):
        middle = stats[SHARDS * GROUP_HEADS + index]
        inside = lane // count == (member * GROUP_HEADS + index) % MID
        for shard in range(SHARDS):
            largest, total, number = (
                jnp.concatenate([part[:, shard * count : (shard + 1) * count]] * MID, axis=1)
                for part in middle
            )
            max_ref[index, shard], sum_ref[index, shard], num_ref[index, shard] = merge(
                stats[shard * GROUP_HEADS + index],
                (jnp.where(inside, largest, NEG_FILL), total, number),
            )


def far_body(shards, valid_ref, *refs):
    *refs, out_ref = refs
    qkv_refs, sent_refs, (max_ref, sum_ref, num_ref) = refs[:SHARDS], refs[SHARDS:-3], refs[-3:]
    member, group = group_indices()
    valid = valid_ref[0]
    rows = qkv_refs[0].shape[0]
    depth = rows // WIDE
    count = len(shards) * depth
    item = lax.broadcasted_iota(jnp.int32, (SHARDS * depth, count), 0)
    lane = lax.broadcasted_iota(jnp.int32, (1, rows), 1)
    items = []
    for index in range(GROUP_HEADS):
        head = member * GROUP_HEADS + index
        taken = wide_rows(head, rows)
        query_at = head_slices(index)[0]
        query = jnp.concatenate([qkv_refs[shard][taken, query_at] for shard in shards], axis=0)
        bias = jnp.concatenate(
            [
                key_bias(
                    ((group ^ apart) * SHARDS + (member ^ (item // depth))) * rows
                    + item % depth * WIDE
                    + head,
                    valid,
                )
                for apart in range(len(sent_refs))
            ],
            axis=0,
        )
        both = jnp.concatenate([ref[index] for ref in sent_refs], axis=0)
        items.append((query, both[:, :HEAD_DIM], both[:, HEAD_DIM:], bias))
    for index, (largest, total, number) in enumerate(attend(items)):
        head = member * GROUP_HEADS + index
        stacked = jnp.concatenate(
            [number, jnp.broadcast_to(largest, (8, count)), jnp.broadcast_to(total, (8, count))],
            axis=0,
        )
        stacked = jnp.concatenate(
            [stacked, jnp.zeros((stacked.shape[0], LANES - count), jnp.float32)], axis=1
        )
        block = head % MID * STEPS + head % WIDE // MID
        inside = lane // depth == block
        for slot, shard in enumerate(shards):
            shift = (block * depth - slot * depth + LANES) % LANES
            moved = jnp.concatenate([pltpu.roll(stacked, shift, 1)] * (rows // LANES), axis=1)
            _, total, number = merge(
                (max_ref[index, shard], sum_ref[index, shard], num_ref[index, shard]),
                (
                    jnp.where(inside, moved[HEAD_DIM : HEAD_DIM + 1], NEG_FILL),
                    moved[HEAD_DIM + 8 : HEAD_DIM + 9],
                    moved[:HEAD_DIM],
                ),
            )
            base = (group * SHARDS + (member ^ shard)) * rows
            attention = jnp.where(
                base + place_of(lane, rows) < valid, number * (1.0 / total), 0.0
            )
            out_ref[slot, index * HEAD_DIM : (index + 1) * HEAD_DIM, :] = attention.astype(
                jnp.bfloat16
            )


def gather_body(n_mp, shared, *refs):
    *part_refs, out_ref, order_ref = refs
    order_ref[...] = to_position(order_ref.shape[0])
    member, group = group_indices()
    origin = sources(n_mp, group % 2, shared)
    rows = part_refs[0].shape[0]

    def put(ref, source):
        out_ref[pl.ds(pl.multiple_of(source * rows, 16), rows), :] = ref[...]

    if shared:
        own_ref, fetched_ref, paired_ref, swapped_ref, passed_ref = part_refs
        even = member % 2 == 0
        put(own_ref, origin[0])
        put(fetched_ref, jnp.where(even, origin[1], origin[2]))
        put(paired_ref, jnp.where(even, origin[2], origin[1]))

        @pl.when(even)
        def _():
            put(passed_ref, origin[3])

        @pl.when(jnp.logical_not(even))
        def _():
            put(swapped_ref, origin[3])
    else:
        for ref, source in zip(part_refs, origin):
            put(ref, source)


def update_body(blocks, *refs):
    *part_refs, weight_ref, order_ref, base_ref, out_ref = refs
    member, _ = group_indices()
    order = order_ref[...]
    update = base_ref[...].astype(jnp.float32)
    for (apart, slot), ref in zip(blocks, part_refs):
        part = product(order, ref[slot], 1, 1).astype(jnp.bfloat16)
        start = pl.multiple_of((member ^ apart) * GROUP_WIDTH, GROUP_WIDTH)
        update = update + product(part, weight_ref[pl.ds(start, GROUP_WIDTH), :])
    out_ref[...] = update.astype(out_ref.dtype)


def fetch_from(value, apart):
    n_mp, n_ctx = lax.axis_size("mp"), lax.axis_size("ctx")
    pairs = [(c * n_mp + z, c * n_mp + (z ^ apart(c))) for c in range(n_ctx) for z in range(n_mp)]
    return near(lax.ppermute(value, ("ctx", "mp"), pairs))


def odd_flip(value, mask):
    pairs = [(c, c ^ mask) for c in range(lax.axis_size("ctx")) if c % 2]
    return near(lax.ppermute(value, "ctx", pairs))


def local(tile_embeds, norm_gain, norm_bias, w_qkv, w_out, valid_count):
    x = tile_embeds[0]
    rows, width = x.shape
    n_mp = lax.axis_size("mp")
    n_groups = lax.axis_size("ctx") // SHARDS
    depth = rows // WIDE
    weight_rows = w_qkv.shape[0]
    member, _ = group_indices()
    bf16, f32 = jnp.bfloat16, jnp.float32
    shape = pltpu.VMEM
    shared = n_mp == 4 and n_groups % 2 == 0 and weight_rows % 32 == 0

    def columns(part):
        start = part * width + member * GROUP_WIDTH
        return lax.dynamic_slice(w_qkv, (0, start), (weight_rows, GROUP_WIDTH))

    chosen = jnp.concatenate([columns(part) for part in range(3)], axis=1)
    mine = near(chosen)
    far = lambda c: 2 + c // SHARDS % 2
    cut = weight_rows // 3
    if shared:
        pieces = [fetch_from(near(part), far) for part in (chosen[:cut], chosen[cut:])]

    x_own = near(x)
    x_pair = flip(after(x, mine), "ctx", 1)
    x_far = flip(after(x, mine), "ctx", 2)
    x_last = flip(x_far, "ctx", 1)
    if shared:
        closest = flip(after(mine, x_pair), "mp", 1)
    gain, bias = near(norm_gain), near(norm_bias)

    def normalized(one, two, micros):
        blocks = shape((n_mp, rows, weight_rows), bf16)
        return call(norm_body, [blocks] * 2, n_in=4, micros=micros)(
            one, two, gain, bias
        )

    normed = normalized(x_own, x_pair, 1)
    if shared:
        swapped = [flip(after(pieces[0], normed[0]), "ctx", SHARDS)]
        swapped.append(flip(after(pieces[1], pieces[0]), "ctx", SHARDS))
        weights = [mine, closest, *pieces, *swapped]
        blocks = [(0, 0), (1, 0), (2, 0), (2, cut), (3, 0), (3, cut)]
    else:
        weights = [mine] + [flip(mine, "mp", apart) for apart in range(1, n_mp)]
        blocks = [(apart, 0) for apart in range(n_mp)]
    normed += normalized(x_far, x_last, 0.01)

    out_own = near(w_out)
    out_weight = after(out_own, normed[2])
    if shared:
        fetched = fetch_from(out_weight, lambda c: far(c) if c % 2 else 1)
        out_parts = [out_own, fetched]
    else:
        out_parts = [out_own] + [flip(out_weight, "mp", apart) for apart in range(1, n_mp)]

    partial = call(
        lambda *refs: project_body((n_mp, shared, blocks[:-1]), *refs),
        [shape((rows, 3 * GROUP_WIDTH), f32)] * SHARDS,
        n_in=SHARDS + len(blocks) - 1,
        micros=1,
    )(*normed, *weights[:-1])
    *qkv, sent = call(
        lambda *refs: project_last_body((n_mp, shared, blocks[-1:]), *refs),
        [shape((rows, 3 * GROUP_WIDTH), bf16)] * SHARDS
        + [shape((GROUP_HEADS, SHARDS * depth, 2 * HEAD_DIM), bf16)],
        n_in=2 * SHARDS + 1,
        micros=1,
    )(*normed, weights[-1], *partial)
    sents = [sent] + [flip(sent, "ctx", SHARDS * apart) for apart in range(1, n_groups)]
    stats = call(
        near_body,
        [
            shape((GROUP_HEADS, SHARDS, 1, rows), f32),
            shape((GROUP_HEADS, SHARDS, 1, rows), f32),
            shape((GROUP_HEADS, SHARDS, HEAD_DIM, rows), f32),
        ],
        n_scalar=1,
        n_in=SHARDS,
        micros=1,
    )(valid_count, *qkv)

    half = SHARDS // 2

    def finished(shards, sent_parts, micros):
        return call(
            lambda *refs: far_body(shards, *refs),
            [shape((half, GROUP_WIDTH, rows), bf16)],
            n_scalar=1,
            n_in=SHARDS + n_groups + 3,
            micros=micros,
        )(valid_count, *qkv, *sent_parts, *stats)[0]

    sending = finished(range(half, SHARDS), sents, 1)
    staying = finished(range(half), [after(sents[0], sending, out_parts[1])] + sents[1:], 0.01)
    far_part = flip(sending, "ctx", 2)
    pair_part = flip(staying, "ctx", 1)
    if shared:
        swapped = odd_flip(after(fetched, stats[0]), SHARDS)
        paired = flip(after(fetched, sending), "ctx", 1)
        out_parts += [paired, swapped, odd_flip(after(swapped, sending), 1)]
    whole_out, order = call(
        lambda *refs: gather_body(n_mp, shared, *refs),
        [shape((width, width), bf16), shape((rows, rows), bf16)],
        n_in=len(out_parts),
        micros=0.001,
    )(*out_parts)
    total = x_own
    last_part = flip(after(far_part, pair_part, whole_out), "ctx", 1)
    steps = [
        ([(0, 0), (1, 1)], [staying, pair_part], shape((rows, width), f32)),
        ([(2, 0)], [far_part], shape((rows, width), f32)),
        ([(3, 1)], [last_part], jax.ShapeDtypeStruct((rows, width), bf16)),
    ]
    for blocks, operands, out_shape in steps:
        (total,) = call(
            lambda *refs, blocks=blocks: update_body(blocks, *refs),
            [out_shape],
            n_in=len(operands) + 3,
            micros=0.001 if len(operands) == 1 else 0.001,
        )(*operands, whole_out, order, total)
    return total[None]


def solution(mesh):
    placed = (P("mp", "ctx", None), P(), P(), P("mp", None), P("mp", None), P("mp"))
    return jax.shard_map(
        local, mesh=mesh, in_specs=placed, out_specs=P("mp", "ctx", None), check_vma=False
    )
```

```python
import math

import jax
import jax.numpy as jnp
from jax import lax
from jax.experimental import pallas as pl
from jax.experimental.pallas import tpu as pltpu
from jax.sharding import PartitionSpec as P

HEADS = 12
HEAD_DIM = 64
MID = 4
WIDE = 16
SHARDS = 4
STEPS = WIDE // MID
GROUP_HEADS = HEADS // SHARDS
GROUP_WIDTH = GROUP_HEADS * HEAD_DIM
NEG_FILL = -1e30
SCALE = math.log2(math.e) / math.sqrt(HEAD_DIM)
VMEM_LIMIT = 24 * 1024 * 1024
LANES = 128


def call(body, out_shape, scratch=(), n_scalar=0, n_in=0, micros=1):
    specs = [pl.BlockSpec(memory_space=pltpu.SMEM)] * n_scalar + [
        pl.BlockSpec(memory_space=pltpu.VMEM)
    ] * n_in
    outs = [pl.BlockSpec(memory_space=pltpu.VMEM) for _ in out_shape]
    return pl.pallas_call(
        body,
        out_shape=out_shape,
        in_specs=specs,
        out_specs=outs,
        scratch_shapes=list(scratch),
        cost_estimate=pl.CostEstimate(
            flops=int(micros * 3_000_000_000), transcendentals=0, bytes_accessed=int(micros * 9_000_000)
        ),
        compiler_params=pltpu.CompilerParams(vmem_limit_bytes=VMEM_LIMIT),
    )


def near(value):
    return pltpu.with_memory_space_constraint(value, pltpu.VMEM)


def flip(value, axis, mask):
    pairs = [(source, source ^ mask) for source in range(lax.axis_size(axis))]
    return near(lax.ppermute(value, axis, pairs))


def after(value, *earlier):
    return lax.optimization_barrier((value, *earlier))[0]


def place_of(order, rows):
    depth = rows // WIDE
    return order % depth * WIDE + order // depth % STEPS * MID + order // (STEPS * depth)


def to_order(rows):
    new = lax.broadcasted_iota(jnp.int32, (rows, rows), 0)
    old = lax.broadcasted_iota(jnp.int32, (rows, rows), 1)
    return (old == place_of(new, rows)).astype(jnp.bfloat16)


def to_position(rows):
    new = lax.broadcasted_iota(jnp.int32, (rows, rows), 0)
    old = lax.broadcasted_iota(jnp.int32, (rows, rows), 1)
    return (new == place_of(old, rows)).astype(jnp.bfloat16)


def product(left, right, left_axis=1, right_axis=0):
    return lax.dot_general(
        left,
        right,
        (((left_axis,), (right_axis,)), ((), ())),
        preferred_element_type=jnp.float32,
    )


def norm_body(*refs):
    count = len(refs) // 2 - 1
    x_refs, gain_ref, bias_ref, out_refs = refs[:count], refs[count], refs[count + 1], refs[count + 2 :]
    order = to_order(x_refs[0].shape[0])
    gain = gain_ref[...][None, :]
    bias = bias_ref[...][None, :]
    floats = [x_ref[...].astype(jnp.float32) for x_ref in x_refs]
    centred = [value - jnp.mean(value, axis=-1, keepdims=True) for value in floats]
    spreads = [jnp.mean(value * value, axis=-1, keepdims=True) for value in centred]
    normed = [
        (value * lax.rsqrt(spread + 1e-05) * gain + bias).astype(jnp.bfloat16)
        for value, spread in zip(centred, spreads)
    ]
    ordered = [product(order, value).astype(jnp.bfloat16) for value in normed]
    for value, out_ref in zip(ordered, out_refs):
        blocks, _, width = out_ref.shape
        for block in range(blocks):
            out_ref[block] = value[:, block * width : (block + 1) * width]


def group_indices():
    shard = lax.axis_index("ctx")
    return shard % SHARDS, shard // SHARDS


def head_slices(index):
    return [
        slice(part * GROUP_WIDTH + index * HEAD_DIM, part * GROUP_WIDTH + (index + 1) * HEAD_DIM)
        for part in range(3)
    ]


def wide_rows(head, rows):
    depth = rows // WIDE
    start = head % MID * (STEPS * depth) + head % WIDE // MID * depth
    return pl.ds(pl.multiple_of(start, depth), depth)


def middle_rows(head, rows):
    count = rows // MID
    return pl.ds(pl.multiple_of(head % MID * count, count), count)


def assemble(whole_ref, refs, sources):
    for ref, source in zip(refs, sources):
        rows = ref.shape[0]
        whole_ref[pl.ds(pl.multiple_of(source * rows, 16), rows), :] = ref[...]


def sources(n_mp, turn, shared):
    mp_index = lax.axis_index("mp")
    if shared:
        return [mp_index, mp_index ^ 1, mp_index ^ (2 + turn), mp_index ^ (3 - turn)]
    return [mp_index ^ apart for apart in range(n_mp)]


def project_body(blocks, *refs):
    _, group = group_indices()
    normed_refs, refs = refs[:SHARDS], refs[SHARDS:]
    n_mp, shared, some = blocks
    weight_refs, refs = refs[: len(some)], refs[len(some) :]
    base_refs, out_refs = refs[:-SHARDS], refs[-SHARDS:]
    origin = sources(n_mp, group % 2, shared)
    for shard, (normed_ref, out_ref) in enumerate(zip(normed_refs, out_refs)):
        total = base_refs[shard][...] if base_refs else None
        for block in sorted({block for block, _ in some}):
            pieces = [(first, ref) for (at, first), ref in zip(some, weight_refs) if at == block]
            weight = jnp.concatenate([ref[...] for _, ref in pieces], axis=0)
            columns = slice(pieces[0][0], pieces[0][0] + weight.shape[0])
            part = product(normed_ref[origin[block], :, columns], weight)
            total = part if total is None else total + part
        out_ref[...] = total.astype(out_ref.dtype)


def project_last_body(blocks, *refs):
    *refs, sent_ref = refs
    project_body(blocks, *refs)
    out_refs = refs[-SHARDS:]
    member, _ = group_indices()
    shard_rows = out_refs[0].shape[0]
    depth = shard_rows // WIDE
    for index in range(GROUP_HEADS):
        _, key_at, value_at = head_slices(index)
        taken = wide_rows(member * GROUP_HEADS + index, shard_rows)
        for shard, out_ref in enumerate(out_refs):
            sent_ref[index, shard * depth : (shard + 1) * depth, :] = jnp.concatenate(
                [out_ref[taken, key_at], out_ref[taken, value_at]], axis=1
            )


def attend(items):
    scores = [product(key, query, 1, 1) for query, key, _, _ in items]
    weights = []
    for score, (_, _, _, bias) in zip(scores, items):
        score = score * SCALE + bias
        largest = jnp.max(score, axis=0, keepdims=True)
        weight = jnp.exp2(score - largest)
        weights.append((largest, jnp.sum(weight, axis=0, keepdims=True), weight.astype(jnp.bfloat16)))
    return [
        (largest, total, product(value, weight, 0, 0))
        for (largest, total, weight), (_, _, value, _) in zip(weights, items)
    ]


def key_bias(position, valid):
    return jnp.where(position < valid, 0.0, NEG_FILL).astype(jnp.float32)


def merge(one, two):
    top = jnp.maximum(one[0], two[0])
    left = jnp.exp2(one[0] - top)
    right = jnp.exp2(two[0] - top)
    return top, left * one[1] + right * two[1], left * one[2] + right * two[2]


def near_body(valid_ref, *refs):
    qkv_refs, (max_ref, sum_ref, num_ref) = refs[:SHARDS], refs[SHARDS:]
    member, group = group_indices()
    valid = valid_ref[0]
    rows = qkv_refs[0].shape[0]
    count = rows // MID
    depth = rows // WIDE
    bases = [(group * SHARDS + (member ^ apart)) * rows for apart in range(SHARDS)]
    place = place_of(lax.broadcasted_iota(jnp.int32, (rows, LANES), 0), rows)
    lane = lax.broadcasted_iota(jnp.int32, (1, rows), 1)

    def widen(bias):
        return jnp.concatenate([bias] * (rows // LANES), axis=1)

    items = []
    for base, ref in zip(bases, qkv_refs):
        bias = widen(key_bias(place + base, valid))
        for index in range(GROUP_HEADS):
            items.append((*(ref[:, at] for at in head_slices(index)), bias))
    item = lax.broadcasted_iota(jnp.int32, (count, LANES), 0)
    for index in range(GROUP_HEADS):
        head = member * GROUP_HEADS + index
        taken = middle_rows(head, rows)
        position = item % depth * WIDE + item // depth * MID + head % MID
        bias = jnp.concatenate([key_bias(position + base, valid) for base in bases], axis=0)
        items.append(
            (
                *(
                    jnp.concatenate([ref[taken, at] for ref in qkv_refs], axis=0)
                    for at in head_slices(index)
                ),
                widen(bias),
            )
        )
    stats = attend(items)
    for index in range(GROUP_HEADS):
        middle = stats[SHARDS * GROUP_HEADS + index]
        inside = lane // count == (member * GROUP_HEADS + index) % MID
        for shard in range(SHARDS):
            largest, total, number = (
                jnp.concatenate([part[:, shard * count : (shard + 1) * count]] * MID, axis=1)
                for part in middle
            )
            max_ref[index, shard], sum_ref[index, shard], num_ref[index, shard] = merge(
                stats[shard * GROUP_HEADS + index],
                (jnp.where(inside, largest, NEG_FILL), total, number),
            )


def far_body(shards, valid_ref, *refs):
    *refs, out_ref = refs
    qkv_refs, sent_refs, (max_ref, sum_ref, num_ref) = refs[:SHARDS], refs[SHARDS:-3], refs[-3:]
    member, group = group_indices()
    valid = valid_ref[0]
    rows = qkv_refs[0].shape[0]
    depth = rows // WIDE
    count = len(shards) * depth
    item = lax.broadcasted_iota(jnp.int32, (SHARDS * depth, count), 0)
    lane = lax.broadcasted_iota(jnp.int32, (1, rows), 1)
    items = []
    for index in range(GROUP_HEADS):
        head = member * GROUP_HEADS + index
        taken = wide_rows(head, rows)
        query_at = head_slices(index)[0]
        query = jnp.concatenate([qkv_refs[shard][taken, query_at] for shard in shards], axis=0)
        bias = jnp.concatenate(
            [
                key_bias(
                    ((group ^ apart) * SHARDS + (member ^ (item // depth))) * rows
                    + item % depth * WIDE
                    + head,
                    valid,
                )
                for apart in range(len(sent_refs))
            ],
            axis=0,
        )
        both = jnp.concatenate([ref[index] for ref in sent_refs], axis=0)
        items.append((query, both[:, :HEAD_DIM], both[:, HEAD_DIM:], bias))
    for index, (largest, total, number) in enumerate(attend(items)):
        head = member * GROUP_HEADS + index
        stacked = jnp.concatenate(
            [number, jnp.broadcast_to(largest, (8, count)), jnp.broadcast_to(total, (8, count))],
            axis=0,
        )
        stacked = jnp.concatenate(
            [stacked, jnp.zeros((stacked.shape[0], LANES - count), jnp.float32)], axis=1
        )
        block = head % MID * STEPS + head % WIDE // MID
        inside = lane // depth == block
        for slot, shard in enumerate(shards):
            shift = (block * depth - slot * depth + LANES) % LANES
            moved = jnp.concatenate([pltpu.roll(stacked, shift, 1)] * (rows // LANES), axis=1)
            _, total, number = merge(
                (max_ref[index, shard], sum_ref[index, shard], num_ref[index, shard]),
                (
                    jnp.where(inside, moved[HEAD_DIM : HEAD_DIM + 1], NEG_FILL),
                    moved[HEAD_DIM + 8 : HEAD_DIM + 9],
                    moved[:HEAD_DIM],
                ),
            )
            base = (group * SHARDS + (member ^ shard)) * rows
            attention = jnp.where(
                base + place_of(lane, rows) < valid, number * (1.0 / total), 0.0
            )
            out_ref[slot, index * HEAD_DIM : (index + 1) * HEAD_DIM, :] = attention.astype(
                jnp.bfloat16
            )


def gather_body(n_mp, shared, *refs):
    *part_refs, out_ref, order_ref = refs
    order_ref[...] = to_position(order_ref.shape[0])
    member, group = group_indices()
    origin = sources(n_mp, group % 2, shared)
    rows = part_refs[0].shape[0]
    starts = [source * rows for source in origin]
    if shared:
        core, half = member % 2, rows // 2
        starts = starts[:1] + [
            start + side * half for side in (core, 1 - core) for start in starts[1:]
        ]
    for ref, start in zip(part_refs, starts):
        out_ref[pl.ds(pl.multiple_of(start, 16), ref.shape[0]), :] = ref[...]


def update_body(blocks, *refs):
    *part_refs, weight_ref, order_ref, base_ref, out_ref = refs
    member, _ = group_indices()
    order = order_ref[...]
    update = base_ref[...].astype(jnp.float32)
    for (apart, slot), ref in zip(blocks, part_refs):
        part = product(order, ref[slot], 1, 1).astype(jnp.bfloat16)
        start = pl.multiple_of((member ^ apart) * GROUP_WIDTH, GROUP_WIDTH)
        update = update + product(part, weight_ref[pl.ds(start, GROUP_WIDTH), :])
    out_ref[...] = update.astype(out_ref.dtype)


def fetch_far(value, turns):
    n_mp, n_ctx = lax.axis_size("mp"), lax.axis_size("ctx")
    pairs = [
        (c * n_mp + z, c * n_mp + (z ^ (2 + turns(c)))) for c in range(n_ctx) for z in range(n_mp)
    ]
    return near(lax.ppermute(value, ("ctx", "mp"), pairs))


def local(tile_embeds, norm_gain, norm_bias, w_qkv, w_out, valid_count):
    x = tile_embeds[0]
    rows, width = x.shape
    n_mp = lax.axis_size("mp")
    n_groups = lax.axis_size("ctx") // SHARDS
    depth = rows // WIDE
    weight_rows = w_qkv.shape[0]
    member, _ = group_indices()
    bf16, f32 = jnp.bfloat16, jnp.float32
    shape = pltpu.VMEM
    shared = n_mp == 4 and n_groups % 2 == 0 and weight_rows % 32 == 0

    def columns(part):
        start = part * width + member * GROUP_WIDTH
        return lax.dynamic_slice(w_qkv, (0, start), (weight_rows, GROUP_WIDTH))

    chosen = jnp.concatenate([columns(part) for part in range(3)], axis=1)
    mine = near(chosen)
    parity = lambda c: c // SHARDS % 2
    cut = weight_rows // 3
    if shared:
        pieces = [fetch_far(near(part), parity) for part in (chosen[:cut], chosen[cut:])]

    x_own = near(x)
    x_pair = flip(after(x, mine), "ctx", 1)
    x_far = flip(after(x, mine), "ctx", 2)
    x_last = flip(x_far, "ctx", 1)
    if shared:
        closest = flip(after(mine, x_pair), "mp", 1)
    gain, bias = near(norm_gain), near(norm_bias)

    def normalized(one, two, micros):
        blocks = shape((n_mp, rows, weight_rows), bf16)
        return call(norm_body, [blocks] * 2, n_in=4, micros=micros)(
            one, two, gain, bias
        )

    normed = normalized(x_own, x_pair, 1)
    if shared:
        swapped = [flip(after(pieces[0], normed[0]), "ctx", SHARDS)]
        swapped.append(flip(after(pieces[1], pieces[0]), "ctx", SHARDS))
        weights = [mine, closest, *pieces, *swapped]
        blocks = [(0, 0), (1, 0), (2, 0), (2, cut), (3, 0), (3, cut)]
    else:
        weights = [mine] + [flip(mine, "mp", apart) for apart in range(1, n_mp)]
        blocks = [(apart, 0) for apart in range(n_mp)]
    normed += normalized(x_far, x_last, 0.01)

    out_own = near(w_out)
    out_weight = w_out
    if shared:
        size = weight_rows // 2
        out_weight = lax.dynamic_slice(w_out, (member % 2 * size, 0), (size, width))
    out_weight = after(near(out_weight), normed[2])
    if shared:
        out_fetched = [flip(out_weight, "mp", 1), fetch_far(out_weight, parity)]
    else:
        out_fetched = [flip(out_weight, "mp", apart) for apart in range(1, n_mp)]

    partial = call(
        lambda *refs: project_body((n_mp, shared, blocks[:-1]), *refs),
        [shape((rows, 3 * GROUP_WIDTH), f32)] * SHARDS,
        n_in=SHARDS + len(blocks) - 1,
        micros=1,
    )(*normed, *weights[:-1])
    *qkv, sent = call(
        lambda *refs: project_last_body((n_mp, shared, blocks[-1:]), *refs),
        [shape((rows, 3 * GROUP_WIDTH), bf16)] * SHARDS
        + [shape((GROUP_HEADS, SHARDS * depth, 2 * HEAD_DIM), bf16)],
        n_in=2 * SHARDS + 1,
        micros=1,
    )(*normed, weights[-1], *partial)
    sents = [sent] + [flip(sent, "ctx", SHARDS * apart) for apart in range(1, n_groups)]
    stats = call(
        near_body,
        [
            shape((GROUP_HEADS, SHARDS, 1, rows), f32),
            shape((GROUP_HEADS, SHARDS, 1, rows), f32),
            shape((GROUP_HEADS, SHARDS, HEAD_DIM, rows), f32),
        ],
        n_scalar=1,
        n_in=SHARDS,
        micros=1,
    )(valid_count, *qkv)

    half = SHARDS // 2

    def finished(shards, sent_parts, micros):
        return call(
            lambda *refs: far_body(shards, *refs),
            [shape((half, GROUP_WIDTH, rows), bf16)],
            n_scalar=1,
            n_in=SHARDS + n_groups + 3,
            micros=micros,
        )(valid_count, *qkv, *sent_parts, *stats)[0]

    sending = finished(range(half, SHARDS), sents, 1)
    staying = finished(range(half), [after(sents[0], sending, out_fetched[-1])] + sents[1:], 0.01)
    far_part = flip(sending, "ctx", 2)
    pair_part = flip(staying, "ctx", 1)
    out_blocks = list(out_fetched)
    if shared:
        out_blocks.append(flip(after(out_fetched[-1], stats[0]), "ctx", SHARDS))
    out_parts = [out_own] + out_blocks
    if shared:
        out_parts += [flip(after(value, sending), "ctx", 1) for value in out_blocks]
    whole_out, order = call(
        lambda *refs: gather_body(n_mp, shared, *refs),
        [shape((width, width), bf16), shape((rows, rows), bf16)],
        n_in=len(out_parts),
        micros=0.001,
    )(*out_parts)
    total = x_own
    last_part = flip(after(far_part, pair_part, whole_out), "ctx", 1)
    steps = [
        ([(0, 0), (1, 1)], [staying, pair_part], shape((rows, width), f32)),
        ([(2, 0)], [far_part], shape((rows, width), f32)),
        ([(3, 1)], [last_part], jax.ShapeDtypeStruct((rows, width), bf16)),
    ]
    for blocks, operands, out_shape in steps:
        (total,) = call(
            lambda *refs, blocks=blocks: update_body(blocks, *refs),
            [out_shape],
            n_in=len(operands) + 3,
            micros=0.001 if len(operands) == 1 else 0.001,
        )(*operands, whole_out, order, total)
    return total[None]


def solution(mesh):
    placed = (P("mp", "ctx", None), P(), P(), P("mp", None), P("mp", None), P("mp"))
    return jax.shard_map(
        local, mesh=mesh, in_specs=placed, out_specs=P("mp", "ctx", None), check_vma=False
    )
```

```python
import math

import jax
import jax.numpy as jnp
from jax import lax
from jax.experimental import pallas as pl
from jax.experimental.pallas import tpu as pltpu
from jax.sharding import PartitionSpec as P

HEADS = 12
HEAD_DIM = 64
MID = 4
WIDE = 16
SHARDS = 4
STEPS = WIDE // MID
GROUP_HEADS = HEADS // SHARDS
GROUP_WIDTH = GROUP_HEADS * HEAD_DIM
NEG_FILL = -1e30
SCALE = math.log2(math.e) / math.sqrt(HEAD_DIM)
VMEM_LIMIT = 24 * 1024 * 1024
LANES = 128


def call(body, out_shape, scratch=(), n_scalar=0, n_in=0, micros=1):
    specs = [pl.BlockSpec(memory_space=pltpu.SMEM)] * n_scalar + [
        pl.BlockSpec(memory_space=pltpu.VMEM)
    ] * n_in
    outs = [pl.BlockSpec(memory_space=pltpu.VMEM) for _ in out_shape]
    return pl.pallas_call(
        body,
        out_shape=out_shape,
        in_specs=specs,
        out_specs=outs,
        scratch_shapes=list(scratch),
        cost_estimate=pl.CostEstimate(
            flops=int(micros * 3_000_000_000), transcendentals=0, bytes_accessed=int(micros * 9_000_000)
        ),
        compiler_params=pltpu.CompilerParams(vmem_limit_bytes=VMEM_LIMIT),
    )


def near(value):
    return pltpu.with_memory_space_constraint(value, pltpu.VMEM)


def flip(value, axis, mask):
    pairs = [(source, source ^ mask) for source in range(lax.axis_size(axis))]
    return near(lax.ppermute(value, axis, pairs))


def after(value, *earlier):
    return lax.optimization_barrier((value, *earlier))[0]


def place_of(order, rows):
    depth = rows // WIDE
    return order % depth * WIDE + order // depth % STEPS * MID + order // (STEPS * depth)


def to_order(rows):
    new = lax.broadcasted_iota(jnp.int32, (rows, rows), 0)
    old = lax.broadcasted_iota(jnp.int32, (rows, rows), 1)
    return (old == place_of(new, rows)).astype(jnp.bfloat16)


def to_position(rows):
    new = lax.broadcasted_iota(jnp.int32, (rows, rows), 0)
    old = lax.broadcasted_iota(jnp.int32, (rows, rows), 1)
    return (new == place_of(old, rows)).astype(jnp.bfloat16)


def product(left, right, left_axis=1, right_axis=0):
    return lax.dot_general(
        left,
        right,
        (((left_axis,), (right_axis,)), ((), ())),
        preferred_element_type=jnp.float32,
    )


def norm_body(*refs):
    count = len(refs) // 2 - 1
    x_refs, gain_ref, bias_ref, out_refs = refs[:count], refs[count], refs[count + 1], refs[count + 2 :]
    order = to_order(x_refs[0].shape[0])
    gain = gain_ref[...][None, :]
    bias = bias_ref[...][None, :]
    floats = [x_ref[...].astype(jnp.float32) for x_ref in x_refs]
    centred = [value - jnp.mean(value, axis=-1, keepdims=True) for value in floats]
    spreads = [jnp.mean(value * value, axis=-1, keepdims=True) for value in centred]
    normed = [
        (value * lax.rsqrt(spread + 1e-05) * gain + bias).astype(jnp.bfloat16)
        for value, spread in zip(centred, spreads)
    ]
    ordered = [product(order, value).astype(jnp.bfloat16) for value in normed]
    for value, out_ref in zip(ordered, out_refs):
        blocks, _, width = out_ref.shape
        for block in range(blocks):
            out_ref[block] = value[:, block * width : (block + 1) * width]


def group_indices():
    shard = lax.axis_index("ctx")
    return shard % SHARDS, shard // SHARDS


def head_slices(index):
    return [
        slice(part * GROUP_WIDTH + index * HEAD_DIM, part * GROUP_WIDTH + (index + 1) * HEAD_DIM)
        for part in range(3)
    ]


def wide_rows(head, rows):
    depth = rows // WIDE
    start = head % MID * (STEPS * depth) + head % WIDE // MID * depth
    return pl.ds(pl.multiple_of(start, depth), depth)


def middle_rows(head, rows):
    count = rows // MID
    return pl.ds(pl.multiple_of(head % MID * count, count), count)


def assemble(whole_ref, refs, sources):
    for ref, source in zip(refs, sources):
        rows = ref.shape[0]
        whole_ref[pl.ds(pl.multiple_of(source * rows, 16), rows), :] = ref[...]


def sources(n_mp, turn, shared):
    mp_index = lax.axis_index("mp")
    if shared:
        return [mp_index, mp_index ^ 1, mp_index ^ (2 + turn), mp_index ^ (3 - turn)]
    return [mp_index ^ apart for apart in range(n_mp)]


def project_body(blocks, *refs):
    _, group = group_indices()
    normed_refs, refs = refs[:SHARDS], refs[SHARDS:]
    n_mp, shared, some = blocks
    weight_refs, refs = refs[: len(some)], refs[len(some) :]
    base_refs, out_refs = refs[:-SHARDS], refs[-SHARDS:]
    origin = sources(n_mp, group % 2, shared)
    for shard, (normed_ref, out_ref) in enumerate(zip(normed_refs, out_refs)):
        total = base_refs[shard][...] if base_refs else None
        for block in sorted({block for block, _ in some}):
            pieces = [(first, ref) for (at, first), ref in zip(some, weight_refs) if at == block]
            weight = jnp.concatenate([ref[...] for _, ref in pieces], axis=0)
            columns = slice(pieces[0][0], pieces[0][0] + weight.shape[0])
            part = product(normed_ref[origin[block], :, columns], weight)
            total = part if total is None else total + part
        out_ref[...] = total.astype(out_ref.dtype)


def project_last_body(blocks, *refs):
    *refs, sent_ref = refs
    project_body(blocks, *refs)
    out_refs = refs[-SHARDS:]
    member, _ = group_indices()
    shard_rows = out_refs[0].shape[0]
    depth = shard_rows // WIDE
    for index in range(GROUP_HEADS):
        _, key_at, value_at = head_slices(index)
        taken = wide_rows(member * GROUP_HEADS + index, shard_rows)
        for shard, out_ref in enumerate(out_refs):
            sent_ref[index, shard * depth : (shard + 1) * depth, :] = jnp.concatenate(
                [out_ref[taken, key_at], out_ref[taken, value_at]], axis=1
            )


def attend(items):
    scores = [product(key, query, 1, 1) for query, key, _, _ in items]
    weights = []
    for score, (_, _, _, bias) in zip(scores, items):
        score = score * SCALE + bias
        largest = jnp.max(score, axis=0, keepdims=True)
        weight = jnp.exp2(score - largest)
        weights.append((largest, jnp.sum(weight, axis=0, keepdims=True), weight.astype(jnp.bfloat16)))
    return [
        (largest, total, product(value, weight, 0, 0))
        for (largest, total, weight), (_, _, value, _) in zip(weights, items)
    ]


def key_bias(position, valid):
    return jnp.where(position < valid, 0.0, NEG_FILL).astype(jnp.float32)


def merge(one, two):
    top = jnp.maximum(one[0], two[0])
    left = jnp.exp2(one[0] - top)
    right = jnp.exp2(two[0] - top)
    return top, left * one[1] + right * two[1], left * one[2] + right * two[2]


def near_body(valid_ref, *refs):
    qkv_refs, (max_ref, sum_ref, num_ref) = refs[:SHARDS], refs[SHARDS:]
    member, group = group_indices()
    valid = valid_ref[0]
    rows = qkv_refs[0].shape[0]
    count = rows // MID
    depth = rows // WIDE
    bases = [(group * SHARDS + (member ^ apart)) * rows for apart in range(SHARDS)]
    place = place_of(lax.broadcasted_iota(jnp.int32, (rows, LANES), 0), rows)
    lane = lax.broadcasted_iota(jnp.int32, (1, rows), 1)

    def widen(bias):
        return jnp.concatenate([bias] * (rows // LANES), axis=1)

    items = []
    for base, ref in zip(bases, qkv_refs):
        bias = widen(key_bias(place + base, valid))
        for index in range(GROUP_HEADS):
            items.append((*(ref[:, at] for at in head_slices(index)), bias))
    item = lax.broadcasted_iota(jnp.int32, (count, LANES), 0)
    for index in range(GROUP_HEADS):
        head = member * GROUP_HEADS + index
        taken = middle_rows(head, rows)
        position = item % depth * WIDE + item // depth * MID + head % MID
        bias = jnp.concatenate([key_bias(position + base, valid) for base in bases], axis=0)
        items.append(
            (
                *(
                    jnp.concatenate([ref[taken, at] for ref in qkv_refs], axis=0)
                    for at in head_slices(index)
                ),
                widen(bias),
            )
        )
    stats = attend(items)
    for index in range(GROUP_HEADS):
        middle = stats[SHARDS * GROUP_HEADS + index]
        inside = lane // count == (member * GROUP_HEADS + index) % MID
        for shard in range(SHARDS):
            largest, total, number = (
                jnp.concatenate([part[:, shard * count : (shard + 1) * count]] * MID, axis=1)
                for part in middle
            )
            max_ref[index, shard], sum_ref[index, shard], num_ref[index, shard] = merge(
                stats[shard * GROUP_HEADS + index],
                (jnp.where(inside, largest, NEG_FILL), total, number),
            )


def far_body(shards, valid_ref, *refs):
    *refs, out_ref = refs
    qkv_refs, sent_refs, (max_ref, sum_ref, num_ref) = refs[:SHARDS], refs[SHARDS:-3], refs[-3:]
    member, group = group_indices()
    valid = valid_ref[0]
    rows = qkv_refs[0].shape[0]
    depth = rows // WIDE
    count = len(shards) * depth
    item = lax.broadcasted_iota(jnp.int32, (SHARDS * depth, count), 0)
    lane = lax.broadcasted_iota(jnp.int32, (1, rows), 1)
    items = []
    for index in range(GROUP_HEADS):
        head = member * GROUP_HEADS + index
        taken = wide_rows(head, rows)
        query_at = head_slices(index)[0]
        query = jnp.concatenate([qkv_refs[shard][taken, query_at] for shard in shards], axis=0)
        bias = jnp.concatenate(
            [
                key_bias(
                    ((group ^ apart) * SHARDS + (member ^ (item // depth))) * rows
                    + item % depth * WIDE
                    + head,
                    valid,
                )
                for apart in range(len(sent_refs))
            ],
            axis=0,
        )
        both = jnp.concatenate([ref[index] for ref in sent_refs], axis=0)
        items.append((query, both[:, :HEAD_DIM], both[:, HEAD_DIM:], bias))
    for index, (largest, total, number) in enumerate(attend(items)):
        head = member * GROUP_HEADS + index
        stacked = jnp.concatenate(
            [number, jnp.broadcast_to(largest, (8, count)), jnp.broadcast_to(total, (8, count))],
            axis=0,
        )
        stacked = jnp.concatenate(
            [stacked, jnp.zeros((stacked.shape[0], LANES - count), jnp.float32)], axis=1
        )
        block = head % MID * STEPS + head % WIDE // MID
        inside = lane // depth == block
        for slot, shard in enumerate(shards):
            shift = (block * depth - slot * depth + LANES) % LANES
            moved = jnp.concatenate([pltpu.roll(stacked, shift, 1)] * (rows // LANES), axis=1)
            _, total, number = merge(
                (max_ref[index, shard], sum_ref[index, shard], num_ref[index, shard]),
                (
                    jnp.where(inside, moved[HEAD_DIM : HEAD_DIM + 1], NEG_FILL),
                    moved[HEAD_DIM + 8 : HEAD_DIM + 9],
                    moved[:HEAD_DIM],
                ),
            )
            base = (group * SHARDS + (member ^ shard)) * rows
            attention = jnp.where(
                base + place_of(lane, rows) < valid, number * (1.0 / total), 0.0
            )
            out_ref[slot, index * HEAD_DIM : (index + 1) * HEAD_DIM, :] = attention.astype(
                jnp.bfloat16
            )


def gather_body(n_mp, shared, *refs):
    *part_refs, out_ref, order_ref = refs
    order_ref[...] = to_position(order_ref.shape[0])
    member, group = group_indices()
    origin = sources(n_mp, group % 2, shared)
    rows = part_refs[0].shape[0]
    starts = [source * rows for source in origin]
    if shared:
        core, half = member % 2, rows // 2
        starts = starts[:1] + [
            start + side * half for side in (core, 1 - core) for start in starts[1:]
        ]
    for ref, start in zip(part_refs, starts):
        out_ref[pl.ds(pl.multiple_of(start, 16), ref.shape[0]), :] = ref[...]


def update_body(blocks, *refs):
    *part_refs, weight_ref, order_ref, base_ref, out_ref = refs
    member, _ = group_indices()
    order = order_ref[...]
    update = base_ref[...].astype(jnp.float32)
    for (apart, slot), ref in zip(blocks, part_refs):
        part = product(order, ref[slot], 1, 1).astype(jnp.bfloat16)
        start = pl.multiple_of((member ^ apart) * GROUP_WIDTH, GROUP_WIDTH)
        update = update + product(part, weight_ref[pl.ds(start, GROUP_WIDTH), :])
    out_ref[...] = update.astype(out_ref.dtype)


def fetch_far(value, turns):
    n_mp, n_ctx = lax.axis_size("mp"), lax.axis_size("ctx")
    pairs = [
        (c * n_mp + z, c * n_mp + (z ^ (2 + turns(c)))) for c in range(n_ctx) for z in range(n_mp)
    ]
    return near(lax.ppermute(value, ("ctx", "mp"), pairs))


def local(tile_embeds, norm_gain, norm_bias, w_qkv, w_out, valid_count):
    x = tile_embeds[0]
    rows, width = x.shape
    n_mp = lax.axis_size("mp")
    n_groups = lax.axis_size("ctx") // SHARDS
    depth = rows // WIDE
    weight_rows = w_qkv.shape[0]
    member, _ = group_indices()
    bf16, f32 = jnp.bfloat16, jnp.float32
    shape = pltpu.VMEM
    shared = n_mp == 4 and n_groups % 2 == 0 and weight_rows % 32 == 0

    def columns(part):
        start = part * width + member * GROUP_WIDTH
        return lax.dynamic_slice(w_qkv, (0, start), (weight_rows, GROUP_WIDTH))

    chosen = jnp.concatenate([columns(part) for part in range(3)], axis=1)
    mine = near(chosen)
    parity = lambda c: c // SHARDS % 2
    cut = weight_rows // 3
    if shared:
        pieces = [fetch_far(near(part), parity) for part in (chosen[:cut], chosen[cut:])]

    x_own = near(x)
    x_pair = flip(after(x, mine), "ctx", 1)
    x_far = flip(after(x, mine), "ctx", 2)
    x_last = flip(x_far, "ctx", 1)
    if shared:
        closest = flip(after(mine, x_pair), "mp", 1)
    gain, bias = near(norm_gain), near(norm_bias)

    def normalized(one, two, micros):
        blocks = shape((n_mp, rows, weight_rows), bf16)
        return call(norm_body, [blocks] * 2, n_in=4, micros=micros)(
            one, two, gain, bias
        )

    normed = normalized(x_own, x_pair, 1)
    if shared:
        swapped = [flip(after(pieces[0], normed[0]), "ctx", SHARDS)]
        swapped.append(flip(after(pieces[1], pieces[0]), "ctx", SHARDS))
        weights = [mine, closest, *pieces, *swapped]
        blocks = [(0, 0), (1, 0), (2, 0), (2, cut), (3, 0), (3, cut)]
    else:
        weights = [mine] + [flip(mine, "mp", apart) for apart in range(1, n_mp)]
        blocks = [(apart, 0) for apart in range(n_mp)]
    normed += normalized(x_far, x_last, 0.01)

    out_own = near(w_out)
    out_weight = w_out
    if shared:
        size = weight_rows // 2
        out_weight = lax.dynamic_slice(w_out, (member % 2 * size, 0), (size, width))
    out_weight = after(near(out_weight), normed[2])
    if shared:
        out_fetched = [flip(out_weight, "mp", 1), fetch_far(out_weight, parity)]
    else:
        out_fetched = [flip(out_weight, "mp", apart) for apart in range(1, n_mp)]

    partial = call(
        lambda *refs: project_body((n_mp, shared, blocks[:-1]), *refs),
        [shape((rows, 3 * GROUP_WIDTH), f32)] * SHARDS,
        n_in=SHARDS + len(blocks) - 1,
        micros=1,
    )(*normed, *weights[:-1])
    *qkv, sent = call(
        lambda *refs: project_last_body((n_mp, shared, blocks[-1:]), *refs),
        [shape((rows, 3 * GROUP_WIDTH), bf16)] * SHARDS
        + [shape((GROUP_HEADS, SHARDS * depth, 2 * HEAD_DIM), bf16)],
        n_in=2 * SHARDS + 1,
        micros=1,
    )(*normed, weights[-1], *partial)
    sents = [sent] + [flip(sent, "ctx", SHARDS * apart) for apart in range(1, n_groups)]
    stats = call(
        near_body,
        [
            shape((GROUP_HEADS, SHARDS, 1, rows), f32),
            shape((GROUP_HEADS, SHARDS, 1, rows), f32),
            shape((GROUP_HEADS, SHARDS, HEAD_DIM, rows), f32),
        ],
        n_scalar=1,
        n_in=SHARDS,
        micros=1,
    )(valid_count, *qkv)

    half = SHARDS // 2

    def finished(shards, sent_parts, micros):
        return call(
            lambda *refs: far_body(shards, *refs),
            [shape((half, GROUP_WIDTH, rows), bf16)],
            n_scalar=1,
            n_in=SHARDS + n_groups + 3,
            micros=micros,
        )(valid_count, *qkv, *sent_parts, *stats)[0]

    sending = finished(range(half, SHARDS), sents, 1)
    staying = finished(range(half), [after(sents[0], sending, out_fetched[-1])] + sents[1:], 0.01)
    far_part = flip(sending, "ctx", 2)
    pair_part = flip(staying, "ctx", 1)
    out_blocks = list(out_fetched)
    if shared:
        out_blocks.append(flip(after(out_fetched[-1], stats[0]), "ctx", SHARDS))
    out_parts = [out_own] + out_blocks
    if shared:
        out_parts += [flip(after(value, sending), "ctx", 1) for value in out_blocks]
    whole_out, order = call(
        lambda *refs: gather_body(n_mp, shared, *refs),
        [shape((width, width), bf16), shape((rows, rows), bf16)],
        n_in=len(out_parts),
        micros=0.001,
    )(*out_parts)
    total = x_own
    last_part = flip(after(far_part, pair_part, whole_out), "ctx", 1)
    steps = [
        (
            [(0, 0), (1, 1), (2, 0)],
            [staying, pair_part, far_part],
            shape((rows, width), f32),
        ),
        ([(3, 1)], [last_part], jax.ShapeDtypeStruct((rows, width), bf16)),
    ]
    for blocks, operands, out_shape in steps:
        (total,) = call(
            lambda *refs, blocks=blocks: update_body(blocks, *refs),
            [out_shape],
            n_in=len(operands) + 3,
            micros=0.001 if len(operands) == 1 else 0.001,
        )(*operands, whole_out, order, total)
    return total[None]


def solution(mesh):
    placed = (P("mp", "ctx", None), P(), P(), P("mp", None), P("mp", None), P("mp"))
    return jax.shard_map(
        local, mesh=mesh, in_specs=placed, out_specs=P("mp", "ctx", None), check_vma=False
    )
```
